32 devices in a mesh: batch: 16 (over z, y, x), mp: 2 (over core).
Axes of the slice: x: 2, y: 2, z: 4, core: 2. Of those that a mesh axis runs over, the one named last changes fastest.
Arguments:
- block_input_slots: bfloat16 [32768, 512], P('batch'), may hold values from -6 to 6
- memory: bfloat16 [16384, 512], P('batch'), may hold values from -6 to 6
- target_sentence_lengths: int32 [16, 32], P('batch'), may hold values from 1 to 1024, 2048 in all within a row
- source_lengths: int32 [16, 32], P('batch'), may hold values from 1 to 512, 1024 in all within a row
- self_qkv: bfloat16 [3, 512, 512], P(None, None, 'mp'), may hold values from -0.25 to 0.25
- self_out: bfloat16 [512, 512], P('mp'), may hold values from -0.75 to 0.75
- cross_query: bfloat16 [512, 512], P(None, 'mp'), may hold values from -0.25 to 0.25
- cross_kv: bfloat16 [2, 512, 512], P(None, None, 'mp'), may hold values from -0.25 to 0.25
- cross_out: bfloat16 [512, 512], P('mp'), may hold values from -0.75 to 0.75
- up_proj: bfloat16 [2048, 512], P('mp'), may hold values from -0.25 to 0.25
- down_proj: bfloat16 [2048, 512], P('mp'), may hold values from -0.125 to 0.125
- norm_gains: float32 [512, 3], replicated, may hold values from 0.1 to 1.9
- norm_biases: float32 [512, 3], replicated, may hold values from -3 to 3
- cotangent: bfloat16 [32768, 512], P(('batch', 'mp')), may hold values from -6 to 6
Outputs:
- layer_output: bfloat16 [32768, 512], P(('batch', 'mp'))
- input_grad: float32 [32768, 512], P(('batch', 'mp'))
- memory_grad: float32 [16384, 512], P(('batch', 'mp'))
- self_qkv_grad: float32 [3, 512, 512], P(None, None, 'mp')
- self_out_grad: float32 [512, 512], P('mp')
- cross_query_grad: float32 [512, 512], P(None, 'mp')
- cross_kv_grad: float32 [2, 512, 512], P(None, None, 'mp')
- cross_out_grad: float32 [512, 512], P('mp')
- up_proj_grad: float32 [2048, 512], P('mp')
- down_proj_grad: float32 [2048, 512], P('mp')
- gain_grad: float32 [512, 3], P('mp')
- bias_grad: float32 [512, 3], P('mp')
The draws below stay inside these ranges and needn't reach their ends.
Inputs may be any that keep to these rules, and one draw needn't show every extreme that they name: `target_sentence_lengths`: in every row the 32 target lengths add up to 2048 and the longest is exactly 1024; sentence j of a row fills the slots right after those of sentences 0 to j-1. `source_lengths`: in every row the 32 source lengths add up to 1024 and the longest is exactly 512; source sentence j of a row pairs with target sentence j and fills the memory slots right after those of sentences 0 to j-1.
All inputs are finite; a program needn't handle non-finite values.
Results may differ from the reference program's by a relative error of at most 0.023.
Values may be sent and summed in bfloat16 or wider, within the bound.
A program may use at most 192 MiB of HBM per device.

```python
import math
import jax
import jax.numpy as jnp
import numpy as np
from jax import lax

MODEL_WIDTH = 512
HEADS = 8
DH = 64
FF = 2048
ROW_SLOTS = 2048
MEMLEN = 1024
SENTENCE_COUNT = 32
LONGEST_TARGET = 1024
SRCMAX = 512
PACKED_ROWS = 16
TOKENS = 32768
MEMTOK = 16384


def steps_of(stream_key, dims, cuts, least, high):
    def one(position, shards_of):
        draws = jax.random.uniform(jax.random.fold_in(jax.random.fold_in(stream_key, 6), position), (shards_of,), jnp.float32, least / len(cuts), high / len(cuts))
        return jnp.repeat(jnp.exp(draws), dims[position] // shards_of).reshape((-1,) + (1,) * (len(dims) - position - 1))

    level = one(*cuts[0])
    for cut in cuts[1:]:
        level = level * one(*cut)
    return level


def profile(amount, total, bound, skew):
    weights = [(1 << 20) // math.isqrt(rank ** skew) + 1 for rank in range(2, amount + 1)]
    rest, given = total - bound - (amount - 1), [1] * (amount - 1)
    while rest > 0:
        movable = [i for i in range(amount - 1) if given[i] < bound]
        mass, remaining = sum([weights[i] for i in movable]), rest
        for i in movable:
            extra = min(bound - given[i], max(1, remaining * weights[i] // mass), rest)
            given[i] = given[i] + extra
            rest = rest - extra
    return np.array([bound] + given)


def uneven(rng, count, total, bound, skew):
    if count == 2:
        one = jax.random.randint(rng, (), max(1, total - bound), min(bound, total - 1) + 1)
        return jnp.stack([one, total - one])
    sizes = jnp.asarray(profile(count, total, bound, skew), jnp.int32)
    twos = (count - 1) // 2
    source_of, taker = sizes[1:1 + 2 * twos:2], sizes[2:2 + 2 * twos:2]
    room = jnp.minimum(source_of - 1, bound - taker)
    shifted = jax.random.randint(jax.random.fold_in(rng, 1), (twos,), 0, 1 << 20) % (room + 1)
    sizes = sizes.at[1:1 + 2 * twos:2].set(source_of - shifted).at[2:2 + 2 * twos:2].set(taker + shifted)
    return sizes[jax.random.permutation(jax.random.fold_in(rng, 2), count)]


def scatter_about(key, dims, width, bound, split=(), kind=jnp.bfloat16):
    result = width * jax.random.normal(key, dims, jnp.float32)
    if split:
        result = result * steps_of(key, dims, split, -0.22, 0.18)
    return jnp.clip(result, -bound, bound).astype(kind)


def setup_inputs(seed: int = 0) -> dict:
    streams_of = jax.random.split(jax.random.key(seed), 15)
    block_input_slots = scatter_about(streams_of[0], (TOKENS, MODEL_WIDTH), 1.0, 6.0, ((0, 16),))
    memory = scatter_about(streams_of[1], (MEMTOK, MODEL_WIDTH), 1.0, 6.0, ((0, 16),))
    target_sentence_lengths = jax.vmap(lambda own: uneven(own, SENTENCE_COUNT, ROW_SLOTS, LONGEST_TARGET, 2))(jax.random.split(streams_of[2], PACKED_ROWS)).reshape((PACKED_ROWS, SENTENCE_COUNT)).astype(jnp.int32)
    source_lengths = jax.vmap(lambda own: uneven(own, SENTENCE_COUNT, MEMLEN, SRCMAX, 2))(jax.random.split(streams_of[3], PACKED_ROWS)).reshape((PACKED_ROWS, SENTENCE_COUNT)).astype(jnp.int32)
    self_qkv = scatter_about(streams_of[4], (3, MODEL_WIDTH, MODEL_WIDTH), MODEL_WIDTH ** -0.5, 0.25, ((2, 2),))
    self_out = scatter_about(streams_of[5], (MODEL_WIDTH, MODEL_WIDTH), (MODEL_WIDTH // 8) ** -0.5, 0.75, ((0, 2),))
    cross_query = scatter_about(streams_of[6], (MODEL_WIDTH, MODEL_WIDTH), MODEL_WIDTH ** -0.5, 0.25, ((1, 2),))
    cross_kv = scatter_about(streams_of[7], (2, MODEL_WIDTH, MODEL_WIDTH), MODEL_WIDTH ** -0.5, 0.25, ((2, 2),))
    cross_out = scatter_about(streams_of[8], (MODEL_WIDTH, MODEL_WIDTH), (MODEL_WIDTH // 8) ** -0.5, 0.75, ((0, 2),))
    up_proj = scatter_about(streams_of[9], (FF, MODEL_WIDTH), MODEL_WIDTH ** -0.5, 0.25, ((0, 2),))
    down_proj = scatter_about(streams_of[10], (FF, MODEL_WIDTH), FF ** -0.5, 0.125, ((0, 2),))
    norm_gains = jnp.clip(1.0 + 0.18 * jax.random.normal(streams_of[11], (MODEL_WIDTH, 3), jnp.float32), 0.1, 1.9)
    norm_biases = scatter_about(streams_of[12], (MODEL_WIDTH, 3), 0.5, 3.0, (), jnp.float32)
    cotangent = scatter_about(streams_of[13], (TOKENS, MODEL_WIDTH), 1.0, 6.0, ((0, 32),))
    return dict(block_input_slots=block_input_slots, memory=memory, target_sentence_lengths=target_sentence_lengths, source_lengths=source_lengths, self_qkv=self_qkv, self_out=self_out, cross_query=cross_query, cross_kv=cross_kv, cross_out=cross_out, up_proj=up_proj, down_proj=down_proj, norm_gains=norm_gains, norm_biases=norm_biases, cotangent=cotangent)


@jax.custom_vjp
def low(v):
    return lax.optimization_barrier(v.astype(jnp.bfloat16)).astype(jnp.float32)

@jax.custom_vjp
def low_back(v):
    return v

def low_keep(v):
    return (low(v), None)

def low_pass(kept, grad):
    return (grad,)

def back_keep(v):
    return (v, None)

def back_low(kept, grad):
    return (low(grad),)
low.defvjp(low_keep, low_pass)
low_back.defvjp(back_keep, back_low)

def segment_labels(lengths, span_len):
    ends_at = jnp.cumsum(lengths, axis=-1).astype(jnp.int32)
    places = jnp.arange(span_len, dtype=jnp.int32)
    return lax.optimization_barrier(jnp.sum((places[None, :, None] >= ends_at[:, None, :]).astype(jnp.int32), axis=-1)).astype(jnp.int32)

def layer_norm(values, gain_vec, shift_vec):
    centre = values - lax.optimization_barrier(jnp.mean(values, axis=-1, keepdims=True))
    spread = lax.optimization_barrier(jnp.mean(centre * centre, axis=-1, keepdims=True))
    return centre * lax.rsqrt(spread + 1e-05) * gain_vec + shift_vec

def block_mask(query_seg, key_seg, first_row, causal):
    same_seg = query_seg[:, None] == key_seg[None, :]
    if causal:
        query_place = first_row + jnp.arange(query_seg.shape[0], dtype=jnp.int32)
        key_place = jnp.arange(key_seg.shape[0], dtype=jnp.int32)
        same_seg = jnp.logical_and(same_seg, query_place[:, None] >= key_place[None, :])
    return same_seg

def attend(query, keys, values, query_seg, key_seg, causal):
    length = query.shape[0]
    block_len = min(512, length)
    score_scale = query.shape[2] ** (-0.5)

    def per_block(block_index):
        first_row = block_index * block_len
        query_blk = lax.dynamic_slice_in_dim(query, first_row, block_len, 0)
        seg_blk = lax.dynamic_slice_in_dim(query_seg, first_row, block_len, 0)
        key_mask = block_mask(seg_blk, key_seg, first_row, causal)
        scores = low_back(jnp.einsum('qhe,khe->hqk', query_blk, keys, precision=lax.Precision.HIGHEST) * score_scale)
        scores = jnp.where(key_mask[None], scores, -1e+30)
        row_top = lax.optimization_barrier(jnp.max(scores, axis=-1, keepdims=True))
        exp_scores = jnp.exp(scores - row_top)
        prob_low = low(exp_scores / lax.optimization_barrier(jnp.sum(exp_scores, axis=-1, keepdims=True)))
        return jnp.einsum('hqk,khe->qhe', prob_low, values, precision=lax.Precision.HIGHEST)
    context = lax.map(jax.checkpoint(per_block), jnp.arange(length // block_len, dtype=jnp.int32))
    return context.reshape(query.shape)

def row_forward(params, input_row, memory_row, target_segment, source_seg):
    self_qkv, self_out, cross_query, cross_kv, cross_out, up_proj, down_proj, norm_gains, norm_biases = params
    length = input_row.shape[0]
    mem_len = memory_row.shape[0]
    hp = lax.Precision.HIGHEST
    self_proj = low_back(low(jnp.einsum('td,cde->cte', input_row, self_qkv, precision=hp)))
    self_proj = self_proj.reshape(3, length, HEADS, DH)
    context = attend(self_proj[0], self_proj[1], self_proj[2], target_segment, target_segment, True)
    context = low_back(low(context.reshape(length, MODEL_WIDTH)))
    sum_one = input_row + low_back(jnp.dot(context, self_out, precision=hp))
    normed_one = low(layer_norm(sum_one, norm_gains[:, 0], norm_biases[:, 0]))
    cross_q = low_back(low(jnp.dot(normed_one, cross_query, precision=hp)))
    cross_pair = low_back(low(jnp.einsum('md,cde->cme', memory_row, cross_kv, precision=hp)))
    cross_pair = cross_pair.reshape(2, mem_len, HEADS, DH)
    cross_ctx = attend(cross_q.reshape(length, HEADS, DH), cross_pair[0], cross_pair[1], target_segment, source_seg, False)
    cross_ctx = low_back(low(cross_ctx.reshape(length, MODEL_WIDTH)))
    sum_two = normed_one + low_back(jnp.dot(cross_ctx, cross_out, precision=hp))
    normed_two = low(layer_norm(sum_two, norm_gains[:, 1], norm_biases[:, 1]))
    pre_act = low_back(jnp.einsum('td,fd->tf', normed_two, up_proj, precision=hp))
    hidden = low(jax.nn.silu(pre_act))
    ffn_value = low_back(jnp.einsum('tf,fd->td', hidden, down_proj, precision=hp))
    sum_three = normed_two + ffn_value
    return layer_norm(sum_three, norm_gains[:, 2], norm_biases[:, 2])

def reference(block_input_slots, memory, target_sentence_lengths, source_lengths, self_qkv, self_out, cross_query, cross_kv, cross_out, up_proj, down_proj, norm_gains, norm_biases, cotangent):
    params = (self_qkv.astype(jnp.float32), self_out.astype(jnp.float32), cross_query.astype(jnp.float32), cross_kv.astype(jnp.float32), cross_out.astype(jnp.float32), up_proj.astype(jnp.float32), down_proj.astype(jnp.float32), norm_gains.astype(jnp.float32), norm_biases.astype(jnp.float32))
    target_segment = segment_labels(target_sentence_lengths, ROW_SLOTS)
    source_seg = segment_labels(source_lengths, MEMLEN)
    packed_input_rows = block_input_slots.astype(jnp.float32).reshape(PACKED_ROWS, ROW_SLOTS, MODEL_WIDTH)
    memory_rows = memory.astype(jnp.float32).reshape(PACKED_ROWS, MEMLEN, MODEL_WIDTH)
    cotangent_rows = cotangent.astype(jnp.float32).reshape(PACKED_ROWS, ROW_SLOTS, MODEL_WIDTH)

    def row_step(totals, row_items):
        input_row, memory_row, seg_t, seg_s, cot_row = row_items

        def forward_only(param_set, input_vals, memory_vals):
            return row_forward(param_set, input_vals, memory_vals, seg_t, seg_s)
        out_row, back_fn = jax.vjp(forward_only, params, input_row, memory_row)
        grad_params, grad_input, grad_memory = back_fn(cot_row)
        totals = jax.tree.map(lambda accum, addend: accum + addend, totals, grad_params)
        return (totals, (out_row.astype(jnp.bfloat16), grad_input, grad_memory))
    empty_sums = jax.tree.map(jnp.zeros_like, params)
    totals, (out_rows, grad_rows, memory_rows_grad) = lax.scan(row_step, empty_sums, (packed_input_rows, memory_rows, target_segment, source_seg, cotangent_rows))
    return (out_rows.reshape(TOKENS, MODEL_WIDTH), grad_rows.reshape(TOKENS, MODEL_WIDTH), memory_rows_grad.reshape(MEMTOK, MODEL_WIDTH), totals[0], totals[1], totals[2], totals[3], totals[4], totals[5], totals[6], totals[7], totals[8])
```

```python
import functools
import math

import jax
import jax.numpy as jnp
from jax import lax
from jax.experimental import pallas as pl
from jax.experimental.pallas import tpu as pltpu
from jax.sharding import PartitionSpec as P

DH = 64
NEG = -1e30
F32 = jnp.float32
BF16 = jnp.bfloat16
SCALE = DH**-0.5
SCALE2 = SCALE * math.log2(math.e)
NT = (((1,), (1,)), ((), ()))
NN = (((1,), (0,)), ((), ()))
TN = (((0,), (0,)), ((), ()))
VMEM_BYTES = 50 << 20


def mm(a, b, dims=NN):
    return lax.dot_general(a, b, dims, preferred_element_type=F32)


def params(semantics=("arbitrary",)):
    return pltpu.CompilerParams(dimension_semantics=semantics, vmem_limit_bytes=VMEM_BYTES)


def cost(flops, nbytes, exps=0):
    return pl.CostEstimate(flops=int(flops), bytes_accessed=int(nbytes), transcendentals=int(exps))


def pick(i, per_part, refs):
    value = refs[0][...]
    for r in range(1, len(refs)):
        value = jnp.where(i >= r * per_part, refs[r][...], value)
    return value


def part_map(r, per_part):
    return lambda i, sc: (jnp.clip(i - r * per_part, 0, per_part - 1), 0)


def attend_kernel(nblk, per_part, n_q, n_out, heads, bq, bk, sc, *refs):
    q_refs, refs = refs[:n_q], refs[n_q:]
    k_ref, v_ref, lo_ref, hi_ref = refs[:4]
    out_refs, (lse_ref, m_ref, l_ref, acc_ref) = refs[4 : 4 + n_out], refs[4 + n_out :]
    i = pl.program_id(0)
    q = pick(i, per_part, q_refs)
    lo = lo_ref[...]
    hi = hi_ref[...]
    m_ref[...] = jnp.full_like(m_ref, NEG)
    l_ref[...] = jnp.zeros_like(l_ref)
    acc_ref[...] = jnp.zeros_like(acc_ref)
    place = lax.broadcasted_iota(jnp.int32, (bk, bq), 0)

    def step(kb, carry):
        start = pl.multiple_of(kb * bk, bk)
        k = k_ref[pl.ds(start, bk), :]
        v = v_ref[pl.ds(start, bk), :]
        keep = jnp.logical_and(place >= lo - start, place < hi - start)
        for h in range(heads):
            cols = slice(h * DH, (h + 1) * DH)
            s = mm(k[:, cols], q[:, cols], NT) * SCALE2
            s = jnp.where(keep, s, NEG)
            m_old = m_ref[h : h + 1, :]
            m_new = jnp.maximum(m_old, jnp.max(s, axis=0, keepdims=True))
            p = jnp.exp2(s - m_new)
            decay = jnp.exp2(m_old - m_new)
            m_ref[h : h + 1, :] = m_new
            l_ref[h : h + 1, :] = l_ref[h : h + 1, :] * decay + jnp.sum(p, axis=0, keepdims=True)
            acc_ref[cols, :] = acc_ref[cols, :] * decay + mm(v[:, cols], p.astype(BF16), TN)
        return carry

    lax.fori_loop(sc[i], sc[nblk + i], step, 0)
    for h in range(heads):
        cols = slice(h * DH, (h + 1) * DH)
        acc_ref[cols, :] = acc_ref[cols, :] / l_ref[h : h + 1, :]
    ctx = acc_ref[...].T.astype(BF16)
    for r in range(n_out):

        @pl.when(jnp.logical_and(i >= r * per_part, i < (r + 1) * per_part))
        def _():
            out_refs[r][...] = ctx

    lse_ref[0, :, :] = m_ref[...] + jnp.log2(l_ref[...])


def attend(sc, q_parts, keys, values, lo, hi, mp, bq, bk):
    tokens, width = sum(q.shape[0] for q in q_parts), keys.shape[1]
    heads = width // DH
    nblk, per_part = tokens // bq, tokens // bq // mp
    if len(q_parts) == 1 and mp > 1:
        q_specs = [pl.BlockSpec((bq, width), lambda i, sc: (sc[2 * nblk + i], 0))]
    else:
        q_specs = [pl.BlockSpec((bq, width), part_map(r, per_part)) for r in range(mp)]
    full = pl.BlockSpec(keys.shape, lambda i, sc: (0, 0))
    row = pl.BlockSpec((1, bq), lambda i, sc: (0, i))
    per_pick = per_part if len(q_parts) > 1 else nblk
    outs = pl.pallas_call(
        functools.partial(attend_kernel, nblk, per_part, len(q_parts), mp, heads, bq, bk),
        grid_spec=pltpu.PrefetchScalarGridSpec(
            num_scalar_prefetch=1,
            grid=(nblk,),
            in_specs=q_specs + [full, full, row, row],
            out_specs=[pl.BlockSpec((bq, width), part_map(r, per_part)) for r in range(mp)]
            + [pl.BlockSpec((1, heads, bq), lambda i, sc: (i, 0, 0))],
            scratch_shapes=[
                pltpu.VMEM((heads, bq), F32),
                pltpu.VMEM((heads, bq), F32),
                pltpu.VMEM((width, bq), F32),
            ],
        ),
        out_shape=[jax.ShapeDtypeStruct((tokens // mp, width), BF16)] * mp
        + [jax.ShapeDtypeStruct((nblk, heads, bq), F32)],
        compiler_params=params(),
        cost_estimate=cost(4 * tokens * 512 * width, 8 * tokens * width, tokens * 512 * heads),
    )(sc, *q_parts, keys, values, lo, hi)
    return outs[:mp], outs[mp]


def attend_back_kernel(nblk, per_part, n_q, n_part, heads, bq, bk, sc, *refs):
    q_refs, refs = refs[:n_q], refs[n_q:]
    do_refs, refs = refs[:n_part], refs[n_part:]
    o_refs, refs = refs[:n_part], refs[n_part:]
    k_ref, v_ref, lo_ref, hi_ref, lse_ref = refs[:5]
    dq_refs, refs = refs[5 : 5 + n_q], refs[5 + n_q :]
    dk_ref, dv_ref, dk_acc, dv_acc, dq_acc, delta_ref = refs
    i = pl.program_id(0)

    @pl.when(i == 0)
    def _():
        dk_acc[...] = jnp.zeros_like(dk_acc)
        dv_acc[...] = jnp.zeros_like(dv_acc)

    q = pick(i, per_part, q_refs)
    do = pick(i, per_part, do_refs)
    o = pick(i, per_part, o_refs)
    lo = lo_ref[...]
    hi = hi_ref[...]
    prod = (do.astype(F32) * o.astype(F32)).T
    for h in range(heads):
        delta_ref[h : h + 1, :] = jnp.sum(prod[h * DH : (h + 1) * DH, :], axis=0, keepdims=True)
    dq_acc[...] = jnp.zeros_like(dq_acc)
    place = lax.broadcasted_iota(jnp.int32, (bk, bq), 0)

    def step(kb, carry):
        start = pl.multiple_of(kb * bk, bk)
        k = k_ref[pl.ds(start, bk), :]
        v = v_ref[pl.ds(start, bk), :]
        keep = jnp.logical_and(place >= lo - start, place < hi - start)
        dks, dvs = [], []
        for h in range(heads):
            cols = slice(h * DH, (h + 1) * DH)
            s = mm(k[:, cols], q[:, cols], NT) * SCALE2 - lse_ref[0, h : h + 1, :]
            p = jnp.where(keep, jnp.exp2(s), 0.0)
            dp = mm(v[:, cols], do[:, cols], NT)
            ds = (p * (dp - delta_ref[h : h + 1, :])).astype(BF16)
            dvs.append(mm(p.astype(BF16), do[:, cols]))
            dks.append(mm(ds, q[:, cols]))
            dq_acc[cols, :] += mm(k[:, cols], ds, TN)
        rows = pl.ds(start, bk)
        dk_acc[rows, :] += jnp.concatenate(dks, axis=1)
        dv_acc[rows, :] += jnp.concatenate(dvs, axis=1)
        return carry

    lax.fori_loop(sc[i], sc[nblk + i], step, 0)
    dq = (dq_acc[...] * SCALE).T.astype(BF16)
    if n_q == 1:
        dq_refs[0][...] = dq
    else:
        for r in range(n_q):

            @pl.when(jnp.logical_and(i >= r * per_part, i < (r + 1) * per_part))
            def _():
                dq_refs[r][...] = dq

    @pl.when(i == nblk - 1)
    def _():
        dk_ref[...] = (dk_acc[...] * SCALE).astype(BF16)
        dv_ref[...] = dv_acc[...].astype(BF16)


def attend_back(sc, q_parts, do_parts, o_parts, keys, values, lo, hi, lse, mp, bq, bk):
    tokens, width = sum(q.shape[0] for q in q_parts), keys.shape[1]
    heads = width // DH
    nblk, per_part = tokens // bq, tokens // bq // mp
    parts = [pl.BlockSpec((bq, width), part_map(r, per_part)) for r in range(mp)]
    if len(q_parts) == 1 and mp > 1:
        q_specs = [pl.BlockSpec((bq, width), lambda i, sc: (sc[2 * nblk + i], 0))]
    else:
        q_specs = parts
    full = pl.BlockSpec(keys.shape, lambda i, sc: (0, 0))
    row = pl.BlockSpec((1, bq), lambda i, sc: (0, i))
    outs = pl.pallas_call(
        functools.partial(attend_back_kernel, nblk, per_part, len(q_parts), mp, heads, bq, bk),
        grid_spec=pltpu.PrefetchScalarGridSpec(
            num_scalar_prefetch=1,
            grid=(nblk,),
            in_specs=q_specs
            + parts
            + parts
            + [full, full, row, row, pl.BlockSpec((1, heads, bq), lambda i, sc: (i, 0, 0))],
            out_specs=q_specs + [full, full],
            scratch_shapes=[
                pltpu.VMEM(keys.shape, F32),
                pltpu.VMEM(keys.shape, F32),
                pltpu.VMEM((width, bq), F32),
                pltpu.VMEM((heads, bq), F32),
            ],
        ),
        out_shape=[jax.ShapeDtypeStruct(q.shape, BF16) for q in q_parts]
        + [jax.ShapeDtypeStruct(keys.shape, BF16)] * 2,
        compiler_params=params(),
        cost_estimate=cost(10 * tokens * 512 * width, 12 * tokens * width, tokens * 512 * heads),
    )(sc, *q_parts, *do_parts, *o_parts, keys, values, lo, hi, lse)
    return outs[: len(q_parts)], outs[-2], outs[-1]


def norm_stats(a):
    centre = a - jnp.mean(a, axis=-1, keepdims=True)
    rstd = lax.rsqrt(jnp.mean(centre * centre, axis=-1, keepdims=True) + 1e-05)
    return centre * rstd, rstd


def norm_back(dy, xhat, rstd, gain):
    t = dy * gain
    mean_t = jnp.mean(t, axis=-1, keepdims=True)
    mean_tx = jnp.mean(t * xhat, axis=-1, keepdims=True)
    return rstd * (t - mean_t - xhat * mean_tx)


def post_self_kernel(mp, sc, *refs):
    x_ref = refs[0]
    ctx, wo, cq = refs[1 : 1 + mp], refs[1 + mp : 1 + 2 * mp], refs[1 + 2 * mp : 1 + 3 * mp]
    gain_ref, shift_ref = refs[1 + 3 * mp : 3 + 3 * mp]
    n1_ref, xhat_ref, rstd_ref = refs[3 + 3 * mp : 6 + 3 * mp]
    qc = refs[6 + 3 * mp :]
    a1 = x_ref[...].astype(F32)
    for r in range(mp):
        a1 += mm(ctx[r][...], wo[r][...])
    xhat, rstd = norm_stats(a1)
    n1 = (xhat * gain_ref[0:1, :] + shift_ref[0:1, :]).astype(BF16)
    n1_ref[...] = n1
    xhat_ref[...] = xhat
    rstd_ref[...] = rstd
    for r in range(mp):
        qc[r][...] = mm(n1, cq[r][...]).astype(BF16)


def whole(a):
    return pl.BlockSpec(a.shape, lambda i, sc: (0,) * a.ndim)


def rows_of(bt, width):
    return pl.BlockSpec((bt, width), lambda i, sc: (i, 0))


def post_self(sc, x, ctx, wo, cq, gain, shift, share, bt):
    mp, d = len(ctx), x.shape[1]
    width = ctx[0].shape[1]
    nb = share // bt
    outs = pl.pallas_call(
        functools.partial(post_self_kernel, mp),
        grid_spec=pltpu.PrefetchScalarGridSpec(
            num_scalar_prefetch=1,
            grid=(nb,),
            in_specs=[pl.BlockSpec((bt, d), lambda i, sc: (sc[0] * nb + i, 0))]
            + [rows_of(bt, width)] * mp
            + [whole(w) for w in (*wo, *cq, gain, shift)],
            out_specs=[rows_of(bt, d), rows_of(bt, d), rows_of(bt, 1)] + [rows_of(bt, width)] * mp,
        ),
        out_shape=[
            jax.ShapeDtypeStruct((share, d), BF16),
            jax.ShapeDtypeStruct((share, d), F32),
            jax.ShapeDtypeStruct((share, 1), F32),
        ]
        + [jax.ShapeDtypeStruct((share, width), BF16)] * mp,
        compiler_params=params(),
        cost_estimate=cost(4 * share * d * d, share * d * 12),
    )(sc, x, *ctx, *wo, *cq, gain, shift)
    return outs[0], outs[1], outs[2], outs[3:]


def middle_kernel(mp, *refs):
    refs = list(refs)

    def take(n):
        got = refs[:n]
        del refs[:n]
        return got

    cctx, (n1_ref, cot_ref) = take(mp), take(2)
    co, up, down = take(mp), take(mp), take(mp)
    gain_ref, shift_ref = take(2)
    out_ref, da2_ref, n2_ref, e3_ref, e2_ref = take(5)
    dcctx, hid, dpre = take(mp), take(mp), take(mp)
    (small_ref,) = take(1)
    (slope_ref,) = take(1)
    ff = up[0].shape[0]
    i = pl.program_id(0)

    a2 = n1_ref[...].astype(F32)
    for r in range(mp):
        a2 += mm(cctx[r][...], co[r][...])
    xhat2, rstd2 = norm_stats(a2)
    n2 = (xhat2 * gain_ref[1:2, :] + shift_ref[1:2, :]).astype(BF16)
    n2_ref[...] = n2
    a3 = n2.astype(F32)
    for r in range(mp):
        u = mm(n2, up[r][...], NT)
        sg = 1.0 / (1.0 + jnp.exp(-u))
        h = u * sg
        hid[r][...] = h.astype(BF16)
        slope_ref[:, r * ff : (r + 1) * ff] = sg + h * (1.0 - sg)
        a3 += mm(hid[r][...], down[r][...])
    xhat3, rstd3 = norm_stats(a3)
    out_ref[...] = (xhat3 * gain_ref[2:3, :] + shift_ref[2:3, :]).astype(BF16)
    g = cot_ref[...].astype(F32)
    da3 = norm_back(g, xhat3, rstd3, gain_ref[2:3, :])
    e3 = da3.astype(BF16)
    e3_ref[...] = e3
    dn2 = da3
    for r in range(mp):
        dh = mm(e3, down[r][...], NT)
        dpre[r][...] = (dh * slope_ref[:, r * ff : (r + 1) * ff]).astype(BF16)
        dn2 += mm(dpre[r][...], up[r][...])
    da2 = norm_back(dn2, xhat2, rstd2, gain_ref[1:2, :])
    da2_ref[...] = da2
    e2 = da2.astype(BF16)
    e2_ref[...] = e2
    for r in range(mp):
        dcctx[r][...] = mm(e2, co[r][...], NT).astype(BF16)
    sums = jnp.concatenate(
        [
            jnp.sum(dn2 * xhat2, axis=0, keepdims=True),
            jnp.sum(g * xhat3, axis=0, keepdims=True),
            jnp.sum(dn2, axis=0, keepdims=True),
            jnp.sum(g, axis=0, keepdims=True),
        ],
        axis=0,
    )

    @pl.when(i == 0)
    def _():
        small_ref[...] = sums

    @pl.when(i > 0)
    def _():
        small_ref[...] += sums


def middle(cctx, n1, cot, co, up, down, gain, shift, bt):
    mp = len(cctx)
    share, d = n1.shape
    width = cctx[0].shape[1]
    ff = up[0].shape[0]
    row = lambda w: pl.BlockSpec((bt, w), lambda i: (i, 0))
    all_of = lambda a: pl.BlockSpec(a.shape, lambda i: (0,) * a.ndim)
    shape = lambda w, t: jax.ShapeDtypeStruct((share, w), t)
    outs = pl.pallas_call(
        functools.partial(middle_kernel, mp),
        grid=(share // bt,),
        in_specs=[row(width)] * mp + [row(d)] * 2 + [all_of(w) for w in (*co, *up, *down, gain, shift)],
        out_specs=[row(d)] * 5
        + [row(width)] * mp
        + [row(ff)] * (2 * mp)
        + [pl.BlockSpec((4, d), lambda i: (0, 0))],
        scratch_shapes=[pltpu.VMEM((bt, ff * mp), F32)],
        out_shape=[shape(d, BF16), shape(d, F32), shape(d, BF16), shape(d, BF16), shape(d, BF16)]
        + [shape(width, BF16)] * mp
        + [shape(ff, BF16)] * (2 * mp)
        + [jax.ShapeDtypeStruct((4, d), F32)],
        compiler_params=params(),
        cost_estimate=cost(8 * share * d * ff * mp + 4 * share * d * d, share * ff * mp * 4, share * ff * mp),
    )(*cctx, n1, cot, *co, *up, *down, gain, shift)
    out, da2, n2, e3, e2 = outs[:5]
    return out, da2, n2, e3, e2, outs[5 : 5 + mp], outs[5 + mp : 5 + 2 * mp], outs[5 + 2 * mp : 5 + 3 * mp], outs[-1]


def pre_self_kernel(mp, *refs):
    dqc, cq, wo = refs[:mp], refs[mp : 2 * mp], refs[2 * mp : 3 * mp]
    da2_ref, xhat_ref, rstd_ref, gain_ref = refs[3 * mp : 3 * mp + 4]
    da1_ref, e1_ref = refs[3 * mp + 4 : 3 * mp + 6]
    dctx = refs[3 * mp + 6 : 4 * mp + 6]
    small_ref = refs[4 * mp + 6]
    i = pl.program_id(0)
    dn1 = da2_ref[...]
    for r in range(mp):
        dn1 += mm(dqc[r][...], cq[r][...], NT)
    xhat = xhat_ref[...]
    da1 = norm_back(dn1, xhat, rstd_ref[...], gain_ref[0:1, :])
    da1_ref[...] = da1
    e1 = da1.astype(BF16)
    e1_ref[...] = e1
    for r in range(mp):
        dctx[r][...] = mm(e1, wo[r][...], NT).astype(BF16)
    sums = jnp.concatenate(
        [jnp.sum(dn1 * xhat, axis=0, keepdims=True), jnp.sum(dn1, axis=0, keepdims=True)], axis=0
    )

    @pl.when(i == 0)
    def _():
        small_ref[...] = sums

    @pl.when(i > 0)
    def _():
        small_ref[...] += sums


def pre_self(dqc, cq, wo, da2, xhat, rstd, gain, bt):
    mp = len(dqc)
    share, d = da2.shape
    width = dqc[0].shape[1]
    row = lambda w: pl.BlockSpec((bt, w), lambda i: (i, 0))
    all_of = lambda a: pl.BlockSpec(a.shape, lambda i: (0,) * a.ndim)
    outs = pl.pallas_call(
        functools.partial(pre_self_kernel, mp),
        grid=(share // bt,),
        in_specs=[row(width)] * mp
        + [all_of(w) for w in (*cq, *wo)]
        + [row(d), row(d), row(1), all_of(gain)],
        out_specs=[row(d), row(d)] + [row(width)] * mp + [pl.BlockSpec((2, d), lambda i: (0, 0))],
        out_shape=[jax.ShapeDtypeStruct((share, d), F32), jax.ShapeDtypeStruct((share, d), BF16)]
        + [jax.ShapeDtypeStruct((share, width), BF16)] * mp
        + [jax.ShapeDtypeStruct((2, d), F32)],
        compiler_params=params(),
        cost_estimate=cost(4 * share * d * d, share * d * 14),
    )(*dqc, *cq, *wo, da2, xhat, rstd, gain)
    return outs[0], outs[1], outs[2 : 2 + mp], outs[-1]


def part_kernel(n_in, n_out, per_part, sc, *refs):
    grads, w_ref, outs = refs[:n_in], refs[n_in], refs[n_in + 1 :]
    i = pl.program_id(0)
    total = mm(grads[0][...], w_ref[0], NT)
    for c in range(1, n_in):
        total += mm(grads[c][...], w_ref[c], NT)
    for r in range(n_out):

        @pl.when(jnp.logical_and(i >= r * per_part, i < (r + 1) * per_part))
        def _():
            outs[r][...] = total.astype(outs[r].dtype)


def input_part(sc, grads, w, mp, bt):
    tokens, width = grads[0].shape
    d = w.shape[1]
    nblk = tokens // bt
    per_part = nblk // mp
    outs = pl.pallas_call(
        functools.partial(part_kernel, len(grads), mp, per_part),
        grid_spec=pltpu.PrefetchScalarGridSpec(
            num_scalar_prefetch=1,
            grid=(nblk,),
            in_specs=[pl.BlockSpec((bt, width), lambda i, sc: (sc[i], 0))] * len(grads) + [whole(w)],
            out_specs=[pl.BlockSpec((bt, d), part_map(r, per_part)) for r in range(mp)],
        ),
        out_shape=[jax.ShapeDtypeStruct((tokens // mp, d), F32)]
        + [jax.ShapeDtypeStruct((tokens // mp, d), BF16)] * (mp - 1),
        compiler_params=params(),
        cost_estimate=cost(2 * tokens * d * width * len(grads), tokens * d * 6),
    )(sc, *grads, w)
    return outs


def shards(
    block_input_slots,
    memory,
    target_sentence_lengths,
    source_lengths,
    self_qkv,
    self_out,
    cross_query,
    cross_kv,
    cross_out,
    up_proj,
    down_proj,
    norm_gains,
    norm_biases,
    cotangent,
    mp,
):
    tokens, d = block_input_slots.shape
    mem_tokens = memory.shape[0]
    share = cotangent.shape[0]
    mem_share = mem_tokens // mp
    width = self_qkv.shape[2]
    me = lax.axis_index("mp")
    bt = min(256, share)
    bq = min(256, share)
    bk = min(256, mem_tokens)

    def spread(own):
        return [own] + [
            lax.ppermute(own, "mp", [(i, (i + r) % mp) for i in range(mp)]) for r in range(1, mp)
        ]

    def exchange(pieces):
        got = [pieces[0]] + [None] * (mp - 1)
        for r in range(1, mp):
            got[mp - r] = lax.ppermute(pieces[r], "mp", [(i, (i - r) % mp) for i in range(mp)])
        return got

    wo, cq, co = spread(self_out), spread(cross_query), spread(cross_out)
    up, down = spread(up_proj), spread(down_proj)
    gain, shift = norm_gains.T, norm_biases.T

    t_len = target_sentence_lengths.reshape(-1)
    s_len = source_lengths.reshape(-1)
    t_end, s_end = jnp.cumsum(t_len), jnp.cumsum(s_len)
    t_start, s_start = t_end - t_len, s_end - s_len
    first = ((me - jnp.arange(mp)) % mp) * share
    place = (first[:, None] + jnp.arange(share)[None, :]).reshape(-1).astype(jnp.int32)
    begun = place[:, None] >= t_start[None, :]
    self_lo = jnp.max(jnp.where(begun, t_start[None, :], 0), axis=1)
    self_hi = place + 1
    cross_lo = jnp.max(jnp.where(begun, s_start[None, :], 0), axis=1)
    cross_hi = jnp.max(jnp.where(begun, s_end[None, :], 0), axis=1)
    nblk = tokens // bq
    q_block = place.reshape(nblk, bq)[:, 0] // bq

    def table(lo, hi):
        return jnp.concatenate(
            [lo.reshape(nblk, bq)[:, 0] // bk, (hi.reshape(nblk, bq)[:, -1] + bk - 1) // bk, q_block]
        ).astype(jnp.int32)

    self_table, cross_table = table(self_lo, self_hi), table(cross_lo, cross_hi)
    as_row = lambda v: v.reshape(1, tokens).astype(jnp.int32)
    self_lo, self_hi, cross_lo, cross_hi = map(as_row, (self_lo, self_hi, cross_lo, cross_hi))

    proj = [
        jnp.dot(block_input_slots, self_qkv[c], preferred_element_type=F32).astype(BF16) for c in range(3)
    ]
    pair = [jnp.dot(memory, cross_kv[c], preferred_element_type=F32).astype(BF16) for c in range(2)]
    ctx_parts, self_lse = attend(
        self_table, proj[:1], proj[1], proj[2], self_lo, self_hi, mp, bq, bk
    )
    ctx = exchange(ctx_parts)
    me_row = me.reshape(1).astype(jnp.int32)
    n1, xhat1, rstd1, qc = post_self(me_row, block_input_slots, ctx, wo, cq, gain, shift, share, bt)
    qc_parts = exchange(qc)
    cctx_parts, cross_lse = attend(
        cross_table, qc_parts, pair[0], pair[1], cross_lo, cross_hi, mp, bq, bk
    )
    cctx = exchange(cctx_parts)
    layer_output, da2, n2, e3, e2, dcctx, hid, dpre, small23 = middle(
        cctx, n1, cotangent, co, up, down, gain, shift, bt
    )
    dcctx_parts = exchange(dcctx)

    def grads(lefts, rights):
        return [mm(a, b, TN).astype(BF16) for a, b in zip(lefts, rights)]

    def collect(pieces):
        got = exchange(pieces)
        total = got[0].astype(F32)
        for g in got[1:]:
            total += g.astype(F32)
        return total

    down_grad = collect(grads(hid, [e3] * mp))
    up_grad = collect(grads(dpre, [n2] * mp))
    cross_out_grad = collect(grads(cctx, [e2] * mp))
    dqc_parts, dkc, dvc = attend_back(
        cross_table, qc_parts, dcctx_parts, cctx_parts, pair[0], pair[1], cross_lo, cross_hi, cross_lse, mp, bq, bk
    )
    dqc = exchange(dqc_parts)
    da1, e1, dctx, small1 = pre_self(dqc, cq, wo, da2, xhat1, rstd1, gain, bt)
    dctx_parts = exchange(dctx)
    mem_bt = min(256, mem_share)
    mem_nb = mem_share // mem_bt
    mem_blocks = ((((me - jnp.arange(mp)) % mp) * mem_nb)[:, None] + jnp.arange(mem_nb)[None, :]).reshape(-1)
    memory_parts = input_part(mem_blocks.astype(jnp.int32), [dkc, dvc], cross_kv, mp, mem_bt)
    memory_grad = collect(memory_parts)
    cross_kv_grad = jnp.stack([mm(memory, g, TN) for g in (dkc, dvc)])
    cross_query_grad = collect(grads([n1] * mp, dqc))
    self_out_grad = collect(grads(ctx, [e1] * mp))
    (dq,), dk, dv = attend_back(
        self_table, proj[:1], dctx_parts, ctx_parts, proj[1], proj[2], self_lo, self_hi, self_lse, mp, bq, bk
    )
    input_parts = input_part(q_block.astype(jnp.int32), [dq, dk, dv], self_qkv, mp, bq)
    input_grad = collect(input_parts) + da1
    self_qkv_grad = jnp.stack([mm(block_input_slots, g, TN) for g in (dq, dk, dv)])

    small = jnp.concatenate([small1[:1], small23[:2], small1[1:], small23[2:]], axis=0)
    part = d // mp
    pieces = [
        lax.dynamic_slice_in_dim(small, ((me - r) % mp) * part, part, 1).astype(BF16) for r in range(mp)
    ]
    small = collect(pieces)
    summed = [
        lax.psum(g.astype(BF16), "batch").astype(F32)
        for g in (
            self_qkv_grad,
            self_out_grad,
            cross_query_grad,
            cross_kv_grad,
            cross_out_grad,
            up_grad,
            down_grad,
            small,
        )
    ]
    small = summed[-1].T
    return (layer_output, input_grad, memory_grad, *summed[:-1], small[:, :3], small[:, 3:])


def solution(mesh):
    mp = mesh.shape["mp"]
    rows = P("batch", None)
    both = P(("batch", "mp"), None)
    first, last, last3 = P("mp", None), P(None, "mp"), P(None, None, "mp")
    return jax.shard_map(
        functools.partial(shards, mp=mp),
        mesh=mesh,
        in_specs=(rows, rows, rows, rows, last3, first, last, last3, first, first, first, P(), P(), both),
        out_specs=(both, both, both, last3, first, last, last3, first, first, first, first, first),
        check_vma=False,
    )
```

```python
import functools
import math

import jax
import jax.numpy as jnp
from jax import lax
from jax.experimental import pallas as pl
from jax.experimental.pallas import tpu as pltpu
from jax.sharding import PartitionSpec as P

DH = 64
NEG = -1e30
F32 = jnp.float32
BF16 = jnp.bfloat16
SCALE = DH**-0.5
SCALE2 = SCALE * math.log2(math.e)
NT = (((1,), (1,)), ((), ()))
NN = (((1,), (0,)), ((), ()))
TN = (((0,), (0,)), ((), ()))
VMEM_BYTES = 50 << 20


def mm(a, b, dims=NN):
    return lax.dot_general(a, b, dims, preferred_element_type=F32)


def params(semantics=("arbitrary",)):
    return pltpu.CompilerParams(dimension_semantics=semantics, vmem_limit_bytes=VMEM_BYTES)


def cost(flops, nbytes, exps=0):
    return pl.CostEstimate(flops=int(flops), bytes_accessed=int(nbytes), transcendentals=int(exps))


def pick(i, per_part, refs):
    value = refs[0][...]
    for r in range(1, len(refs)):
        value = jnp.where(i >= r * per_part, refs[r][...], value)
    return value


def part_map(r, per_part):
    return lambda i, sc: (jnp.clip(i - r * per_part, 0, per_part - 1), 0)


def attend_kernel(nblk, per_part, n_q, n_out, heads, bq, bk, sc, *refs):
    q_refs, refs = refs[:n_q], refs[n_q:]
    k_ref, v_ref, lo_ref, hi_ref = refs[:4]
    out_refs, (lse_ref, m_ref, l_ref, acc_ref) = refs[4 : 4 + n_out], refs[4 + n_out :]
    i = pl.program_id(0)
    q = pick(i, per_part, q_refs)
    lo = lo_ref[...]
    hi = hi_ref[...]
    m_ref[...] = jnp.full_like(m_ref, NEG)
    l_ref[...] = jnp.zeros_like(l_ref)
    acc_ref[...] = jnp.zeros_like(acc_ref)
    place = lax.broadcasted_iota(jnp.int32, (bk, bq), 0)

    def step(kb, carry):
        start = pl.multiple_of(kb * bk, bk)
        k = k_ref[pl.ds(start, bk), :]
        v = v_ref[pl.ds(start, bk), :]
        keep = jnp.logical_and(place >= lo - start, place < hi - start)
        for h in range(heads):
            cols = slice(h * DH, (h + 1) * DH)
            s = mm(k[:, cols], q[:, cols], NT) * SCALE2
            s = jnp.where(keep, s, NEG)
            m_old = m_ref[h : h + 1, :]
            m_new = jnp.maximum(m_old, jnp.max(s, axis=0, keepdims=True))
            p = jnp.exp2(s - m_new)
            decay = jnp.exp2(m_old - m_new)
            m_ref[h : h + 1, :] = m_new
            l_ref[h : h + 1, :] = l_ref[h : h + 1, :] * decay + jnp.sum(p, axis=0, keepdims=True)
            acc_ref[cols, :] = acc_ref[cols, :] * decay + mm(v[:, cols], p.astype(BF16), TN)
        return carry

    lax.fori_loop(sc[i], sc[nblk + i], step, 0)
    for h in range(heads):
        cols = slice(h * DH, (h + 1) * DH)
        acc_ref[cols, :] = acc_ref[cols, :] / l_ref[h : h + 1, :]
    ctx = acc_ref[...].T.astype(BF16)
    for r in range(n_out):

        @pl.when(jnp.logical_and(i >= r * per_part, i < (r + 1) * per_part))
        def _():
            out_refs[r][...] = ctx

    lse_ref[0, :, :] = m_ref[...] + jnp.log2(l_ref[...])


def attend(sc, q_parts, keys, values, lo, hi, mp, bq, bk):
    tokens, width = sum(q.shape[0] for q in q_parts), keys.shape[1]
    heads = width // DH
    nblk, per_part = tokens // bq, tokens // bq // mp
    if len(q_parts) == 1 and mp > 1:
        q_specs = [pl.BlockSpec((bq, width), lambda i, sc: (sc[2 * nblk + i], 0))]
    else:
        q_specs = [pl.BlockSpec((bq, width), part_map(r, per_part)) for r in range(mp)]
    full = pl.BlockSpec(keys.shape, lambda i, sc: (0, 0))
    row = pl.BlockSpec((1, bq), lambda i, sc: (0, i))
    per_pick = per_part if len(q_parts) > 1 else nblk
    outs = pl.pallas_call(
        functools.partial(attend_kernel, nblk, per_part, len(q_parts), mp, heads, bq, bk),
        grid_spec=pltpu.PrefetchScalarGridSpec(
            num_scalar_prefetch=1,
            grid=(nblk,),
            in_specs=q_specs + [full, full, row, row],
            out_specs=[pl.BlockSpec((bq, width), part_map(r, per_part)) for r in range(mp)]
            + [pl.BlockSpec((1, heads, bq), lambda i, sc: (i, 0, 0))],
            scratch_shapes=[
                pltpu.VMEM((heads, bq), F32),
                pltpu.VMEM((heads, bq), F32),
                pltpu.VMEM((width, bq), F32),
            ],
        ),
        out_shape=[jax.ShapeDtypeStruct((tokens // mp, width), BF16)] * mp
        + [jax.ShapeDtypeStruct((nblk, heads, bq), F32)],
        compiler_params=params(),
        cost_estimate=cost(4 * tokens * 512 * width, 8 * tokens * width, tokens * 512 * heads),
    )(sc, *q_parts, keys, values, lo, hi)
    return outs[:mp], outs[mp]


def attend_back_kernel(nblk, per_part, n_q, n_part, heads, bq, bk, sc, *refs):
    q_refs, refs = refs[:n_q], refs[n_q:]
    do_refs, refs = refs[:n_part], refs[n_part:]
    o_refs, refs = refs[:n_part], refs[n_part:]
    k_ref, v_ref, lo_ref, hi_ref, lse_ref = refs[:5]
    dq_refs, refs = refs[5 : 5 + n_q], refs[5 + n_q :]
    dk_ref, dv_ref, dk_acc, dv_acc, dq_acc, delta_ref = refs
    i = pl.program_id(0)

    @pl.when(i == 0)
    def _():
        dk_acc[...] = jnp.zeros_like(dk_acc)
        dv_acc[...] = jnp.zeros_like(dv_acc)

    q = pick(i, per_part, q_refs)
    do = pick(i, per_part, do_refs)
    o = pick(i, per_part, o_refs)
    lo = lo_ref[...]
    hi = hi_ref[...]
    prod = (do.astype(F32) * o.astype(F32)).T
    for h in range(heads):
        delta_ref[h : h + 1, :] = jnp.sum(prod[h * DH : (h + 1) * DH, :], axis=0, keepdims=True)
    dq_acc[...] = jnp.zeros_like(dq_acc)
    place = lax.broadcasted_iota(jnp.int32, (bk, bq), 0)

    def step(kb, carry):
        start = pl.multiple_of(kb * bk, bk)
        k = k_ref[pl.ds(start, bk), :]
        v = v_ref[pl.ds(start, bk), :]
        keep = jnp.logical_and(place >= lo - start, place < hi - start)
        dks, dvs = [], []
        for h in range(heads):
            cols = slice(h * DH, (h + 1) * DH)
            s = mm(k[:, cols], q[:, cols], NT) * SCALE2 - lse_ref[0, h : h + 1, :]
            p = jnp.where(keep, jnp.exp2(s), 0.0)
            dp = mm(v[:, cols], do[:, cols], NT)
            ds = (p * (dp - delta_ref[h : h + 1, :])).astype(BF16)
            dvs.append(mm(p.astype(BF16), do[:, cols]))
            dks.append(mm(ds, q[:, cols]))
            dq_acc[cols, :] += mm(k[:, cols], ds, TN)
        rows = pl.ds(start, bk)
        dk_acc[rows, :] += jnp.concatenate(dks, axis=1)
        dv_acc[rows, :] += jnp.concatenate(dvs, axis=1)
        return carry

    lax.fori_loop(sc[i], sc[nblk + i], step, 0)
    dq = (dq_acc[...] * SCALE).T.astype(BF16)
    if n_q == 1:
        dq_refs[0][...] = dq
    else:
        for r in range(n_q):

            @pl.when(jnp.logical_and(i >= r * per_part, i < (r + 1) * per_part))
            def _():
                dq_refs[r][...] = dq

    @pl.when(i == nblk - 1)
    def _():
        dk_ref[...] = (dk_acc[...] * SCALE).astype(BF16)
        dv_ref[...] = dv_acc[...].astype(BF16)


def attend_back(sc, q_parts, do_parts, o_parts, keys, values, lo, hi, lse, mp, bq, bk):
    tokens, width = sum(q.shape[0] for q in q_parts), keys.shape[1]
    heads = width // DH
    nblk, per_part = tokens // bq, tokens // bq // mp
    parts = [pl.BlockSpec((bq, width), part_map(r, per_part)) for r in range(mp)]
    if len(q_parts) == 1 and mp > 1:
        q_specs = [pl.BlockSpec((bq, width), lambda i, sc: (sc[2 * nblk + i], 0))]
    else:
        q_specs = parts
    full = pl.BlockSpec(keys.shape, lambda i, sc: (0, 0))
    row = pl.BlockSpec((1, bq), lambda i, sc: (0, i))
    outs = pl.pallas_call(
        functools.partial(attend_back_kernel, nblk, per_part, len(q_parts), mp, heads, bq, bk),
        grid_spec=pltpu.PrefetchScalarGridSpec(
            num_scalar_prefetch=1,
            grid=(nblk,),
            in_specs=q_specs
            + parts
            + parts
            + [full, full, row, row, pl.BlockSpec((1, heads, bq), lambda i, sc: (i, 0, 0))],
            out_specs=q_specs + [full, full],
            scratch_shapes=[
                pltpu.VMEM(keys.shape, F32),
                pltpu.VMEM(keys.shape, F32),
                pltpu.VMEM((width, bq), F32),
                pltpu.VMEM((heads, bq), F32),
            ],
        ),
        out_shape=[jax.ShapeDtypeStruct(q.shape, BF16) for q in q_parts]
        + [jax.ShapeDtypeStruct(keys.shape, BF16)] * 2,
        compiler_params=params(),
        cost_estimate=cost(10 * tokens * 512 * width, 12 * tokens * width, tokens * 512 * heads),
    )(sc, *q_parts, *do_parts, *o_parts, keys, values, lo, hi, lse)
    return outs[: len(q_parts)], outs[-2], outs[-1]


def norm_stats(a):
    centre = a - jnp.mean(a, axis=-1, keepdims=True)
    rstd = lax.rsqrt(jnp.mean(centre * centre, axis=-1, keepdims=True) + 1e-05)
    return centre * rstd, rstd


def norm_back(dy, xhat, rstd, gain):
    t = dy * gain
    mean_t = jnp.mean(t, axis=-1, keepdims=True)
    mean_tx = jnp.mean(t * xhat, axis=-1, keepdims=True)
    return rstd * (t - mean_t - xhat * mean_tx)


def post_self_kernel(mp, sc, *refs):
    x_ref = refs[0]
    ctx, wo, cq = refs[1 : 1 + mp], refs[1 + mp : 1 + 2 * mp], refs[1 + 2 * mp : 1 + 3 * mp]
    gain_ref, shift_ref = refs[1 + 3 * mp : 3 + 3 * mp]
    n1_ref, xhat_ref, rstd_ref = refs[3 + 3 * mp : 6 + 3 * mp]
    qc = refs[6 + 3 * mp :]
    a1 = x_ref[...].astype(F32)
    for r in range(mp):
        a1 += mm(ctx[r][...], wo[r][...])
    xhat, rstd = norm_stats(a1)
    n1 = (xhat * gain_ref[0:1, :] + shift_ref[0:1, :]).astype(BF16)
    n1_ref[...] = n1
    xhat_ref[...] = xhat
    rstd_ref[...] = rstd
    for r in range(mp):
        qc[r][...] = mm(n1, cq[r][...]).astype(BF16)


def whole(a):
    return pl.BlockSpec(a.shape, lambda i, sc: (0,) * a.ndim)


def rows_of(bt, width):
    return pl.BlockSpec((bt, width), lambda i, sc: (i, 0))


def post_self(sc, x, ctx, wo, cq, gain, shift, share, bt):
    mp, d = len(ctx), x.shape[1]
    width = ctx[0].shape[1]
    nb = share // bt
    outs = pl.pallas_call(
        functools.partial(post_self_kernel, mp),
        grid_spec=pltpu.PrefetchScalarGridSpec(
            num_scalar_prefetch=1,
            grid=(nb,),
            in_specs=[pl.BlockSpec((bt, d), lambda i, sc: (sc[0] * nb + i, 0))]
            + [rows_of(bt, width)] * mp
            + [whole(w) for w in (*wo, *cq, gain, shift)],
            out_specs=[rows_of(bt, d), rows_of(bt, d), rows_of(bt, 1)] + [rows_of(bt, width)] * mp,
        ),
        out_shape=[
            jax.ShapeDtypeStruct((share, d), BF16),
            jax.ShapeDtypeStruct((share, d), F32),
            jax.ShapeDtypeStruct((share, 1), F32),
        ]
        + [jax.ShapeDtypeStruct((share, width), BF16)] * mp,
        compiler_params=params(),
        cost_estimate=cost(4 * share * d * d, share * d * 12),
    )(sc, x, *ctx, *wo, *cq, gain, shift)
    return outs[0], outs[1], outs[2], outs[3:]


def middle_kernel(mp, *refs):
    refs = list(refs)

    def take(n):
        got = refs[:n]
        del refs[:n]
        return got

    cctx, (n1_ref, cot_ref) = take(mp), take(2)
    co, up, down = take(mp), take(mp), take(mp)
    gain_ref, shift_ref = take(2)
    out_ref, da2_ref, n2_ref, e3_ref, e2_ref = take(5)
    dcctx, hid, dpre = take(mp), take(mp), take(mp)
    (small_ref,) = take(1)
    (slope_ref,) = take(1)
    ff = up[0].shape[0]
    i = pl.program_id(0)

    a2 = n1_ref[...].astype(F32)
    for r in range(mp):
        a2 += mm(cctx[r][...], co[r][...])
    xhat2, rstd2 = norm_stats(a2)
    n2 = (xhat2 * gain_ref[1:2, :] + shift_ref[1:2, :]).astype(BF16)
    n2_ref[...] = n2
    a3 = n2.astype(F32)
    for r in range(mp):
        u = mm(n2, up[r][...], NT)
        sg = 1.0 / (1.0 + jnp.exp(-u))
        h = u * sg
        hid[r][...] = h.astype(BF16)
        slope_ref[:, r * ff : (r + 1) * ff] = sg + h * (1.0 - sg)
        a3 += mm(hid[r][...], down[r][...])
    xhat3, rstd3 = norm_stats(a3)
    out_ref[...] = (xhat3 * gain_ref[2:3, :] + shift_ref[2:3, :]).astype(BF16)
    g = cot_ref[...].astype(F32)
    da3 = norm_back(g, xhat3, rstd3, gain_ref[2:3, :])
    e3 = da3.astype(BF16)
    e3_ref[...] = e3
    dn2 = da3
    for r in range(mp):
        dh = mm(e3, down[r][...], NT)
        dpre[r][...] = (dh * slope_ref[:, r * ff : (r + 1) * ff]).astype(BF16)
        dn2 += mm(dpre[r][...], up[r][...])
    da2 = norm_back(dn2, xhat2, rstd2, gain_ref[1:2, :])
    da2_ref[...] = da2
    e2 = da2.astype(BF16)
    e2_ref[...] = e2
    for r in range(mp):
        dcctx[r][...] = mm(e2, co[r][...], NT).astype(BF16)
    sums = jnp.concatenate(
        [
            jnp.sum(dn2 * xhat2, axis=0, keepdims=True),
            jnp.sum(g * xhat3, axis=0, keepdims=True),
            jnp.sum(dn2, axis=0, keepdims=True),
            jnp.sum(g, axis=0, keepdims=True),
        ],
        axis=0,
    )

    @pl.when(i == 0)
    def _():
        small_ref[...] = sums

    @pl.when(i > 0)
    def _():
        small_ref[...] += sums


def middle(cctx, n1, cot, co, up, down, gain, shift, bt):
    mp = len(cctx)
    share, d = n1.shape
    width = cctx[0].shape[1]
    ff = up[0].shape[0]
    row = lambda w: pl.BlockSpec((bt, w), lambda i: (i, 0))
    all_of = lambda a: pl.BlockSpec(a.shape, lambda i: (0,) * a.ndim)
    shape = lambda w, t: jax.ShapeDtypeStruct((share, w), t)
    outs = pl.pallas_call(
        functools.partial(middle_kernel, mp),
        grid=(share // bt,),
        in_specs=[row(width)] * mp + [row(d)] * 2 + [all_of(w) for w in (*co, *up, *down, gain, shift)],
        out_specs=[row(d)] * 5
        + [row(width)] * mp
        + [row(ff)] * (2 * mp)
        + [pl.BlockSpec((4, d), lambda i: (0, 0))],
        scratch_shapes=[pltpu.VMEM((bt, ff * mp), F32)],
        out_shape=[shape(d, BF16), shape(d, F32), shape(d, BF16), shape(d, BF16), shape(d, BF16)]
        + [shape(width, BF16)] * mp
        + [shape(ff, BF16)] * (2 * mp)
        + [jax.ShapeDtypeStruct((4, d), F32)],
        compiler_params=params(),
        cost_estimate=cost(8 * share * d * ff * mp + 4 * share * d * d, share * ff * mp * 4, share * ff * mp),
    )(*cctx, n1, cot, *co, *up, *down, gain, shift)
    out, da2, n2, e3, e2 = outs[:5]
    return out, da2, n2, e3, e2, outs[5 : 5 + mp], outs[5 + mp : 5 + 2 * mp], outs[5 + 2 * mp : 5 + 3 * mp], outs[-1]


def pre_self_kernel(mp, *refs):
    dqc, cq, wo = refs[:mp], refs[mp : 2 * mp], refs[2 * mp : 3 * mp]
    da2_ref, xhat_ref, rstd_ref, gain_ref = refs[3 * mp : 3 * mp + 4]
    da1_ref, e1_ref = refs[3 * mp + 4 : 3 * mp + 6]
    dctx = refs[3 * mp + 6 : 4 * mp + 6]
    small_ref = refs[4 * mp + 6]
    i = pl.program_id(0)
    dn1 = da2_ref[...]
    for r in range(mp):
        dn1 += mm(dqc[r][...], cq[r][...], NT)
    xhat = xhat_ref[...]
    da1 = norm_back(dn1, xhat, rstd_ref[...], gain_ref[0:1, :])
    da1_ref[...] = da1
    e1 = da1.astype(BF16)
    e1_ref[...] = e1
    for r in range(mp):
        dctx[r][...] = mm(e1, wo[r][...], NT).astype(BF16)
    sums = jnp.concatenate(
        [jnp.sum(dn1 * xhat, axis=0, keepdims=True), jnp.sum(dn1, axis=0, keepdims=True)], axis=0
    )

    @pl.when(i == 0)
    def _():
        small_ref[...] = sums

    @pl.when(i > 0)
    def _():
        small_ref[...] += sums


def pre_self(dqc, cq, wo, da2, xhat, rstd, gain, bt):
    mp = len(dqc)
    share, d = da2.shape
    width = dqc[0].shape[1]
    row = lambda w: pl.BlockSpec((bt, w), lambda i: (i, 0))
    all_of = lambda a: pl.BlockSpec(a.shape, lambda i: (0,) * a.ndim)
    outs = pl.pallas_call(
        functools.partial(pre_self_kernel, mp),
        grid=(share // bt,),
        in_specs=[row(width)] * mp
        + [all_of(w) for w in (*cq, *wo)]
        + [row(d), row(d), row(1), all_of(gain)],
        out_specs=[row(d), row(d)] + [row(width)] * mp + [pl.BlockSpec((2, d), lambda i: (0, 0))],
        out_shape=[jax.ShapeDtypeStruct((share, d), F32), jax.ShapeDtypeStruct((share, d), BF16)]
        + [jax.ShapeDtypeStruct((share, width), BF16)] * mp
        + [jax.ShapeDtypeStruct((2, d), F32)],
        compiler_params=params(),
        cost_estimate=cost(4 * share * d * d, share * d * 14),
    )(*dqc, *cq, *wo, da2, xhat, rstd, gain)
    return outs[0], outs[1], outs[2 : 2 + mp], outs[-1]


def part_kernel(n_in, n_out, per_part, sc, *refs):
    grads, w_ref, outs = refs[:n_in], refs[n_in], refs[n_in + 1 :]
    i = pl.program_id(0)
    total = mm(grads[0][...], w_ref[0], NT)
    for c in range(1, n_in):
        total += mm(grads[c][...], w_ref[c], NT)
    for r in range(n_out):

        @pl.when(jnp.logical_and(i >= r * per_part, i < (r + 1) * per_part))
        def _():
            outs[r][...] = total.astype(outs[r].dtype)


def input_part(sc, grads, w, mp, bt):
    tokens, width = grads[0].shape
    d = w.shape[1]
    nblk = tokens // bt
    per_part = nblk // mp
    outs = pl.pallas_call(
        functools.partial(part_kernel, len(grads), mp, per_part),
        grid_spec=pltpu.PrefetchScalarGridSpec(
            num_scalar_prefetch=1,
            grid=(nblk,),
            in_specs=[pl.BlockSpec((bt, width), lambda i, sc: (sc[i], 0))] * len(grads) + [whole(w)],
            out_specs=[pl.BlockSpec((bt, d), part_map(r, per_part)) for r in range(mp)],
        ),
        out_shape=[jax.ShapeDtypeStruct((tokens // mp, d), F32)]
        + [jax.ShapeDtypeStruct((tokens // mp, d), BF16)] * (mp - 1),
        compiler_params=params(),
        cost_estimate=cost(2 * tokens * d * width * len(grads), tokens * d * 6),
    )(sc, *grads, w)
    return outs


MESH = pl.DeviceIdType.MESH


def all_sum_kernel(plan, nbits, n, *refs):
    ins, outs = refs[: n + 1], refs[n + 1 : 2 * n + 2]
    got = refs[2 * n + 2 : 2 * n + 3 + len(plan)]
    send_sem, recv_sem = refs[2 * n + 3 + len(plan) :]
    me, core = lax.axis_index("batch"), lax.axis_index("mp")
    bit = [(me // (1 << b)) % 2 for b in range(nbits)]
    partner = [(me + (1 << b) * (1 - 2 * bit[b]), core) for b in range(nbits)]
    barrier = pltpu.get_barrier_semaphore()
    for b in range(nbits):
        pl.semaphore_signal(barrier, inc=1, device_id=partner[b], device_id_type=MESH)
    pl.semaphore_wait(barrier, nbits)

    def send(c, s, b, src, dst):
        copy = pltpu.make_async_remote_copy(
            src_ref=src,
            dst_ref=dst,
            send_sem=send_sem.at[c, s],
            recv_sem=recv_sem.at[c, s],
            device_id=partner[b],
            device_id_type=MESH,
        )
        copy.start()
        copies[c].append(copy)

    def rows(off, count):
        return pl.ds(pl.multiple_of(off, 16), count)

    copies = [[] for _ in range(len(plan) + 1)]
    spans = [[(first, count)] for _, first, count, _ in plan]
    slots = [[] for _ in plan]

    def held(c, s, b):
        a, first, count, _ = plan[c]
        half = count >> (s + 1)
        base = first if s == 0 else slots[c][s - 1]
        ref = ins[a] if s == 0 else got[c]
        return ref, base + (1 - bit[b]) * half, base + bit[b] * half, half

    def begin(c, s):
        a, first, count, order = plan[c]
        if s < nbits:
            b = order[s]
            ref, gives, _, half = held(c, s, b)
            slots[c].append(count - (count >> s))
            off = spans[c][s][0]
            spans[c].append((off + bit[b] * half, half))
            send(c, s, b, ref.at[rows(gives, half), :], got[c].at[pl.ds(slots[c][s], half), :])
        else:
            j = 2 * nbits - 1 - s
            block = outs[a].at[rows(*spans[c][j + 1]), :]
            send(c, s, order[j], block, block)

    def finish(c, s):
        copies[c][s].wait_recv()
        if s < nbits:
            a, _, _, order = plan[c]
            ref, _, stays, half = held(c, s, order[s])
            came = pl.ds(slots[c][s], half)
            total = ref[rows(stays, half), :].astype(F32) + got[c][came, :].astype(F32)
            if s < nbits - 1:
                got[c][came, :] = total.astype(BF16)
            else:
                outs[a][rows(*spans[c][s + 1]), :] = total.astype(BF16)

    last = len(plan)
    size = ins[n].shape[0]
    outs[n][...] = ins[n][...]
    for s in range(2 * nbits + 1):
        if 1 <= s <= nbits:
            copies[last][s - 1].wait()
            outs[n][...] = (
                outs[n][...].astype(F32) + got[last][(s - 1) * size : s * size, :].astype(F32)
            ).astype(BF16)
        if s < nbits:
            send(last, s, s, outs[n], got[last].at[pl.ds(s * size, size), :])
        for c in range(len(plan)):
            if s >= 1:
                finish(c, s - 1)
            if s < 2 * nbits:
                begin(c, s)
    for c in range(len(plan)):
        for copy in copies[c]:
            copy.wait_send()


def all_sum(arrays, splits, small, devices):
    nbits = devices.bit_length() - 1
    if devices != 1 << nbits or nbits < 3:
        return [lax.psum(a, "batch") for a in (*arrays, small)]
    x_y, y_x = tuple(range(nbits)), (1, 0, *range(2, nbits))
    far = (*range(2, nbits), 0, 1)
    flat = [a.reshape(-1, a.shape[-1]) for a in arrays]
    plan, used = [], []
    for a, parts in zip(flat, splits):
        count = a.shape[0] // parts
        if a.shape[0] % parts == 0 and count % (16 * devices) == 0:
            for p in range(parts):
                order = far if parts == 3 else (x_y, y_x)[len(plan) % 2]
                plan.append((len(used), p * count, count, order))
            used.append(a)
        else:
            used.append(None)
    keep = [i for i, a in enumerate(used) if a is not None]
    plan = [(keep.index(i), *rest) for i, *rest in plan]
    small = jnp.pad(small, ((0, 16 - small.shape[0]), (0, 0)))
    operands = [used[i] for i in keep] + [small]
    vmem = pl.BlockSpec(memory_space=pltpu.VMEM)
    sums = pl.pallas_call(
        functools.partial(all_sum_kernel, plan, nbits, len(keep)),
        in_specs=[vmem] * len(operands),
        out_specs=[vmem] * len(operands),
        out_shape=[jax.ShapeDtypeStruct(a.shape, a.dtype) for a in operands],
        scratch_shapes=[pltpu.VMEM((rows, operands[i].shape[1]), BF16) for i, _, rows, _ in plan]
        + [pltpu.VMEM((16 * nbits, small.shape[1]), BF16)]
        + [pltpu.SemaphoreType.DMA((len(plan) + 1, 2 * nbits))] * 2,
        compiler_params=pltpu.CompilerParams(
            collective_id=7, has_side_effects=True, vmem_limit_bytes=VMEM_BYTES
        ),
    )(*operands)
    outs = [
        sums[keep.index(i)].reshape(a.shape) if i in keep else lax.psum(a, "batch")
        for i, a in enumerate(arrays)
    ]
    return outs + [sums[-1]]


def shards(
    block_input_slots,
    memory,
    target_sentence_lengths,
    source_lengths,
    self_qkv,
    self_out,
    cross_query,
    cross_kv,
    cross_out,
    up_proj,
    down_proj,
    norm_gains,
    norm_biases,
    cotangent,
    mp,
    devices,
):
    tokens, d = block_input_slots.shape
    mem_tokens = memory.shape[0]
    share = cotangent.shape[0]
    mem_share = mem_tokens // mp
    width = self_qkv.shape[2]
    me = lax.axis_index("mp")
    bt = min(256, share)
    bq = min(256, share)
    bk = min(256, mem_tokens)

    def spread(own):
        return [own] + [
            lax.ppermute(own, "mp", [(i, (i + r) % mp) for i in range(mp)]) for r in range(1, mp)
        ]

    def exchange(pieces):
        got = [pieces[0]] + [None] * (mp - 1)
        for r in range(1, mp):
            got[mp - r] = lax.ppermute(pieces[r], "mp", [(i, (i - r) % mp) for i in range(mp)])
        return got

    wo, cq, co = spread(self_out), spread(cross_query), spread(cross_out)
    up, down = spread(up_proj), spread(down_proj)
    gain, shift = norm_gains.T, norm_biases.T

    t_len = target_sentence_lengths.reshape(-1)
    s_len = source_lengths.reshape(-1)
    t_end, s_end = jnp.cumsum(t_len), jnp.cumsum(s_len)
    t_start, s_start = t_end - t_len, s_end - s_len
    first = ((me - jnp.arange(mp)) % mp) * share
    place = (first[:, None] + jnp.arange(share)[None, :]).reshape(-1).astype(jnp.int32)
    begun = place[:, None] >= t_start[None, :]
    self_lo = jnp.max(jnp.where(begun, t_start[None, :], 0), axis=1)
    self_hi = place + 1
    cross_lo = jnp.max(jnp.where(begun, s_start[None, :], 0), axis=1)
    cross_hi = jnp.max(jnp.where(begun, s_end[None, :], 0), axis=1)
    nblk = tokens // bq
    q_block = place.reshape(nblk, bq)[:, 0] // bq

    def table(lo, hi):
        return jnp.concatenate(
            [lo.reshape(nblk, bq)[:, 0] // bk, (hi.reshape(nblk, bq)[:, -1] + bk - 1) // bk, q_block]
        ).astype(jnp.int32)

    self_table, cross_table = table(self_lo, self_hi), table(cross_lo, cross_hi)
    as_row = lambda v: v.reshape(1, tokens).astype(jnp.int32)
    self_lo, self_hi, cross_lo, cross_hi = map(as_row, (self_lo, self_hi, cross_lo, cross_hi))

    proj = [
        jnp.dot(block_input_slots, self_qkv[c], preferred_element_type=F32).astype(BF16) for c in range(3)
    ]
    pair = [jnp.dot(memory, cross_kv[c], preferred_element_type=F32).astype(BF16) for c in range(2)]
    ctx_parts, self_lse = attend(
        self_table, proj[:1], proj[1], proj[2], self_lo, self_hi, mp, bq, bk
    )
    ctx = exchange(ctx_parts)
    me_row = me.reshape(1).astype(jnp.int32)
    n1, xhat1, rstd1, qc = post_self(me_row, block_input_slots, ctx, wo, cq, gain, shift, share, bt)
    qc_parts = exchange(qc)
    cctx_parts, cross_lse = attend(
        cross_table, qc_parts, pair[0], pair[1], cross_lo, cross_hi, mp, bq, bk
    )
    cctx = exchange(cctx_parts)
    layer_output, da2, n2, e3, e2, dcctx, hid, dpre, small23 = middle(
        cctx, n1, cotangent, co, up, down, gain, shift, bt
    )
    dcctx_parts = exchange(dcctx)

    def grads(lefts, rights):
        return [mm(a, b, TN).astype(BF16) for a, b in zip(lefts, rights)]

    def collect(pieces):
        got = exchange(pieces)
        total = got[0].astype(F32)
        for g in got[1:]:
            total += g.astype(F32)
        return total

    down_grad = collect(grads(hid, [e3] * mp))
    up_grad = collect(grads(dpre, [n2] * mp))
    cross_out_grad = collect(grads(cctx, [e2] * mp))
    dqc_parts, dkc, dvc = attend_back(
        cross_table, qc_parts, dcctx_parts, cctx_parts, pair[0], pair[1], cross_lo, cross_hi, cross_lse, mp, bq, bk
    )
    dqc = exchange(dqc_parts)
    da1, e1, dctx, small1 = pre_self(dqc, cq, wo, da2, xhat1, rstd1, gain, bt)
    dctx_parts = exchange(dctx)
    mem_bt = min(256, mem_share)
    mem_nb = mem_share // mem_bt
    mem_blocks = ((((me - jnp.arange(mp)) % mp) * mem_nb)[:, None] + jnp.arange(mem_nb)[None, :]).reshape(-1)
    memory_parts = input_part(mem_blocks.astype(jnp.int32), [dkc, dvc], cross_kv, mp, mem_bt)
    memory_grad = collect(memory_parts)
    cross_kv_grad = jnp.stack([mm(memory, g, TN) for g in (dkc, dvc)])
    cross_query_grad = collect(grads([n1] * mp, dqc))
    self_out_grad = collect(grads(ctx, [e1] * mp))
    (dq,), dk, dv = attend_back(
        self_table, proj[:1], dctx_parts, ctx_parts, proj[1], proj[2], self_lo, self_hi, self_lse, mp, bq, bk
    )
    input_parts = input_part(q_block.astype(jnp.int32), [dq, dk, dv], self_qkv, mp, bq)
    input_grad = collect(input_parts) + da1
    self_qkv_grad = jnp.stack([mm(block_input_slots, g, TN) for g in (dq, dk, dv)])

    small = jnp.concatenate([small1[:1], small23[:2], small1[1:], small23[2:]], axis=0)
    part = d // mp
    pieces = [
        lax.dynamic_slice_in_dim(small, ((me - r) % mp) * part, part, 1).astype(BF16) for r in range(mp)
    ]
    small = collect(pieces)
    *summed, small = all_sum(
        [
            g.astype(BF16)
            for g in (
                self_qkv_grad,
                self_out_grad,
                cross_query_grad,
                cross_kv_grad,
                cross_out_grad,
                up_grad,
                down_grad,
            )
        ],
        (3, 1, 1, 2, 1, 2, 2),
        small.astype(BF16),
        devices,
    )
    summed = [g.astype(F32) for g in summed]
    small = small.astype(F32).T
    return (layer_output, input_grad, memory_grad, *summed, small[:, :3], small[:, 3:6])


def solution(mesh):
    mp = mesh.shape["mp"]
    rows = P("batch", None)
    both = P(("batch", "mp"), None)
    first, last, last3 = P("mp", None), P(None, "mp"), P(None, None, "mp")
    return jax.shard_map(
        functools.partial(shards, mp=mp, devices=mesh.shape["batch"]),
        mesh=mesh,
        in_specs=(rows, rows, rows, rows, last3, first, last, last3, first, first, first, P(), P(), both),
        out_specs=(both, both, both, last3, first, last, last3, first, first, first, first, first),
        check_vma=False,
    )
```

```python
import functools
import math

import jax
import jax.numpy as jnp
from jax import lax
from jax.experimental import pallas as pl
from jax.experimental.pallas import tpu as pltpu
from jax.sharding import PartitionSpec as P

DH = 64
NEG = -1e30
F32 = jnp.float32
BF16 = jnp.bfloat16
SCALE = DH**-0.5
SCALE2 = SCALE * math.log2(math.e)
NT = (((1,), (1,)), ((), ()))
NN = (((1,), (0,)), ((), ()))
TN = (((0,), (0,)), ((), ()))
VMEM_BYTES = 50 << 20


def mm(a, b, dims=NN):
    return lax.dot_general(a, b, dims, preferred_element_type=F32)


def params(semantics=("arbitrary",)):
    return pltpu.CompilerParams(dimension_semantics=semantics, vmem_limit_bytes=VMEM_BYTES)


def cost(flops, nbytes, exps=0):
    return pl.CostEstimate(flops=int(flops), bytes_accessed=int(nbytes), transcendentals=int(exps))


def pick(i, per_part, refs):
    value = refs[0][...]
    for r in range(1, len(refs)):
        value = jnp.where(i >= r * per_part, refs[r][...], value)
    return value


def part_map(r, per_part):
    return lambda i, sc: (jnp.clip(i - r * per_part, 0, per_part - 1), 0)


def per_head(block, heads):
    head = lax.broadcasted_iota(jnp.int32, block.shape, 1) // DH
    return jnp.concatenate([jnp.where(head == h, block, jnp.zeros_like(block)) for h in range(heads)], axis=0)


def attend_kernel(nblk, per_part, n_q, n_out, heads, bq, bk, sc, *refs):
    q_refs, refs = refs[:n_q], refs[n_q:]
    k_ref, vt_ref, lo_ref, hi_ref = refs[:4]
    out_refs, (lse_ref, acc_ref, q_heads, s_ref, p_ref) = refs[4 : 4 + n_out], refs[4 + n_out :]
    i = pl.program_id(0)
    q_heads[...] = per_head(pick(i, per_part, q_refs), heads)
    lo = lo_ref[...]
    hi = hi_ref[...]
    acc_ref[...] = jnp.zeros_like(acc_ref)
    place = lax.broadcasted_iota(jnp.int32, (bk, bq), 0)
    span = [slice(h * bq, (h + 1) * bq) for h in range(heads)]
    cols = [slice(h * DH, (h + 1) * DH) for h in range(heads)]

    first, end = sc[i], sc[nblk + i]

    def rows(kb):
        return pl.ds(pl.multiple_of(kb * bk, bk), bk)

    def scores(kb, h):
        s_ref[:, span[h]] = mm(k_ref[rows(kb), :], q_heads[span[h], :], NT)

    def soften(kb, h, keep, top, total):
        t = jnp.where(keep, s_ref[:, span[h]] * SCALE2, NEG)
        new_top = jnp.maximum(top, jnp.max(t, axis=0, keepdims=True))
        e = jnp.exp2(t - new_top)
        decay = jnp.exp2(top - new_top)
        p_ref[:, span[h]] = e.astype(BF16)
        return new_top, total * decay + jnp.sum(e, axis=0, keepdims=True), decay

    def gather(kb, h, decay):
        acc_ref[cols[h], :] = acc_ref[cols[h], :] * decay + mm(vt_ref[cols[h], rows(kb)], p_ref[:, span[h]])

    def stage(kb, carry):
        start = kb * bk
        keep = jnp.logical_and(place >= lo - start, place < hi - start)
        after = jnp.minimum(kb + 1, end - 1)
        new = []
        for h in range(heads):
            top, total, decay = carry[h]
            if decay is not None:
                gather(kb - 1, h, decay)
            new.append(soften(kb, h, keep, top, total))
            scores(after, h)
        return new

    for h in range(heads):
        scores(first, h)
    none = jnp.full((1, bq), NEG, F32), jnp.zeros((1, bq), F32), None
    carry = lax.fori_loop(first + 1, end, stage, stage(first, [none] * heads))
    for h in range(heads):
        gather(end - 1, h, carry[h][2])
    top = [carry[h][0] for h in range(heads)]
    total = [carry[h][1] for h in range(heads)]
    for h in range(heads):
        acc_ref[cols[h], :] = acc_ref[cols[h], :] / total[h]
        lse_ref[0, h : h + 1, :] = top[h] + jnp.log2(total[h])
    ctx = acc_ref[...].T.astype(BF16)
    for r in range(n_out):

        @pl.when(jnp.logical_and(i >= r * per_part, i < (r + 1) * per_part))
        def _():
            out_refs[r][...] = ctx


def attend(sc, q_parts, keys, values_t, lo, hi, mp, bq, bk):
    tokens, width = sum(q.shape[0] for q in q_parts), keys.shape[1]
    heads = width // DH
    nblk, per_part = tokens // bq, tokens // bq // mp
    if len(q_parts) == 1 and mp > 1:
        q_specs = [pl.BlockSpec((bq, width), lambda i, sc: (sc[2 * nblk + i], 0))]
    else:
        q_specs = [pl.BlockSpec((bq, width), part_map(r, per_part)) for r in range(mp)]
    full = lambda a: pl.BlockSpec(a.shape, lambda i, sc: (0, 0))
    row = pl.BlockSpec((1, bq), lambda i, sc: (0, i))
    outs = pl.pallas_call(
        functools.partial(attend_kernel, nblk, per_part, len(q_parts), mp, heads, bq, bk),
        grid_spec=pltpu.PrefetchScalarGridSpec(
            num_scalar_prefetch=1,
            grid=(nblk,),
            in_specs=q_specs + [full(keys), full(values_t), row, row],
            out_specs=[pl.BlockSpec((bq, width), part_map(r, per_part)) for r in range(mp)]
            + [pl.BlockSpec((1, heads, bq), lambda i, sc: (i, 0, 0))],
            scratch_shapes=[
                pltpu.VMEM((width, bq), F32),
                pltpu.VMEM((heads * bq, width), BF16),
                pltpu.VMEM((bk, heads * bq), F32),
                pltpu.VMEM((bk, heads * bq), BF16),
            ],
        ),
        out_shape=[jax.ShapeDtypeStruct((tokens // mp, width), BF16)] * mp
        + [jax.ShapeDtypeStruct((nblk, heads, bq), F32)],
        compiler_params=params(),
        cost_estimate=cost(4 * tokens * 512 * width, 8 * tokens * width, tokens * 512 * heads),
    )(sc, *q_parts, keys, values_t, lo, hi)
    return outs[:mp], outs[mp]


def attend_back_kernel(nblk, per_part, n_q, n_part, heads, bq, bk, sc, *refs):
    q_refs, refs = refs[:n_q], refs[n_q:]
    do_refs, refs = refs[:n_part], refs[n_part:]
    o_refs, refs = refs[:n_part], refs[n_part:]
    k_ref, kt_ref, v_ref, lo_ref, hi_ref, lse_ref = refs[:6]
    dq_refs, refs = refs[6 : 6 + n_q], refs[6 + n_q :]
    dk_ref, dv_ref, dk_acc, dv_acc, dq_acc, q_heads, do_heads = refs
    i = pl.program_id(0)

    @pl.when(i == 0)
    def _():
        dk_acc[...] = jnp.zeros_like(dk_acc)
        dv_acc[...] = jnp.zeros_like(dv_acc)

    q_heads[...] = per_head(pick(i, per_part, q_refs), heads)
    do = pick(i, per_part, do_refs)
    do_heads[...] = per_head(do, heads)
    lo = lo_ref[...]
    hi = hi_ref[...]
    span = [slice(h * bq, (h + 1) * bq) for h in range(heads)]
    cols = [slice(h * DH, (h + 1) * DH) for h in range(heads)]
    prod = (do.astype(F32) * pick(i, per_part, o_refs).astype(F32)).T
    delta = [jnp.sum(prod[cols[h], :], axis=0, keepdims=True) for h in range(heads)]
    lse = [lse_ref[0, h : h + 1, :] for h in range(heads)]
    dq_acc[...] = jnp.zeros_like(dq_acc)
    place = lax.broadcasted_iota(jnp.int32, (bk, bq), 0)

    def step(kb, carry):
        start = pl.multiple_of(kb * bk, bk)
        rows = pl.ds(start, bk)
        kt = kt_ref[:, rows]
        keep = jnp.logical_and(place >= lo - start, place < hi - start)
        s = mm(k_ref[rows, :], q_heads[...], NT) * SCALE2
        dp = mm(v_ref[rows, :], do_heads[...], NT)
        p = [jnp.where(keep, jnp.exp2(s[:, span[h]] - lse[h]), 0.0) for h in range(heads)]
        ds = [(p[h] * (dp[:, span[h]] - delta[h])).astype(BF16) for h in range(heads)]
        p = [p[h].astype(BF16) for h in range(heads)]
        dv_acc[rows, :] += mm(jnp.concatenate(p, axis=1), do_heads[...])
        dk_acc[rows, :] += mm(jnp.concatenate(ds, axis=1), q_heads[...])
        for h in range(heads):
            dq_acc[cols[h], :] += mm(kt[cols[h], :], ds[h])
        return carry

    lax.fori_loop(sc[i], sc[nblk + i], step, 0)
    dq = (dq_acc[...] * SCALE).T.astype(BF16)
    if n_q == 1:
        dq_refs[0][...] = dq
    else:
        for r in range(n_q):

            @pl.when(jnp.logical_and(i >= r * per_part, i < (r + 1) * per_part))
            def _():
                dq_refs[r][...] = dq

    @pl.when(i == nblk - 1)
    def _():
        dk_ref[...] = (dk_acc[...] * SCALE).astype(BF16)
        dv_ref[...] = dv_acc[...].astype(BF16)


def attend_back(sc, q_parts, do_parts, o_parts, keys, keys_t, values, lo, hi, lse, mp, bq, bk):
    tokens, width = sum(q.shape[0] for q in q_parts), keys.shape[1]
    heads = width // DH
    nblk, per_part = tokens // bq, tokens // bq // mp
    parts = [pl.BlockSpec((bq, width), part_map(r, per_part)) for r in range(mp)]
    if len(q_parts) == 1 and mp > 1:
        q_specs = [pl.BlockSpec((bq, width), lambda i, sc: (sc[2 * nblk + i], 0))]
    else:
        q_specs = parts
    full = lambda a: pl.BlockSpec(a.shape, lambda i, sc: (0, 0))
    row = pl.BlockSpec((1, bq), lambda i, sc: (0, i))
    outs = pl.pallas_call(
        functools.partial(attend_back_kernel, nblk, per_part, len(q_parts), mp, heads, bq, bk),
        grid_spec=pltpu.PrefetchScalarGridSpec(
            num_scalar_prefetch=1,
            grid=(nblk,),
            in_specs=q_specs
            + parts
            + parts
            + [full(keys), full(keys_t), full(values), row, row]
            + [pl.BlockSpec((1, heads, bq), lambda i, sc: (i, 0, 0))],
            out_specs=q_specs + [full(keys), full(keys)],
            scratch_shapes=[
                pltpu.VMEM(keys.shape, F32),
                pltpu.VMEM(keys.shape, F32),
                pltpu.VMEM((width, bq), F32),
                pltpu.VMEM((heads * bq, width), BF16),
                pltpu.VMEM((heads * bq, width), BF16),
            ],
        ),
        out_shape=[jax.ShapeDtypeStruct(q.shape, BF16) for q in q_parts]
        + [jax.ShapeDtypeStruct(keys.shape, BF16)] * 2,
        compiler_params=params(),
        cost_estimate=cost(10 * tokens * 512 * width, 12 * tokens * width, tokens * 512 * heads),
    )(sc, *q_parts, *do_parts, *o_parts, keys, keys_t, values, lo, hi, lse)
    return outs[: len(q_parts)], outs[-2], outs[-1]


def norm_stats(a):
    centre = a - jnp.mean(a, axis=-1, keepdims=True)
    rstd = lax.rsqrt(jnp.mean(centre * centre, axis=-1, keepdims=True) + 1e-05)
    return centre * rstd, rstd


def norm_back(dy, xhat, rstd, gain):
    t = dy * gain
    mean_t = jnp.mean(t, axis=-1, keepdims=True)
    mean_tx = jnp.mean(t * xhat, axis=-1, keepdims=True)
    return rstd * (t - mean_t - xhat * mean_tx)


def post_self_kernel(mp, sc, *refs):
    x_ref = refs[0]
    ctx, wo, cq = refs[1 : 1 + mp], refs[1 + mp : 1 + 2 * mp], refs[1 + 2 * mp : 1 + 3 * mp]
    gain_ref, shift_ref = refs[1 + 3 * mp : 3 + 3 * mp]
    n1_ref, xhat_ref, rstd_ref = refs[3 + 3 * mp : 6 + 3 * mp]
    qc = refs[6 + 3 * mp :]
    a1 = x_ref[...].astype(F32)
    for r in range(mp):
        a1 += mm(ctx[r][...], wo[r][...])
    xhat, rstd = norm_stats(a1)
    n1 = (xhat * gain_ref[0:1, :] + shift_ref[0:1, :]).astype(BF16)
    n1_ref[...] = n1
    xhat_ref[...] = xhat
    rstd_ref[...] = rstd
    for r in range(mp):
        qc[r][...] = mm(n1, cq[r][...]).astype(BF16)


def whole(a):
    return pl.BlockSpec(a.shape, lambda i, sc: (0,) * a.ndim)


def rows_of(bt, width):
    return pl.BlockSpec((bt, width), lambda i, sc: (i, 0))


def post_self(sc, x, ctx, wo, cq, gain, shift, share, bt):
    mp, d = len(ctx), x.shape[1]
    width = ctx[0].shape[1]
    nb = share // bt
    outs = pl.pallas_call(
        functools.partial(post_self_kernel, mp),
        grid_spec=pltpu.PrefetchScalarGridSpec(
            num_scalar_prefetch=1,
            grid=(nb,),
            in_specs=[pl.BlockSpec((bt, d), lambda i, sc: (sc[0] * nb + i, 0))]
            + [rows_of(bt, width)] * mp
            + [whole(w) for w in (*wo, *cq, gain, shift)],
            out_specs=[rows_of(bt, d), rows_of(bt, d), rows_of(bt, 1)] + [rows_of(bt, width)] * mp,
        ),
        out_shape=[
            jax.ShapeDtypeStruct((share, d), BF16),
            jax.ShapeDtypeStruct((share, d), F32),
            jax.ShapeDtypeStruct((share, 1), F32),
        ]
        + [jax.ShapeDtypeStruct((share, width), BF16)] * mp,
        compiler_params=params(),
        cost_estimate=cost(4 * share * d * d, share * d * 12),
    )(sc, x, *ctx, *wo, *cq, gain, shift)
    return outs[0], outs[1], outs[2], outs[3:]


def middle_kernel(mp, *refs):
    refs = list(refs)

    def take(n):
        got = refs[:n]
        del refs[:n]
        return got

    cctx, (n1_ref, cot_ref) = take(mp), take(2)
    co, up, down = take(mp), take(mp), take(mp)
    gain_ref, shift_ref = take(2)
    out_ref, da2_ref, n2_ref, e3_ref, e2_ref = take(5)
    dcctx, hid, dpre = take(mp), take(mp), take(mp)
    (small_ref,) = take(1)
    (slope_ref,) = take(1)
    ff = up[0].shape[0]
    i = pl.program_id(0)

    a2 = n1_ref[...].astype(F32)
    for r in range(mp):
        a2 += mm(cctx[r][...], co[r][...])
    xhat2, rstd2 = norm_stats(a2)
    n2 = (xhat2 * gain_ref[1:2, :] + shift_ref[1:2, :]).astype(BF16)
    n2_ref[...] = n2
    a3 = n2.astype(F32)
    for r in range(mp):
        u = mm(n2, up[r][...], NT)
        sg = 1.0 / (1.0 + jnp.exp(-u))
        h = u * sg
        hid[r][...] = h.astype(BF16)
        slope_ref[:, r * ff : (r + 1) * ff] = sg + h * (1.0 - sg)
        a3 += mm(hid[r][...], down[r][...])
    xhat3, rstd3 = norm_stats(a3)
    out_ref[...] = (xhat3 * gain_ref[2:3, :] + shift_ref[2:3, :]).astype(BF16)
    g = cot_ref[...].astype(F32)
    da3 = norm_back(g, xhat3, rstd3, gain_ref[2:3, :])
    e3 = da3.astype(BF16)
    e3_ref[...] = e3
    dn2 = da3
    for r in range(mp):
        dh = mm(e3, down[r][...], NT)
        dpre[r][...] = (dh * slope_ref[:, r * ff : (r + 1) * ff]).astype(BF16)
        dn2 += mm(dpre[r][...], up[r][...])
    da2 = norm_back(dn2, xhat2, rstd2, gain_ref[1:2, :])
    da2_ref[...] = da2
    e2 = da2.astype(BF16)
    e2_ref[...] = e2
    for r in range(mp):
        dcctx[r][...] = mm(e2, co[r][...], NT).astype(BF16)
    sums = jnp.concatenate(
        [
            jnp.sum(dn2 * xhat2, axis=0, keepdims=True),
            jnp.sum(g * xhat3, axis=0, keepdims=True),
            jnp.sum(dn2, axis=0, keepdims=True),
            jnp.sum(g, axis=0, keepdims=True),
        ],
        axis=0,
    )

    @pl.when(i == 0)
    def _():
        small_ref[...] = sums

    @pl.when(i > 0)
    def _():
        small_ref[...] += sums


def middle(cctx, n1, cot, co, up, down, gain, shift, bt):
    mp = len(cctx)
    share, d = n1.shape
    width = cctx[0].shape[1]
    ff = up[0].shape[0]
    row = lambda w: pl.BlockSpec((bt, w), lambda i: (i, 0))
    all_of = lambda a: pl.BlockSpec(a.shape, lambda i: (0,) * a.ndim)
    shape = lambda w, t: jax.ShapeDtypeStruct((share, w), t)
    outs = pl.pallas_call(
        functools.partial(middle_kernel, mp),
        grid=(share // bt,),
        in_specs=[row(width)] * mp + [row(d)] * 2 + [all_of(w) for w in (*co, *up, *down, gain, shift)],
        out_specs=[row(d)] * 5
        + [row(width)] * mp
        + [row(ff)] * (2 * mp)
        + [pl.BlockSpec((4, d), lambda i: (0, 0))],
        scratch_shapes=[pltpu.VMEM((bt, ff * mp), F32)],
        out_shape=[shape(d, BF16), shape(d, F32), shape(d, BF16), shape(d, BF16), shape(d, BF16)]
        + [shape(width, BF16)] * mp
        + [shape(ff, BF16)] * (2 * mp)
        + [jax.ShapeDtypeStruct((4, d), F32)],
        compiler_params=params(),
        cost_estimate=cost(8 * share * d * ff * mp + 4 * share * d * d, share * ff * mp * 4, share * ff * mp),
    )(*cctx, n1, cot, *co, *up, *down, gain, shift)
    out, da2, n2, e3, e2 = outs[:5]
    return out, da2, n2, e3, e2, outs[5 : 5 + mp], outs[5 + mp : 5 + 2 * mp], outs[5 + 2 * mp : 5 + 3 * mp], outs[-1]


def pre_self_kernel(mp, *refs):
    dqc, cq, wo = refs[:mp], refs[mp : 2 * mp], refs[2 * mp : 3 * mp]
    da2_ref, xhat_ref, rstd_ref, gain_ref = refs[3 * mp : 3 * mp + 4]
    da1_ref, e1_ref = refs[3 * mp + 4 : 3 * mp + 6]
    dctx = refs[3 * mp + 6 : 4 * mp + 6]
    small_ref = refs[4 * mp + 6]
    i = pl.program_id(0)
    dn1 = da2_ref[...]
    for r in range(mp):
        dn1 += mm(dqc[r][...], cq[r][...], NT)
    xhat = xhat_ref[...]
    da1 = norm_back(dn1, xhat, rstd_ref[...], gain_ref[0:1, :])
    da1_ref[...] = da1
    e1 = da1.astype(BF16)
    e1_ref[...] = e1
    for r in range(mp):
        dctx[r][...] = mm(e1, wo[r][...], NT).astype(BF16)
    sums = jnp.concatenate(
        [jnp.sum(dn1 * xhat, axis=0, keepdims=True), jnp.sum(dn1, axis=0, keepdims=True)], axis=0
    )

    @pl.when(i == 0)
    def _():
        small_ref[...] = sums

    @pl.when(i > 0)
    def _():
        small_ref[...] += sums


def pre_self(dqc, cq, wo, da2, xhat, rstd, gain, bt):
    mp = len(dqc)
    share, d = da2.shape
    width = dqc[0].shape[1]
    row = lambda w: pl.BlockSpec((bt, w), lambda i: (i, 0))
    all_of = lambda a: pl.BlockSpec(a.shape, lambda i: (0,) * a.ndim)
    outs = pl.pallas_call(
        functools.partial(pre_self_kernel, mp),
        grid=(share // bt,),
        in_specs=[row(width)] * mp
        + [all_of(w) for w in (*cq, *wo)]
        + [row(d), row(d), row(1), all_of(gain)],
        out_specs=[row(d), row(d)] + [row(width)] * mp + [pl.BlockSpec((2, d), lambda i: (0, 0))],
        out_shape=[jax.ShapeDtypeStruct((share, d), F32), jax.ShapeDtypeStruct((share, d), BF16)]
        + [jax.ShapeDtypeStruct((share, width), BF16)] * mp
        + [jax.ShapeDtypeStruct((2, d), F32)],
        compiler_params=params(),
        cost_estimate=cost(4 * share * d * d, share * d * 14),
    )(*dqc, *cq, *wo, da2, xhat, rstd, gain)
    return outs[0], outs[1], outs[2 : 2 + mp], outs[-1]


def part_kernel(n_in, n_out, per_part, sc, *refs):
    grads, w_ref, outs = refs[:n_in], refs[n_in], refs[n_in + 1 :]
    i = pl.program_id(0)
    total = mm(grads[0][...], w_ref[0], NT)
    for c in range(1, n_in):
        total += mm(grads[c][...], w_ref[c], NT)
    for r in range(n_out):

        @pl.when(jnp.logical_and(i >= r * per_part, i < (r + 1) * per_part))
        def _():
            outs[r][...] = total.astype(outs[r].dtype)


def input_part(sc, grads, w, mp, bt):
    tokens, width = grads[0].shape
    d = w.shape[1]
    nblk = tokens // bt
    per_part = nblk // mp
    outs = pl.pallas_call(
        functools.partial(part_kernel, len(grads), mp, per_part),
        grid_spec=pltpu.PrefetchScalarGridSpec(
            num_scalar_prefetch=1,
            grid=(nblk,),
            in_specs=[pl.BlockSpec((bt, width), lambda i, sc: (sc[i], 0))] * len(grads) + [whole(w)],
            out_specs=[pl.BlockSpec((bt, d), part_map(r, per_part)) for r in range(mp)],
        ),
        out_shape=[jax.ShapeDtypeStruct((tokens // mp, d), F32)]
        + [jax.ShapeDtypeStruct((tokens // mp, d), BF16)] * (mp - 1),
        compiler_params=params(),
        cost_estimate=cost(2 * tokens * d * width * len(grads), tokens * d * 6),
    )(sc, *grads, w)
    return outs


MESH = pl.DeviceIdType.MESH


def all_sum_kernel(plan, nbits, n, *refs):
    ins, outs = refs[: n + 1], refs[n + 1 : 2 * n + 2]
    got = refs[2 * n + 2 : 2 * n + 3 + len(plan)]
    send_sem, recv_sem = refs[2 * n + 3 + len(plan) :]
    me, core = lax.axis_index("batch"), lax.axis_index("mp")
    bit = [(me // (1 << b)) % 2 for b in range(nbits)]
    partner = [(me + (1 << b) * (1 - 2 * bit[b]), core) for b in range(nbits)]
    barrier = pltpu.get_barrier_semaphore()
    for b in range(nbits):
        pl.semaphore_signal(barrier, inc=1, device_id=partner[b], device_id_type=MESH)
    pl.semaphore_wait(barrier, nbits)

    def send(c, s, b, src, dst):
        copy = pltpu.make_async_remote_copy(
            src_ref=src,
            dst_ref=dst,
            send_sem=send_sem.at[c, s],
            recv_sem=recv_sem.at[c, s],
            device_id=partner[b],
            device_id_type=MESH,
        )
        copy.start()
        copies[c].append(copy)

    def rows(off, count):
        return pl.ds(pl.multiple_of(off, 16), count)

    copies = [[] for _ in range(len(plan) + 1)]
    spans = [[(first, count)] for _, first, count, _ in plan]
    slots = [[] for _ in plan]

    def held(c, s, b):
        a, first, count, _ = plan[c]
        half = count >> (s + 1)
        base = first if s == 0 else slots[c][s - 1]
        ref = ins[a] if s == 0 else got[c]
        return ref, base + (1 - bit[b]) * half, base + bit[b] * half, half

    def begin(c, s):
        a, first, count, order = plan[c]
        if s < nbits:
            b = order[s]
            ref, gives, _, half = held(c, s, b)
            slots[c].append(count - (count >> s))
            off = spans[c][s][0]
            spans[c].append((off + bit[b] * half, half))
            send(c, s, b, ref.at[rows(gives, half), :], got[c].at[pl.ds(slots[c][s], half), :])
        else:
            j = 2 * nbits - 1 - s
            block = outs[a].at[rows(*spans[c][j + 1]), :]
            send(c, s, order[j], block, block)

    def finish(c, s):
        copies[c][s].wait_recv()
        if s < nbits:
            a, _, _, order = plan[c]
            ref, _, stays, half = held(c, s, order[s])
            came = pl.ds(slots[c][s], half)
            total = ref[rows(stays, half), :].astype(F32) + got[c][came, :].astype(F32)
            if s < nbits - 1:
                got[c][came, :] = total.astype(BF16)
            else:
                outs[a][rows(*spans[c][s + 1]), :] = total.astype(BF16)

    last = len(plan)
    size = ins[n].shape[0]
    outs[n][...] = ins[n][...]
    for s in range(2 * nbits + 1):
        if 1 <= s <= nbits:
            copies[last][s - 1].wait()
            outs[n][...] = (
                outs[n][...].astype(F32) + got[last][(s - 1) * size : s * size, :].astype(F32)
            ).astype(BF16)
        if s < nbits:
            send(last, s, s, outs[n], got[last].at[pl.ds(s * size, size), :])
        for c in range(len(plan)):
            if s >= 1:
                finish(c, s - 1)
            if s < 2 * nbits:
                begin(c, s)
    for c in range(len(plan)):
        for copy in copies[c]:
            copy.wait_send()


def all_sum(arrays, splits, small, devices):
    nbits = devices.bit_length() - 1
    if devices != 1 << nbits or nbits < 3:
        return [lax.psum(a, "batch") for a in (*arrays, small)]
    x_y, y_x = tuple(range(nbits)), (1, 0, *range(2, nbits))
    far = (*range(2, nbits), 0, 1)
    flat = [a.reshape(-1, a.shape[-1]) for a in arrays]
    plan, used = [], []
    for a, parts in zip(flat, splits):
        count = a.shape[0] // parts
        if a.shape[0] % parts == 0 and count % (16 * devices) == 0:
            for p in range(parts):
                order = far if parts == 3 else (x_y, y_x)[len(plan) % 2]
                plan.append((len(used), p * count, count, order))
            used.append(a)
        else:
            used.append(None)
    keep = [i for i, a in enumerate(used) if a is not None]
    plan = [(keep.index(i), *rest) for i, *rest in plan]
    small = jnp.pad(small, ((0, 16 - small.shape[0]), (0, 0)))
    operands = [used[i] for i in keep] + [small]
    vmem = pl.BlockSpec(memory_space=pltpu.VMEM)
    sums = pl.pallas_call(
        functools.partial(all_sum_kernel, plan, nbits, len(keep)),
        in_specs=[vmem] * len(operands),
        out_specs=[vmem] * len(operands),
        out_shape=[jax.ShapeDtypeStruct(a.shape, a.dtype) for a in operands],
        scratch_shapes=[pltpu.VMEM((rows, operands[i].shape[1]), BF16) for i, _, rows, _ in plan]
        + [pltpu.VMEM((16 * nbits, small.shape[1]), BF16)]
        + [pltpu.SemaphoreType.DMA((len(plan) + 1, 2 * nbits))] * 2,
        compiler_params=pltpu.CompilerParams(
            collective_id=7, has_side_effects=True, vmem_limit_bytes=VMEM_BYTES
        ),
    )(*operands)
    outs = [
        sums[keep.index(i)].reshape(a.shape) if i in keep else lax.psum(a, "batch")
        for i, a in enumerate(arrays)
    ]
    return outs + [sums[-1]]


def across(r, shift, devices):
    return [(i, i ^ (r << shift)) for i in range(devices)]


def cut(blocks, shift, bits, me):
    place = (me >> shift) % (1 << bits)
    return [lax.dynamic_index_in_dim(blocks, place ^ r, 0, keepdims=False) for r in range(1 << bits)]


def scatter_step(blocks, shift, devices):
    return blocks[:1] + [lax.ppermute(b, "batch", across(r, shift, devices)) for r, b in enumerate(blocks) if r]


def add_up(blocks):
    total = blocks[0].astype(F32)
    for b in blocks[1:]:
        total += b.astype(F32)
    return total.astype(BF16)


def gather_step(block, shift, bits, devices):
    return [block] + [lax.ppermute(block, "batch", across(r, shift, devices)) for r in range(1, 1 << bits)]


def in_order(pieces, place):
    return jnp.stack(
        [lax.select_n(place ^ c, *pieces) if len(pieces) > 1 else pieces[0] for c in range(len(pieces))]
    )


def lay_kernel(n, rows, sc, *refs):
    pieces, outs = refs[:n], refs[n:]
    c = pl.program_id(0)
    for r in range(n):

        @pl.when((sc[0] ^ c) == r)
        def _():
            at = 0
            for out, count in zip(outs, rows):
                out[...] = pieces[r][:, at : at + count, :].astype(F32).reshape(out.shape)
                at += count


def lay_out(pieces, place, shapes, rows):
    n = len(pieces)
    d = pieces[0].shape[-1]
    if any(count % 16 for count in rows):
        blocks = in_order(pieces, place)
        flat = blocks.reshape(-1, *blocks.shape[2:]).astype(F32)
        at, outs = 0, []
        for shape, count in zip(shapes, rows):
            outs.append(flat[:, at : at + count].reshape(shape))
            at += count
        return outs
    return pl.pallas_call(
        functools.partial(lay_kernel, n, rows),
        grid_spec=pltpu.PrefetchScalarGridSpec(
            num_scalar_prefetch=1,
            grid=(n,),
            in_specs=[whole(p) for p in pieces],
            out_specs=[pl.BlockSpec((s[0] // n, d), lambda i, sc: (i, 0)) for s in shapes],
        ),
        out_shape=[jax.ShapeDtypeStruct(s, F32) for s in shapes],
        compiler_params=params(),
        cost_estimate=cost(0, sum(s[0] * d * 6 for s in shapes)),
    )(place.reshape(1).astype(jnp.int32), *pieces)


def shards(
    block_input_slots,
    memory,
    target_sentence_lengths,
    source_lengths,
    self_qkv,
    self_out,
    cross_query,
    cross_kv,
    cross_out,
    up_proj,
    down_proj,
    norm_gains,
    norm_biases,
    cotangent,
    mp,
    devices,
):
    tokens, d = block_input_slots.shape
    mem_tokens = memory.shape[0]
    share = cotangent.shape[0]
    mem_share = mem_tokens // mp
    width = self_qkv.shape[2]
    me = lax.axis_index("mp")
    bt = min(256, share)
    bq = min(256, share)
    bk = min(256, mem_tokens)

    def spread(own):
        return [own] + [
            lax.ppermute(own, "mp", [(i, (i + r) % mp) for i in range(mp)]) for r in range(1, mp)
        ]

    def exchange(pieces):
        got = [pieces[0]] + [None] * (mp - 1)
        for r in range(1, mp):
            got[mp - r] = lax.ppermute(pieces[r], "mp", [(i, (i - r) % mp) for i in range(mp)])
        return got

    wo, cq, co = spread(self_out), spread(cross_query), spread(cross_out)
    up, down = spread(up_proj), spread(down_proj)
    gain, shift = norm_gains.T, norm_biases.T

    t_len = target_sentence_lengths.reshape(-1)
    s_len = source_lengths.reshape(-1)
    t_end, s_end = jnp.cumsum(t_len), jnp.cumsum(s_len)
    t_start, s_start = t_end - t_len, s_end - s_len
    first = ((me - jnp.arange(mp)) % mp) * share
    place = (first[:, None] + jnp.arange(share)[None, :]).reshape(-1).astype(jnp.int32)
    begun = place[:, None] >= t_start[None, :]
    self_lo = jnp.max(jnp.where(begun, t_start[None, :], 0), axis=1)
    self_hi = place + 1
    cross_lo = jnp.max(jnp.where(begun, s_start[None, :], 0), axis=1)
    cross_hi = jnp.max(jnp.where(begun, s_end[None, :], 0), axis=1)
    nblk = tokens // bq
    q_block = place.reshape(nblk, bq)[:, 0] // bq

    def table(lo, hi):
        return jnp.concatenate(
            [lo.reshape(nblk, bq)[:, 0] // bk, (hi.reshape(nblk, bq)[:, -1] + bk - 1) // bk, q_block]
        ).astype(jnp.int32)

    self_table, cross_table = table(self_lo, self_hi), table(cross_lo, cross_hi)
    as_row = lambda v: v.reshape(1, tokens).astype(jnp.int32)
    self_lo, self_hi, cross_lo, cross_hi = map(as_row, (self_lo, self_hi, cross_lo, cross_hi))

    proj = [mm(block_input_slots, self_qkv[c]).astype(BF16) for c in range(3)]
    pair = [mm(memory, cross_kv[c]).astype(BF16) for c in range(2)]
    self_kt, self_vt = proj[1].T, proj[2].T
    cross_kt, cross_vt = pair[0].T, pair[1].T
    ctx_parts, self_lse = attend(
        self_table, proj[:1], proj[1], self_vt, self_lo, self_hi, mp, bq, bk
    )
    ctx = exchange(ctx_parts)
    me_row = me.reshape(1).astype(jnp.int32)
    n1, xhat1, rstd1, qc = post_self(me_row, block_input_slots, ctx, wo, cq, gain, shift, share, bt)
    qc_parts = exchange(qc)
    cctx_parts, cross_lse = attend(
        cross_table, qc_parts, pair[0], cross_vt, cross_lo, cross_hi, mp, bq, bk
    )
    cctx = exchange(cctx_parts)
    layer_output, da2, n2, e3, e2, dcctx, hid, dpre, small23 = middle(
        cctx, n1, cotangent, co, up, down, gain, shift, bt
    )
    dcctx_parts = exchange(dcctx)

    def grads(lefts, rights):
        return [mm(a, b, TN).astype(BF16) for a, b in zip(lefts, rights)]

    def collect(pieces):
        got = exchange(pieces)
        total = got[0].astype(F32)
        for g in got[1:]:
            total += g.astype(F32)
        return total

    early = [
        collect(grads(dpre, [n2] * mp)).astype(BF16),
        collect(grads(hid, [e3] * mp)).astype(BF16),
        collect(grads(cctx, [e2] * mp)).astype(BF16),
    ]
    row = lax.axis_index("batch")
    near, far = 2, devices.bit_length() - 3
    blocks = jnp.concatenate([g.reshape(devices, -1, d) for g in early], axis=1)
    blocks = blocks.reshape(1 << near, 1 << far, -1, d)
    dcctx_parts, blocks = lax.optimization_barrier((dcctx_parts, cut(blocks, 0, near, row)))
    blocks = scatter_step(blocks, 0, devices)
    dqc_parts, dkc, dvc = attend_back(
        cross_table, qc_parts, dcctx_parts, cctx_parts, pair[0], cross_kt, pair[1], cross_lo, cross_hi, cross_lse, mp, bq, bk
    )
    dqc = exchange(dqc_parts)
    dqc, blocks = lax.optimization_barrier((dqc, cut(add_up(blocks), near, far, row)))
    blocks = scatter_step(blocks, near, devices)
    da1, e1, dctx, small1 = pre_self(dqc, cq, wo, da2, xhat1, rstd1, gain, bt)
    dctx_parts = exchange(dctx)
    mem_bt = min(256, mem_share)
    mem_nb = mem_share // mem_bt
    mem_blocks = ((((me - jnp.arange(mp)) % mp) * mem_nb)[:, None] + jnp.arange(mem_nb)[None, :]).reshape(-1)
    memory_parts = input_part(mem_blocks.astype(jnp.int32), [dkc, dvc], cross_kv, mp, mem_bt)
    memory_grad = collect(memory_parts)
    cross_kv_grad = jnp.stack([mm(memory, g, TN) for g in (dkc, dvc)])
    cross_query_grad = collect(grads([n1] * mp, dqc))
    self_out_grad = collect(grads(ctx, [e1] * mp))
    dctx_parts, block = lax.optimization_barrier((dctx_parts, add_up(blocks)))
    blocks = gather_step(block, near, far, devices)
    (dq,), dk, dv = attend_back(
        self_table, proj[:1], dctx_parts, ctx_parts, proj[1], self_kt, proj[2], self_lo, self_hi, self_lse, mp, bq, bk
    )
    dq, block = lax.optimization_barrier((dq, in_order(blocks, row >> near)))
    spread_out = gather_step(block, 0, near, devices)
    input_parts = input_part(q_block.astype(jnp.int32), [dq, dk, dv], self_qkv, mp, bq)
    input_grad = collect(input_parts) + da1
    self_qkv_grad = jnp.stack([mm(block_input_slots, g, TN) for g in (dq, dk, dv)])

    small = jnp.concatenate([small1[:1], small23[:2], small1[1:], small23[2:]], axis=0)
    part = d // mp
    pieces = [
        lax.dynamic_slice_in_dim(small, ((me - r) % mp) * part, part, 1).astype(BF16) for r in range(mp)
    ]
    small = collect(pieces)
    *summed, small = all_sum(
        [
            g.astype(BF16)
            for g in (
                self_qkv_grad,
                self_out_grad,
                cross_query_grad,
                cross_kv_grad,
            )
        ],
        (3, 1, 1, 2),
        small.astype(BF16),
        devices,
    )
    up_grad, down_grad, cross_out_grad = lay_out(
        spread_out, row % (1 << near), [g.shape for g in early], [g.shape[0] // devices for g in early]
    )
    summed = [g.astype(F32) for g in summed] + [cross_out_grad, up_grad, down_grad]
    small = small.astype(F32).T
    return (layer_output, input_grad, memory_grad, *summed, small[:, :3], small[:, 3:6])


def solution(mesh):
    mp = mesh.shape["mp"]
    rows = P("batch", None)
    both = P(("batch", "mp"), None)
    first, last, last3 = P("mp", None), P(None, "mp"), P(None, None, "mp")
    return jax.shard_map(
        functools.partial(shards, mp=mp, devices=mesh.shape["batch"]),
        mesh=mesh,
        in_specs=(rows, rows, rows, rows, last3, first, last, last3, first, first, first, P(), P(), both),
        out_specs=(both, both, both, last3, first, last, last3, first, first, first, first, first),
        check_vma=False,
    )
```

```python
import functools
import math

import jax
import jax.numpy as jnp
from jax import lax
from jax.experimental import pallas as pl
from jax.experimental.pallas import tpu as pltpu
from jax.sharding import PartitionSpec as P

DH = 64
NEG = -1e30
F32 = jnp.float32
BF16 = jnp.bfloat16
SCALE = DH**-0.5
SCALE2 = SCALE * math.log2(math.e)
NT = (((1,), (1,)), ((), ()))
NN = (((1,), (0,)), ((), ()))
TN = (((0,), (0,)), ((), ()))


def mm(a, b, dims=NN):
    return lax.dot_general(a, b, dims, preferred_element_type=F32)


def params(mib):
    return pltpu.CompilerParams(dimension_semantics=("arbitrary",), vmem_limit_bytes=mib << 20)


def cost(flops, nbytes, exps=0):
    return pl.CostEstimate(flops=int(flops), bytes_accessed=int(nbytes), transcendentals=int(exps))


def pick(i, per_part, refs):
    value = refs[0][...]
    for r in range(1, len(refs)):
        value = jnp.where(i >= r * per_part, refs[r][...], value)
    return value


def part_map(r, per_part):
    return lambda i, sc: (jnp.clip(i - r * per_part, 0, per_part - 1), 0)


def group_of(heads):
    return min(heads, 128 // DH)


def per_head(block, heads):
    many = group_of(heads)
    wide = many * DH
    head = lax.broadcasted_iota(jnp.int32, (block.shape[0], wide), 1) // DH
    parts = []
    for h in range(heads):
        cols = block[:, h // many * wide : (h // many + 1) * wide]
        parts.append(jnp.where(head == h % many, cols, jnp.zeros_like(cols)))
    return jnp.concatenate(parts, axis=0)


def attend_kernel(nblk, per_part, n_q, n_out, heads, bq, bk, sc, *refs):
    q_refs, refs = refs[:n_q], refs[n_q:]
    k_ref, vt_ref, lo_ref, hi_ref = refs[:4]
    out_refs, (lse_ref, acc_ref, q_heads, s_ref, p_ref) = refs[4 : 4 + n_out], refs[4 + n_out :]
    i = pl.program_id(0)
    q_heads[...] = per_head(pick(i, per_part, q_refs), heads)
    lo = lo_ref[...]
    hi = hi_ref[...]
    acc_ref[...] = jnp.zeros_like(acc_ref)
    place = lax.broadcasted_iota(jnp.int32, (bk, bq), 0)
    span = [slice(h * bq, (h + 1) * bq) for h in range(heads)]
    cols = [slice(h * DH, (h + 1) * DH) for h in range(heads)]
    many = group_of(heads)
    wide = [slice(h // many * many * DH, (h // many + 1) * many * DH) for h in range(heads)]

    first, end = sc[i], sc[nblk + i]

    def rows(kb):
        return pl.ds(pl.multiple_of(kb * bk, bk), bk)

    def scores(kb, h):
        s_ref[:, span[h]] = mm(k_ref[rows(kb), wide[h]], q_heads[span[h], :], NT)

    def soften(kb, h, keep, top, total):
        t = jnp.where(keep, s_ref[:, span[h]] * SCALE2, NEG)
        new_top = jnp.maximum(top, jnp.max(t, axis=0, keepdims=True))
        e = jnp.exp2(t - new_top)
        decay = jnp.exp2(top - new_top)
        p_ref[:, span[h]] = e.astype(BF16)
        return new_top, total * decay + jnp.sum(e, axis=0, keepdims=True), decay

    def gather(kb, h, decay):
        acc_ref[cols[h], :] = acc_ref[cols[h], :] * decay + mm(vt_ref[cols[h], rows(kb)], p_ref[:, span[h]])

    def stage(kb, carry):
        start = kb * bk
        keep = jnp.logical_and(place >= lo - start, place < hi - start)
        after = jnp.minimum(kb + 1, end - 1)
        new = []
        for h in range(heads):
            top, total, decay = carry[h]
            if decay is not None:
                gather(kb - 1, h, decay)
            new.append(soften(kb, h, keep, top, total))
            scores(after, h)
        return new

    for h in range(heads):
        scores(first, h)
    none = jnp.full((1, bq), NEG, F32), jnp.zeros((1, bq), F32), None
    carry = lax.fori_loop(first + 1, end, stage, stage(first, [none] * heads))
    for h in range(heads):
        gather(end - 1, h, carry[h][2])
    top = [carry[h][0] for h in range(heads)]
    total = [carry[h][1] for h in range(heads)]
    for h in range(heads):
        acc_ref[cols[h], :] = acc_ref[cols[h], :] / total[h]
        lse_ref[0, h : h + 1, :] = top[h] + jnp.log2(total[h])
    ctx = acc_ref[...].T.astype(BF16)
    for r in range(n_out):

        @pl.when(jnp.logical_and(i >= r * per_part, i < (r + 1) * per_part))
        def _():
            out_refs[r][...] = ctx


def attend(sc, q_parts, keys, values_t, lo, hi, mp, bq, bk):
    tokens, width = sum(q.shape[0] for q in q_parts), keys.shape[1]
    heads = width // DH
    nblk, per_part = tokens // bq, tokens // bq // mp
    if len(q_parts) == 1 and mp > 1:
        q_specs = [pl.BlockSpec((bq, width), lambda i, sc: (sc[2 * nblk + i], 0))]
    else:
        q_specs = [pl.BlockSpec((bq, width), part_map(r, per_part)) for r in range(mp)]
    full = lambda a: pl.BlockSpec(a.shape, lambda i, sc: (0, 0))
    row = pl.BlockSpec((1, bq), lambda i, sc: (0, i))
    outs = pl.pallas_call(
        functools.partial(attend_kernel, nblk, per_part, len(q_parts), mp, heads, bq, bk),
        grid_spec=pltpu.PrefetchScalarGridSpec(
            num_scalar_prefetch=1,
            grid=(nblk,),
            in_specs=q_specs + [full(keys), full(values_t), row, row],
            out_specs=[pl.BlockSpec((bq, width), part_map(r, per_part)) for r in range(mp)]
            + [pl.BlockSpec((1, heads, bq), lambda i, sc: (i, 0, 0))],
            scratch_shapes=[
                pltpu.VMEM((width, bq), F32),
                pltpu.VMEM((heads * bq, group_of(heads) * DH), BF16),
                pltpu.VMEM((bk, heads * bq), F32),
                pltpu.VMEM((bk, heads * bq), BF16),
            ],
        ),
        out_shape=[jax.ShapeDtypeStruct((tokens // mp, width), BF16)] * mp
        + [jax.ShapeDtypeStruct((nblk, heads, bq), F32)],
        compiler_params=params(14),
        cost_estimate=cost(4 * tokens * 512 * width, 8 * tokens * width, tokens * 512 * heads),
    )(sc, *q_parts, keys, values_t, lo, hi)
    return outs[:mp], outs[mp]


def attend_back_kernel(nblk, per_part, n_q, n_part, heads, bq, bk, sc, *refs):
    q_refs, refs = refs[:n_q], refs[n_q:]
    do_refs, refs = refs[:n_part], refs[n_part:]
    o_refs, refs = refs[:n_part], refs[n_part:]
    k_ref, kt_ref, v_ref, lo_ref, hi_ref, lse_ref = refs[:6]
    dq_refs, refs = refs[6 : 6 + n_q], refs[6 + n_q :]
    dk_ref, dv_ref, dk_acc, dv_acc, dq_acc, q_heads, do_heads = refs
    i = pl.program_id(0)

    @pl.when(i == 0)
    def _():
        dk_acc[...] = jnp.zeros_like(dk_acc)
        dv_acc[...] = jnp.zeros_like(dv_acc)

    q_heads[...] = per_head(pick(i, per_part, q_refs), heads)
    do = pick(i, per_part, do_refs)
    do_heads[...] = per_head(do, heads)
    lo = lo_ref[...]
    hi = hi_ref[...]
    span = [slice(h * bq, (h + 1) * bq) for h in range(heads)]
    cols = [slice(h * DH, (h + 1) * DH) for h in range(heads)]
    many = group_of(heads)
    wide = [slice(h // many * many * DH, (h // many + 1) * many * DH) for h in range(heads)]
    prod = (do.astype(F32) * pick(i, per_part, o_refs).astype(F32)).T
    delta = [jnp.sum(prod[cols[h], :], axis=0, keepdims=True) for h in range(heads)]
    lse = [lse_ref[0, h : h + 1, :] for h in range(heads)]
    dq_acc[...] = jnp.zeros_like(dq_acc)
    place = lax.broadcasted_iota(jnp.int32, (bk, bq), 0)

    def step(kb, carry):
        start = pl.multiple_of(kb * bk, bk)
        rows = pl.ds(start, bk)
        kt = kt_ref[:, rows]
        keep = jnp.logical_and(place >= lo - start, place < hi - start)
        groups = [(slice(h * bq, (h + many) * bq), wide[h]) for h in range(0, heads, many)]
        s = [mm(k_ref[rows, w], q_heads[g, :], NT) * SCALE2 for g, w in groups]
        dp = [mm(v_ref[rows, w], do_heads[g, :], NT) for g, w in groups]
        at = [(h // many, slice(h % many * bq, (h % many + 1) * bq)) for h in range(heads)]
        p = [jnp.where(keep, jnp.exp2(s[g][:, c] - lse[h]), 0.0) for h, (g, c) in enumerate(at)]
        ds = [(p[h] * (dp[g][:, c] - delta[h])).astype(BF16) for h, (g, c) in enumerate(at)]
        p = [p[h].astype(BF16) for h in range(heads)]
        for g, (r, w) in enumerate(groups):
            here = slice(g * many, (g + 1) * many)
            dv_acc[rows, w] += mm(jnp.concatenate(p[here], axis=1), do_heads[r, :])
            dk_acc[rows, w] += mm(jnp.concatenate(ds[here], axis=1), q_heads[r, :])
        for h in range(heads):
            dq_acc[cols[h], :] += mm(kt[cols[h], :], ds[h])
        return carry

    lax.fori_loop(sc[i], sc[nblk + i], step, 0)
    dq = (dq_acc[...] * SCALE).T.astype(BF16)
    if n_q == 1:
        dq_refs[0][...] = dq
    else:
        for r in range(n_q):

            @pl.when(jnp.logical_and(i >= r * per_part, i < (r + 1) * per_part))
            def _():
                dq_refs[r][...] = dq

    @pl.when(i == nblk - 1)
    def _():
        dk_ref[...] = (dk_acc[...] * SCALE).astype(BF16)
        dv_ref[...] = dv_acc[...].astype(BF16)


def attend_back(sc, q_parts, do_parts, o_parts, keys, keys_t, values, lo, hi, lse, mp, bq, bk):
    tokens, width = sum(q.shape[0] for q in q_parts), keys.shape[1]
    heads = width // DH
    nblk, per_part = tokens // bq, tokens // bq // mp
    parts = [pl.BlockSpec((bq, width), part_map(r, per_part)) for r in range(mp)]
    if len(q_parts) == 1 and mp > 1:
        q_specs = [pl.BlockSpec((bq, width), lambda i, sc: (sc[2 * nblk + i], 0))]
    else:
        q_specs = parts
    full = lambda a: pl.BlockSpec(a.shape, lambda i, sc: (0, 0))
    row = pl.BlockSpec((1, bq), lambda i, sc: (0, i))
    outs = pl.pallas_call(
        functools.partial(attend_back_kernel, nblk, per_part, len(q_parts), mp, heads, bq, bk),
        grid_spec=pltpu.PrefetchScalarGridSpec(
            num_scalar_prefetch=1,
            grid=(nblk,),
            in_specs=q_specs
            + parts
            + parts
            + [full(keys), full(keys_t), full(values), row, row]
            + [pl.BlockSpec((1, heads, bq), lambda i, sc: (i, 0, 0))],
            out_specs=q_specs + [full(keys), full(keys)],
            scratch_shapes=[
                pltpu.VMEM(keys.shape, F32),
                pltpu.VMEM(keys.shape, F32),
                pltpu.VMEM((width, bq), F32),
                pltpu.VMEM((heads * bq, group_of(heads) * DH), BF16),
                pltpu.VMEM((heads * bq, group_of(heads) * DH), BF16),
            ],
        ),
        out_shape=[jax.ShapeDtypeStruct(q.shape, BF16) for q in q_parts]
        + [jax.ShapeDtypeStruct(keys.shape, BF16)] * 2,
        compiler_params=params(26),
        cost_estimate=cost(10 * tokens * 512 * width, 12 * tokens * width, tokens * 512 * heads),
    )(sc, *q_parts, *do_parts, *o_parts, keys, keys_t, values, lo, hi, lse)
    return outs[: len(q_parts)], outs[-2], outs[-1]


def norm_stats(a):
    centre = a - jnp.mean(a, axis=-1, keepdims=True)
    rstd = lax.rsqrt(jnp.mean(centre * centre, axis=-1, keepdims=True) + 1e-05)
    return centre * rstd, rstd


def norm_back(dy, xhat, rstd, gain):
    t = dy * gain
    mean_t = jnp.mean(t, axis=-1, keepdims=True)
    mean_tx = jnp.mean(t * xhat, axis=-1, keepdims=True)
    return rstd * (t - mean_t - xhat * mean_tx)


def project_kernel(n, turned, x_ref, w_ref, *outs):
    x = x_ref[...]
    for c in range(n):
        y = mm(x, w_ref[c])
        outs[c][...] = y.astype(BF16)
        if c in turned:
            outs[n + turned.index(c)][...] = y.T.astype(BF16)


def project(x, w, turned, bt):
    n, d, width = w.shape
    tokens = x.shape[0]
    return pl.pallas_call(
        functools.partial(project_kernel, n, turned),
        grid=(tokens // bt,),
        in_specs=[pl.BlockSpec((bt, d), lambda i: (i, 0)), pl.BlockSpec(w.shape, lambda i: (0, 0, 0))],
        out_specs=[pl.BlockSpec((bt, width), lambda i: (i, 0))] * n
        + [pl.BlockSpec((width, bt), lambda i: (0, i))] * len(turned),
        out_shape=[jax.ShapeDtypeStruct((tokens, width), BF16)] * n
        + [jax.ShapeDtypeStruct((width, tokens), BF16)] * len(turned),
        compiler_params=params(14),
        cost_estimate=cost(2 * tokens * d * width * n, tokens * (d + 2 * n * width) * 2),
    )(x, w)


def post_self_kernel(mp, sc, *refs):
    x_ref = refs[0]
    ctx, wo, cq = refs[1 : 1 + mp], refs[1 + mp : 1 + 2 * mp], refs[1 + 2 * mp : 1 + 3 * mp]
    gain_ref, shift_ref = refs[1 + 3 * mp : 3 + 3 * mp]
    n1_ref, xhat_ref, rstd_ref = refs[3 + 3 * mp : 6 + 3 * mp]
    qc = refs[6 + 3 * mp :]
    a1 = x_ref[...].astype(F32)
    for r in range(mp):
        a1 += mm(ctx[r][...], wo[r][...])
    xhat, rstd = norm_stats(a1)
    n1 = (xhat * gain_ref[0:1, :] + shift_ref[0:1, :]).astype(BF16)
    n1_ref[...] = n1
    xhat_ref[...] = xhat
    rstd_ref[...] = rstd
    for r in range(mp):
        qc[r][...] = mm(n1, cq[r][...]).astype(BF16)


def whole(a):
    return pl.BlockSpec(a.shape, lambda i, sc: (0,) * a.ndim)


def rows_of(bt, width):
    return pl.BlockSpec((bt, width), lambda i, sc: (i, 0))


def post_self(sc, x, ctx, wo, cq, gain, shift, share, bt):
    mp, d = len(ctx), x.shape[1]
    width = ctx[0].shape[1]
    nb = share // bt
    outs = pl.pallas_call(
        functools.partial(post_self_kernel, mp),
        grid_spec=pltpu.PrefetchScalarGridSpec(
            num_scalar_prefetch=1,
            grid=(nb,),
            in_specs=[pl.BlockSpec((bt, d), lambda i, sc: (sc[0] * nb + i, 0))]
            + [rows_of(bt, width)] * mp
            + [whole(w) for w in (*wo, *cq, gain, shift)],
            out_specs=[rows_of(bt, d), rows_of(bt, d), rows_of(bt, 1)] + [rows_of(bt, width)] * mp,
        ),
        out_shape=[
            jax.ShapeDtypeStruct((share, d), BF16),
            jax.ShapeDtypeStruct((share, d), F32),
            jax.ShapeDtypeStruct((share, 1), F32),
        ]
        + [jax.ShapeDtypeStruct((share, width), BF16)] * mp,
        compiler_params=params(16),
        cost_estimate=cost(4 * share * d * d, share * d * 12),
    )(sc, x, *ctx, *wo, *cq, gain, shift)
    return outs[0], outs[1], outs[2], outs[3:]


def middle_kernel(mp, *refs):
    refs = list(refs)

    def take(n):
        got = refs[:n]
        del refs[:n]
        return got

    cctx, (n1_ref, cot_ref) = take(mp), take(2)
    co, up, down = take(mp), take(mp), take(mp)
    gain_ref, shift_ref = take(2)
    out_ref, da2_ref, n2_ref, e3_ref, e2_ref = take(5)
    dcctx, hid, dpre = take(mp), take(mp), take(mp)
    (small_ref,) = take(1)
    (slope_ref,) = take(1)
    ff = up[0].shape[0]
    i = pl.program_id(0)

    a2 = n1_ref[...].astype(F32)
    for r in range(mp):
        a2 += mm(cctx[r][...], co[r][...])
    xhat2, rstd2 = norm_stats(a2)
    n2 = (xhat2 * gain_ref[1:2, :] + shift_ref[1:2, :]).astype(BF16)
    n2_ref[...] = n2
    a3 = n2.astype(F32)
    for r in range(mp):
        u = mm(n2, up[r][...], NT)
        sg = 0.5 * jnp.tanh(0.5 * u) + 0.5
        h = u * sg
        hid[r][...] = h.astype(BF16)
        slope_ref[:, r * ff : (r + 1) * ff] = sg + h * (1.0 - sg)
        a3 += mm(hid[r][...], down[r][...])
    xhat3, rstd3 = norm_stats(a3)
    out_ref[...] = (xhat3 * gain_ref[2:3, :] + shift_ref[2:3, :]).astype(BF16)
    g = cot_ref[...].astype(F32)
    da3 = norm_back(g, xhat3, rstd3, gain_ref[2:3, :])
    e3 = da3.astype(BF16)
    e3_ref[...] = e3
    dn2 = da3
    for r in range(mp):
        dh = mm(e3, down[r][...], NT)
        dpre[r][...] = (dh * slope_ref[:, r * ff : (r + 1) * ff]).astype(BF16)
        dn2 += mm(dpre[r][...], up[r][...])
    da2 = norm_back(dn2, xhat2, rstd2, gain_ref[1:2, :])
    da2_ref[...] = da2
    e2 = da2.astype(BF16)
    e2_ref[...] = e2
    for r in range(mp):
        dcctx[r][...] = mm(e2, co[r][...], NT).astype(BF16)
    sums = jnp.concatenate(
        [
            jnp.sum(dn2 * xhat2, axis=0, keepdims=True),
            jnp.sum(g * xhat3, axis=0, keepdims=True),
            jnp.sum(dn2, axis=0, keepdims=True),
            jnp.sum(g, axis=0, keepdims=True),
        ],
        axis=0,
    )

    @pl.when(i == 0)
    def _():
        small_ref[...] = sums

    @pl.when(i > 0)
    def _():
        small_ref[...] += sums


def middle(cctx, n1, cot, co, up, down, gain, shift, bt):
    mp = len(cctx)
    share, d = n1.shape
    width = cctx[0].shape[1]
    ff = up[0].shape[0]
    row = lambda w: pl.BlockSpec((bt, w), lambda i: (i, 0))
    all_of = lambda a: pl.BlockSpec(a.shape, lambda i: (0,) * a.ndim)
    shape = lambda w, t: jax.ShapeDtypeStruct((share, w), t)
    outs = pl.pallas_call(
        functools.partial(middle_kernel, mp),
        grid=(share // bt,),
        in_specs=[row(width)] * mp + [row(d)] * 2 + [all_of(w) for w in (*co, *up, *down, gain, shift)],
        out_specs=[row(d)] * 5
        + [row(width)] * mp
        + [row(ff)] * (2 * mp)
        + [pl.BlockSpec((4, d), lambda i: (0, 0))],
        scratch_shapes=[pltpu.VMEM((bt, ff * mp), F32)],
        out_shape=[shape(d, BF16), shape(d, F32), shape(d, BF16), shape(d, BF16), shape(d, BF16)]
        + [shape(width, BF16)] * mp
        + [shape(ff, BF16)] * (2 * mp)
        + [jax.ShapeDtypeStruct((4, d), F32)],
        compiler_params=params(44),
        cost_estimate=cost(8 * share * d * ff * mp + 4 * share * d * d, share * ff * mp * 4, share * ff * mp),
    )(*cctx, n1, cot, *co, *up, *down, gain, shift)
    out, da2, n2, e3, e2 = outs[:5]
    return out, da2, n2, e3, e2, outs[5 : 5 + mp], outs[5 + mp : 5 + 2 * mp], outs[5 + 2 * mp : 5 + 3 * mp], outs[-1]


def pre_self_kernel(mp, *refs):
    dqc, cq, wo = refs[:mp], refs[mp : 2 * mp], refs[2 * mp : 3 * mp]
    da2_ref, xhat_ref, rstd_ref, gain_ref = refs[3 * mp : 3 * mp + 4]
    da1_ref, e1_ref = refs[3 * mp + 4 : 3 * mp + 6]
    dctx = refs[3 * mp + 6 : 4 * mp + 6]
    small_ref = refs[4 * mp + 6]
    i = pl.program_id(0)
    dn1 = da2_ref[...]
    for r in range(mp):
        dn1 += mm(dqc[r][...], cq[r][...], NT)
    xhat = xhat_ref[...]
    da1 = norm_back(dn1, xhat, rstd_ref[...], gain_ref[0:1, :])
    da1_ref[...] = da1
    e1 = da1.astype(BF16)
    e1_ref[...] = e1
    for r in range(mp):
        dctx[r][...] = mm(e1, wo[r][...], NT).astype(BF16)
    sums = jnp.concatenate(
        [jnp.sum(dn1 * xhat, axis=0, keepdims=True), jnp.sum(dn1, axis=0, keepdims=True)], axis=0
    )

    @pl.when(i == 0)
    def _():
        small_ref[...] = sums

    @pl.when(i > 0)
    def _():
        small_ref[...] += sums


def pre_self(dqc, cq, wo, da2, xhat, rstd, gain, bt):
    mp = len(dqc)
    share, d = da2.shape
    width = dqc[0].shape[1]
    row = lambda w: pl.BlockSpec((bt, w), lambda i: (i, 0))
    all_of = lambda a: pl.BlockSpec(a.shape, lambda i: (0,) * a.ndim)
    outs = pl.pallas_call(
        functools.partial(pre_self_kernel, mp),
        grid=(share // bt,),
        in_specs=[row(width)] * mp
        + [all_of(w) for w in (*cq, *wo)]
        + [row(d), row(d), row(1), all_of(gain)],
        out_specs=[row(d), row(d)] + [row(width)] * mp + [pl.BlockSpec((2, d), lambda i: (0, 0))],
        out_shape=[jax.ShapeDtypeStruct((share, d), F32), jax.ShapeDtypeStruct((share, d), BF16)]
        + [jax.ShapeDtypeStruct((share, width), BF16)] * mp
        + [jax.ShapeDtypeStruct((2, d), F32)],
        compiler_params=params(16),
        cost_estimate=cost(4 * share * d * d, share * d * 14),
    )(*dqc, *cq, *wo, da2, xhat, rstd, gain)
    return outs[0], outs[1], outs[2 : 2 + mp], outs[-1]


def part_kernel(n_in, n_out, per_part, sc, *refs):
    grads, w_ref, outs = refs[:n_in], refs[n_in], refs[n_in + 1 :]
    i = pl.program_id(0)
    total = mm(jnp.concatenate([g[...] for g in grads], axis=1), w_ref[...])
    for r in range(n_out):

        @pl.when(jnp.logical_and(i >= r * per_part, i < (r + 1) * per_part))
        def _():
            outs[r][...] = total.astype(outs[r].dtype)


def input_part(sc, grads, w, mp, bt):
    tokens, width = grads[0].shape
    d = w.shape[1]
    w = w.swapaxes(1, 2).reshape(-1, d)
    nblk = tokens // bt
    per_part = nblk // mp
    outs = pl.pallas_call(
        functools.partial(part_kernel, len(grads), mp, per_part),
        grid_spec=pltpu.PrefetchScalarGridSpec(
            num_scalar_prefetch=1,
            grid=(nblk,),
            in_specs=[pl.BlockSpec((bt, width), lambda i, sc: (sc[i], 0))] * len(grads) + [whole(w)],
            out_specs=[pl.BlockSpec((bt, d), part_map(r, per_part)) for r in range(mp)],
        ),
        out_shape=[jax.ShapeDtypeStruct((tokens // mp, d), F32)]
        + [jax.ShapeDtypeStruct((tokens // mp, d), BF16)] * (mp - 1),
        compiler_params=params(16),
        cost_estimate=cost(2 * tokens * d * width * len(grads), tokens * d * 6),
    )(sc, *grads, w)
    return outs


MESH = pl.DeviceIdType.MESH


def all_sum_kernel(plan, nbits, n, *refs):
    ins, outs = refs[: n + 1], refs[n + 1 : 2 * n + 2]
    got = refs[2 * n + 2 : 2 * n + 3 + len(plan)]
    send_sem, recv_sem = refs[2 * n + 3 + len(plan) :]
    me, core = lax.axis_index("batch"), lax.axis_index("mp")
    bit = [(me // (1 << b)) % 2 for b in range(nbits)]
    partner = [(me + (1 << b) * (1 - 2 * bit[b]), core) for b in range(nbits)]
    barrier = pltpu.get_barrier_semaphore()
    for b in range(nbits):
        pl.semaphore_signal(barrier, inc=1, device_id=partner[b], device_id_type=MESH)
    pl.semaphore_wait(barrier, nbits)

    def send(c, s, b, src, dst):
        copy = pltpu.make_async_remote_copy(
            src_ref=src,
            dst_ref=dst,
            send_sem=send_sem.at[c, s],
            recv_sem=recv_sem.at[c, s],
            device_id=partner[b],
            device_id_type=MESH,
        )
        copy.start()
        copies[c].append(copy)

    def rows(off, count):
        return pl.ds(pl.multiple_of(off, 16), count)

    copies = [[] for _ in range(len(plan) + 1)]
    spans = [[(first, count)] for _, first, count, _ in plan]
    slots = [[] for _ in plan]

    def held(c, s, b):
        a, first, count, _ = plan[c]
        half = count >> (s + 1)
        base = first if s == 0 else slots[c][s - 1]
        ref = ins[a] if s == 0 else got[c]
        return ref, base + (1 - bit[b]) * half, base + bit[b] * half, half

    def begin(c, s):
        a, first, count, order = plan[c]
        if s < nbits:
            b = order[s]
            ref, gives, _, half = held(c, s, b)
            slots[c].append(count - (count >> s))
            off = spans[c][s][0]
            spans[c].append((off + bit[b] * half, half))
            send(c, s, b, ref.at[rows(gives, half), :], got[c].at[pl.ds(slots[c][s], half), :])
        else:
            j = 2 * nbits - 1 - s
            block = outs[a].at[rows(*spans[c][j + 1]), :]
            send(c, s, order[j], block, block)

    def finish(c, s):
        copies[c][s].wait_recv()
        if s < nbits:
            a, _, _, order = plan[c]
            ref, _, stays, half = held(c, s, order[s])
            came = pl.ds(slots[c][s], half)
            total = ref[rows(stays, half), :].astype(F32) + got[c][came, :].astype(F32)
            if s < nbits - 1:
                got[c][came, :] = total.astype(BF16)
            else:
                outs[a][rows(*spans[c][s + 1]), :] = total.astype(BF16)

    last = len(plan)
    size = ins[n].shape[0]
    outs[n][...] = ins[n][...]
    for s in range(2 * nbits + 1):
        if 1 <= s <= nbits:
            copies[last][s - 1].wait()
            outs[n][...] = (
                outs[n][...].astype(F32) + got[last][(s - 1) * size : s * size, :].astype(F32)
            ).astype(BF16)
        if s < nbits:
            send(last, s, s, outs[n], got[last].at[pl.ds(s * size, size), :])
        for c in range(len(plan)):
            if s >= 1:
                finish(c, s - 1)
            if s < 2 * nbits:
                begin(c, s)
    for c in range(len(plan)):
        for copy in copies[c]:
            copy.wait_send()


def all_sum(arrays, splits, small, devices):
    nbits = devices.bit_length() - 1
    if devices != 1 << nbits or nbits < 3:
        return [lax.psum(a, "batch") for a in (*arrays, small)]
    x_y, y_x = tuple(range(nbits)), (1, 0, *range(2, nbits))
    far = (*range(2, nbits), 0, 1)
    flat = [a.reshape(-1, a.shape[-1]) for a in arrays]
    plan, used = [], []
    for a, parts in zip(flat, splits):
        count = a.shape[0] // parts
        if a.shape[0] % parts == 0 and count % (16 * devices) == 0:
            for p in range(parts):
                order = (x_y, y_x, far)[len(plan) % 3]
                plan.append((len(used), p * count, count, order))
            used.append(a)
        else:
            used.append(None)
    keep = [i for i, a in enumerate(used) if a is not None]
    plan = [(keep.index(i), *rest) for i, *rest in plan]
    small = jnp.pad(small, ((0, 16 - small.shape[0]), (0, 0)))
    operands = [used[i] for i in keep] + [small]
    vmem = pl.BlockSpec(memory_space=pltpu.VMEM)
    sums = pl.pallas_call(
        functools.partial(all_sum_kernel, plan, nbits, len(keep)),
        in_specs=[vmem] * len(operands),
        out_specs=[vmem] * len(operands),
        out_shape=[jax.ShapeDtypeStruct(a.shape, a.dtype) for a in operands],
        scratch_shapes=[pltpu.VMEM((rows, operands[i].shape[1]), BF16) for i, _, rows, _ in plan]
        + [pltpu.VMEM((16 * nbits, small.shape[1]), BF16)]
        + [pltpu.SemaphoreType.DMA((len(plan) + 1, 2 * nbits))] * 2,
        compiler_params=pltpu.CompilerParams(
            collective_id=7, has_side_effects=True, vmem_limit_bytes=20 << 20
        ),
    )(*operands)
    outs = [
        sums[keep.index(i)].reshape(a.shape) if i in keep else lax.psum(a, "batch")
        for i, a in enumerate(arrays)
    ]
    return outs + [sums[-1]]


def across(r, shift, devices):
    return [(i, i ^ (r << shift)) for i in range(devices)]


def cut(blocks, shift, bits, me):
    place = (me >> shift) % (1 << bits)
    return [lax.dynamic_index_in_dim(blocks, place ^ r, 0, keepdims=False) for r in range(1 << bits)]


def scatter_step(blocks, shift, devices):
    return blocks[:1] + [lax.ppermute(b, "batch", across(r, shift, devices)) for r, b in enumerate(blocks) if r]


def add_up(blocks):
    total = blocks[0].astype(F32)
    for b in blocks[1:]:
        total += b.astype(F32)
    return total.astype(BF16)


def gather_step(block, shift, bits, devices):
    return [block] + [lax.ppermute(block, "batch", across(r, shift, devices)) for r in range(1, 1 << bits)]


def in_order(pieces, place):
    return jnp.stack(
        [lax.select_n(place ^ c, *pieces) if len(pieces) > 1 else pieces[0] for c in range(len(pieces))]
    )


def lay_kernel(n, rows, sc, *refs):
    pieces, outs = refs[:n], refs[n:]
    c = pl.program_id(0)
    for r in range(n):

        @pl.when((sc[0] ^ c) == r)
        def _():
            at = 0
            for out, count in zip(outs, rows):
                out[...] = pieces[r][:, at : at + count, :].astype(F32).reshape(out.shape)
                at += count


def lay_out(pieces, place, shapes, rows):
    n = len(pieces)
    d = pieces[0].shape[-1]
    if any(count % 16 for count in rows):
        blocks = in_order(pieces, place)
        flat = blocks.reshape(-1, *blocks.shape[2:]).astype(F32)
        at, outs = 0, []
        for shape, count in zip(shapes, rows):
            outs.append(flat[:, at : at + count].reshape(shape))
            at += count
        return outs
    return pl.pallas_call(
        functools.partial(lay_kernel, n, rows),
        grid_spec=pltpu.PrefetchScalarGridSpec(
            num_scalar_prefetch=1,
            grid=(n,),
            in_specs=[whole(p) for p in pieces],
            out_specs=[pl.BlockSpec((s[0] // n, d), lambda i, sc: (i, 0)) for s in shapes],
        ),
        out_shape=[jax.ShapeDtypeStruct(s, F32) for s in shapes],
        compiler_params=params(14),
        cost_estimate=cost(0, sum(s[0] * d * 6 for s in shapes)),
    )(place.reshape(1).astype(jnp.int32), *pieces)


def shards(
    block_input_slots,
    memory,
    target_sentence_lengths,
    source_lengths,
    self_qkv,
    self_out,
    cross_query,
    cross_kv,
    cross_out,
    up_proj,
    down_proj,
    norm_gains,
    norm_biases,
    cotangent,
    mp,
    devices,
):
    tokens, d = block_input_slots.shape
    mem_tokens = memory.shape[0]
    share = cotangent.shape[0]
    mem_share = mem_tokens // mp
    width = self_qkv.shape[2]
    me = lax.axis_index("mp")
    bt = min(256, share)
    bq = min(256, share)
    bk = min(256, mem_tokens)

    def spread(own):
        return [own] + [
            lax.ppermute(own, "mp", [(i, (i + r) % mp) for i in range(mp)]) for r in range(1, mp)
        ]

    def exchange(pieces):
        got = [pieces[0]] + [None] * (mp - 1)
        for r in range(1, mp):
            got[mp - r] = lax.ppermute(pieces[r], "mp", [(i, (i - r) % mp) for i in range(mp)])
        return got

    wo, cq, co = spread(self_out), spread(cross_query), spread(cross_out)
    up, down = spread(up_proj), spread(down_proj)
    gain, shift = norm_gains.T, norm_biases.T

    t_len = target_sentence_lengths.reshape(-1)
    s_len = source_lengths.reshape(-1)
    t_end, s_end = jnp.cumsum(t_len), jnp.cumsum(s_len)
    t_start, s_start = t_end - t_len, s_end - s_len
    first = ((me - jnp.arange(mp)) % mp) * share
    place = (first[:, None] + jnp.arange(share)[None, :]).reshape(-1).astype(jnp.int32)
    begun = place[:, None] >= t_start[None, :]
    self_lo = jnp.max(jnp.where(begun, t_start[None, :], 0), axis=1)
    self_hi = place + 1
    cross_lo = jnp.max(jnp.where(begun, s_start[None, :], 0), axis=1)
    cross_hi = jnp.max(jnp.where(begun, s_end[None, :], 0), axis=1)
    nblk = tokens // bq
    q_block = place.reshape(nblk, bq)[:, 0] // bq

    def table(lo, hi):
        return jnp.concatenate(
            [lo.reshape(nblk, bq)[:, 0] // bk, (hi.reshape(nblk, bq)[:, -1] + bk - 1) // bk, q_block]
        ).astype(jnp.int32)

    self_table, cross_table = table(self_lo, self_hi), table(cross_lo, cross_hi)
    as_row = lambda v: v.reshape(1, tokens).astype(jnp.int32)
    self_lo, self_hi, cross_lo, cross_hi = map(as_row, (self_lo, self_hi, cross_lo, cross_hi))

    *proj, self_kt, self_vt = project(block_input_slots, self_qkv, (1, 2), min(512, mem_tokens))
    *pair, cross_kt, cross_vt = project(memory, cross_kv, (0, 1), min(512, mem_tokens))
    ctx_parts, self_lse = attend(
        self_table, proj[:1], proj[1], self_vt, self_lo, self_hi, mp, bq, bk
    )
    ctx = exchange(ctx_parts)
    me_row = me.reshape(1).astype(jnp.int32)
    n1, xhat1, rstd1, qc = post_self(me_row, block_input_slots, ctx, wo, cq, gain, shift, share, bt)
    qc_parts = exchange(qc)
    cctx_parts, cross_lse = attend(
        cross_table, qc_parts, pair[0], cross_vt, cross_lo, cross_hi, mp, bq, bk
    )
    cctx = exchange(cctx_parts)
    layer_output, da2, n2, e3, e2, dcctx, hid, dpre, small23 = middle(
        cctx, n1, cotangent, co, up, down, gain, shift, min(512, share)
    )
    dcctx_parts = exchange(dcctx)

    def grads(lefts, rights):
        return [mm(a, b, TN).astype(BF16) for a, b in zip(lefts, rights)]

    def collect(pieces):
        got = exchange(pieces)
        total = got[0].astype(F32)
        for g in got[1:]:
            total += g.astype(F32)
        return total

    early = [
        collect(grads(dpre, [n2] * mp)).astype(BF16),
        collect(grads(hid, [e3] * mp)).astype(BF16),
        collect(grads(cctx, [e2] * mp)).astype(BF16),
    ]
    row = lax.axis_index("batch")
    far = devices.bit_length() - 3
    one = early[0].reshape(2, 2, 1 << far, -1, d)
    two = jnp.concatenate([g.reshape(devices, -1, d) for g in early[1:]], axis=1)
    two = two.reshape(2, 2, 1 << far, -1, d)
    dcctx_parts, one, two = lax.optimization_barrier((dcctx_parts, cut(one, 0, 1, row), cut(two, 1, 1, row)))
    one, two = scatter_step(one, 0, devices), scatter_step(two, 1, devices)
    dqc_parts, dkc, dvc = attend_back(
        cross_table, qc_parts, dcctx_parts, cctx_parts, pair[0], cross_kt, pair[1], cross_lo, cross_hi, cross_lse, mp, bq, bk
    )
    dqc = exchange(dqc_parts)
    dkc, one, two = lax.optimization_barrier((dkc, cut(add_up(one), 1, 1, row), cut(add_up(two), 0, 1, row)))
    one, two = scatter_step(one, 1, devices), scatter_step(two, 0, devices)
    mem_bt = min(512, mem_share)
    mem_nb = mem_share // mem_bt
    mem_blocks = ((((me - jnp.arange(mp)) % mp) * mem_nb)[:, None] + jnp.arange(mem_nb)[None, :]).reshape(-1)
    memory_parts = input_part(mem_blocks.astype(jnp.int32), [dkc, dvc], cross_kv, mp, mem_bt)
    memory_grad = collect(memory_parts)
    cross_kv_grad = [mm(memory, g, TN).astype(BF16) for g in (dkc, dvc)]
    blocks = jnp.concatenate([add_up(one), add_up(two)], axis=1)
    dqc, cross_kv_grad, memory_grad, blocks = lax.optimization_barrier(
        (dqc, cross_kv_grad, memory_grad, cut(blocks, 2, far, row))
    )
    blocks = scatter_step(blocks, 2, devices)
    da1, e1, dctx, small1 = pre_self(dqc, cq, wo, da2, xhat1, rstd1, gain, bt)
    dctx_parts = exchange(dctx)
    cross_query_grad = collect(grads([n1] * mp, dqc))
    self_out_grad = collect(grads(ctx, [e1] * mp))
    dctx_parts, block = lax.optimization_barrier((dctx_parts, add_up(blocks)))
    blocks = gather_step(block, 2, far, devices)
    (dq,), dk, dv = attend_back(
        self_table, proj[:1], dctx_parts, ctx_parts, proj[1], self_kt, proj[2], self_lo, self_hi, self_lse, mp, bq, bk
    )
    blocks = in_order(blocks, row >> 2)
    cut_at = one[0].shape[1]
    dq, one, two = lax.optimization_barrier((dq, blocks[:, :cut_at], blocks[:, cut_at:]))
    one, two = gather_step(one, 1, 1, devices), gather_step(two, 0, 1, devices)
    in_bt = min(512, share)
    in_blocks = place.reshape(-1, in_bt)[:, 0] // in_bt
    input_parts = input_part(in_blocks.astype(jnp.int32), [dq, dk, dv], self_qkv, mp, in_bt)
    input_grad = collect(input_parts) + da1
    self_qkv_grad = [mm(block_input_slots, g, TN) for g in (dq, dk, dv)]

    small = jnp.concatenate([small1[:1], small23[:2], small1[1:], small23[2:]], axis=0)
    part = d // mp
    pieces = [
        lax.dynamic_slice_in_dim(small, ((me - r) % mp) * part, part, 1).astype(BF16) for r in range(mp)
    ]
    small = collect(pieces)
    self_qkv_grad, one, two = lax.optimization_barrier(
        (self_qkv_grad, in_order(one, row // 2 % 2), in_order(two, row % 2))
    )
    one = gather_step(one.reshape(-1, *one.shape[2:]), 0, 1, devices)
    two = gather_step(two.reshape(-1, *two.shape[2:]), 1, 1, devices)
    *summed, small = all_sum(
        [
            g.astype(BF16)
            for g in (
                *self_qkv_grad,
                self_out_grad,
                cross_query_grad,
                *cross_kv_grad,
            )
        ],
        (1, 1, 1, 1, 1, 1, 1),
        small.astype(BF16),
        devices,
    )
    rows = [g.shape[0] // devices for g in early]
    (up_grad,) = lay_out(one, row % 2, [early[0].shape], rows[:1])
    down_grad, cross_out_grad = lay_out(two, row // 2 % 2, [g.shape for g in early[1:]], rows[1:])
    dwq, dwk, dwv, self_out_grad, cross_query_grad, dck, dcv = [g.astype(F32) for g in summed]
    summed = [jnp.stack([dwq, dwk, dwv]), self_out_grad, cross_query_grad, jnp.stack([dck, dcv])]
    summed += [cross_out_grad, up_grad, down_grad]
    small = small.astype(F32).T
    return (layer_output, input_grad, memory_grad, *summed, small[:, :3], small[:, 3:6])


def solution(mesh):
    mp = mesh.shape["mp"]
    rows = P("batch", None)
    both = P(("batch", "mp"), None)
    first, last, last3 = P("mp", None), P(None, "mp"), P(None, None, "mp")
    return jax.shard_map(
        functools.partial(shards, mp=mp, devices=mesh.shape["batch"]),
        mesh=mesh,
        in_specs=(rows, rows, rows, rows, last3, first, last, last3, first, first, first, P(), P(), both),
        out_specs=(both, both, both, last3, first, last, last3, first, first, first, first, first),
        check_vma=False,
    )
```

```python
import functools
import math

import jax
import jax.numpy as jnp
from jax import lax
from jax.experimental import pallas as pl
from jax.experimental.pallas import tpu as pltpu
from jax.sharding import PartitionSpec as P

DH = 64
NEG = -1e30
F32 = jnp.float32
BF16 = jnp.bfloat16
SCALE = DH**-0.5
SCALE2 = SCALE * math.log2(math.e)
NT = (((1,), (1,)), ((), ()))
NN = (((1,), (0,)), ((), ()))
TN = (((0,), (0,)), ((), ()))


def mm(a, b, dims=NN):
    return lax.dot_general(a, b, dims, preferred_element_type=F32)


def params(mib):
    return pltpu.CompilerParams(dimension_semantics=("arbitrary",), vmem_limit_bytes=mib << 20)


def cost(flops, nbytes, exps=0):
    return pl.CostEstimate(flops=int(flops), bytes_accessed=int(nbytes), transcendentals=int(exps))


def pick(i, per_part, refs):
    value = refs[0][...]
    for r in range(1, len(refs)):
        value = jnp.where(i >= r * per_part, refs[r][...], value)
    return value


def part_map(r, per_part):
    return lambda i, sc: (jnp.clip(i - r * per_part, 0, per_part - 1), 0)


def group_of(heads):
    return min(heads, 128 // DH)


def per_head(block, heads):
    many = group_of(heads)
    wide = many * DH
    head = lax.broadcasted_iota(jnp.int32, (block.shape[0], wide), 1) // DH
    parts = []
    for h in range(heads):
        cols = block[:, h // many * wide : (h // many + 1) * wide]
        parts.append(jnp.where(head == h % many, cols, jnp.zeros_like(cols)))
    return jnp.concatenate(parts, axis=0)


def attend_kernel(nblk, per_part, n_q, n_out, heads, bq, bk, sc, *refs):
    q_refs, refs = refs[:n_q], refs[n_q:]
    k_ref, vt_ref, lo_ref, hi_ref = refs[:4]
    out_refs, (lse_ref, acc_ref, q_heads, s_ref, p_ref) = refs[4 : 4 + n_out], refs[4 + n_out :]
    i = pl.program_id(0)
    q_heads[...] = per_head(pick(i, per_part, q_refs), heads)
    lo = lo_ref[...]
    hi = hi_ref[...]
    acc_ref[...] = jnp.zeros_like(acc_ref)
    place = lax.broadcasted_iota(jnp.int32, (bk, bq), 0)
    span = [slice(h * bq, (h + 1) * bq) for h in range(heads)]
    cols = [slice(h * DH, (h + 1) * DH) for h in range(heads)]
    many = group_of(heads)
    wide = [slice(h // many * many * DH, (h // many + 1) * many * DH) for h in range(heads)]

    first, end = sc[i], sc[nblk + i]

    def rows(kb):
        return pl.ds(pl.multiple_of(kb * bk, bk), bk)

    def scores(kb, h):
        s_ref[:, span[h]] = mm(k_ref[rows(kb), wide[h]], q_heads[span[h], :], NT)

    def soften(kb, h, keep, top, total):
        t = jnp.where(keep, s_ref[:, span[h]] * SCALE2, NEG)
        new_top = jnp.maximum(top, jnp.max(t, axis=0, keepdims=True))
        e = jnp.exp2(t - new_top)
        decay = jnp.exp2(top - new_top)
        p_ref[:, span[h]] = e.astype(BF16)
        return new_top, total * decay + jnp.sum(e, axis=0, keepdims=True), decay

    def gather(kb, h, decay):
        acc_ref[cols[h], :] = acc_ref[cols[h], :] * decay + mm(vt_ref[cols[h], rows(kb)], p_ref[:, span[h]])

    def stage(kb, carry):
        start = kb * bk
        keep = jnp.logical_and(place >= lo - start, place < hi - start)
        after = jnp.minimum(kb + 1, end - 1)
        new = []
        for h in range(heads):
            top, total, decay = carry[h]
            if decay is not None:
                gather(kb - 1, h, decay)
            new.append(soften(kb, h, keep, top, total))
            scores(after, h)
        return new

    for h in range(heads):
        scores(first, h)
    none = jnp.full((1, bq), NEG, F32), jnp.zeros((1, bq), F32), None
    carry = lax.fori_loop(first + 1, end, stage, stage(first, [none] * heads))
    for h in range(heads):
        gather(end - 1, h, carry[h][2])
    top = [carry[h][0] for h in range(heads)]
    total = [carry[h][1] for h in range(heads)]
    for h in range(heads):
        acc_ref[cols[h], :] = acc_ref[cols[h], :] / total[h]
        lse_ref[0, h : h + 1, :] = top[h] + jnp.log2(total[h])
    ctx = acc_ref[...].T.astype(BF16)
    for r in range(n_out):

        @pl.when(jnp.logical_and(i >= r * per_part, i < (r + 1) * per_part))
        def _():
            out_refs[r][...] = ctx


def attend(sc, q_parts, keys, values_t, lo, hi, mp, bq, bk):
    tokens, width = sum(q.shape[0] for q in q_parts), keys.shape[1]
    heads = width // DH
    nblk, per_part = tokens // bq, tokens // bq // mp
    if len(q_parts) == 1 and mp > 1:
        q_specs = [pl.BlockSpec((bq, width), lambda i, sc: (sc[2 * nblk + i], 0))]
    else:
        q_specs = [pl.BlockSpec((bq, width), part_map(r, per_part)) for r in range(mp)]
    full = lambda a: pl.BlockSpec(a.shape, lambda i, sc: (0, 0))
    row = pl.BlockSpec((1, bq), lambda i, sc: (0, i))
    outs = pl.pallas_call(
        functools.partial(attend_kernel, nblk, per_part, len(q_parts), mp, heads, bq, bk),
        grid_spec=pltpu.PrefetchScalarGridSpec(
            num_scalar_prefetch=1,
            grid=(nblk,),
            in_specs=q_specs + [full(keys), full(values_t), row, row],
            out_specs=[pl.BlockSpec((bq, width), part_map(r, per_part)) for r in range(mp)]
            + [pl.BlockSpec((1, heads, bq), lambda i, sc: (i, 0, 0))],
            scratch_shapes=[
                pltpu.VMEM((width, bq), F32),
                pltpu.VMEM((heads * bq, group_of(heads) * DH), BF16),
                pltpu.VMEM((bk, heads * bq), F32),
                pltpu.VMEM((bk, heads * bq), BF16),
            ],
        ),
        out_shape=[jax.ShapeDtypeStruct((tokens // mp, width), BF16)] * mp
        + [jax.ShapeDtypeStruct((nblk, heads, bq), F32)],
        compiler_params=params(14),
        cost_estimate=cost(4 * tokens * 512 * width, 8 * tokens * width, tokens * 512 * heads),
    )(sc, *q_parts, keys, values_t, lo, hi)
    return outs[:mp], outs[mp]


def attend_back_kernel(nblk, per_part, n_q, n_part, heads, bq, bk, sc, *refs):
    q_refs, refs = refs[:n_q], refs[n_q:]
    do_refs, refs = refs[:n_part], refs[n_part:]
    o_refs, refs = refs[:n_part], refs[n_part:]
    k_ref, kt_ref, v_ref, lo_ref, hi_ref, lse_ref = refs[:6]
    dq_refs, refs = refs[6 : 6 + n_q], refs[6 + n_q :]
    dk_ref, dv_ref, dk_acc, dv_acc, dq_acc, q_heads, do_heads = refs
    i = pl.program_id(0)

    @pl.when(i == 0)
    def _():
        dk_acc[...] = jnp.zeros_like(dk_acc)
        dv_acc[...] = jnp.zeros_like(dv_acc)

    q_heads[...] = per_head(pick(i, per_part, q_refs), heads)
    do = pick(i, per_part, do_refs)
    do_heads[...] = per_head(do, heads)
    lo = lo_ref[...]
    hi = hi_ref[...]
    span = [slice(h * bq, (h + 1) * bq) for h in range(heads)]
    cols = [slice(h * DH, (h + 1) * DH) for h in range(heads)]
    many = group_of(heads)
    wide = [slice(h // many * many * DH, (h // many + 1) * many * DH) for h in range(heads)]
    prod = (do.astype(F32) * pick(i, per_part, o_refs).astype(F32)).T
    delta = [jnp.sum(prod[cols[h], :], axis=0, keepdims=True) for h in range(heads)]
    lse = [lse_ref[0, h : h + 1, :] for h in range(heads)]
    dq_acc[...] = jnp.zeros_like(dq_acc)
    place = lax.broadcasted_iota(jnp.int32, (bk, bq), 0)

    def step(kb, carry):
        start = pl.multiple_of(kb * bk, bk)
        rows = pl.ds(start, bk)
        kt = kt_ref[:, rows]
        keep = jnp.logical_and(place >= lo - start, place < hi - start)
        groups = [(slice(h * bq, (h + many) * bq), wide[h]) for h in range(0, heads, many)]
        s = [mm(k_ref[rows, w], q_heads[g, :], NT) * SCALE2 for g, w in groups]
        dp = [mm(v_ref[rows, w], do_heads[g, :], NT) for g, w in groups]
        at = [(h // many, slice(h % many * bq, (h % many + 1) * bq)) for h in range(heads)]
        p = [jnp.where(keep, jnp.exp2(s[g][:, c] - lse[h]), 0.0) for h, (g, c) in enumerate(at)]
        ds = [(p[h] * (dp[g][:, c] - delta[h])).astype(BF16) for h, (g, c) in enumerate(at)]
        p = [p[h].astype(BF16) for h in range(heads)]
        for g, (r, w) in enumerate(groups):
            here = slice(g * many, (g + 1) * many)
            dv_acc[rows, w] += mm(jnp.concatenate(p[here], axis=1), do_heads[r, :])
            dk_acc[rows, w] += mm(jnp.concatenate(ds[here], axis=1), q_heads[r, :])
        for h in range(heads):
            dq_acc[cols[h], :] += mm(kt[cols[h], :], ds[h])
        return carry

    lax.fori_loop(sc[i], sc[nblk + i], step, 0)
    dq = (dq_acc[...] * SCALE).T.astype(BF16)
    if n_q == 1:
        dq_refs[0][...] = dq
    else:
        for r in range(n_q):

            @pl.when(jnp.logical_and(i >= r * per_part, i < (r + 1) * per_part))
            def _():
                dq_refs[r][...] = dq

    @pl.when(i == nblk - 1)
    def _():
        dk_ref[...] = (dk_acc[...] * SCALE).astype(BF16)
        dv_ref[...] = dv_acc[...].astype(BF16)


def attend_back(sc, q_parts, do_parts, o_parts, keys, keys_t, values, lo, hi, lse, mp, bq, bk):
    tokens, width = sum(q.shape[0] for q in q_parts), keys.shape[1]
    heads = width // DH
    nblk, per_part = tokens // bq, tokens // bq // mp
    parts = [pl.BlockSpec((bq, width), part_map(r, per_part)) for r in range(mp)]
    if len(q_parts) == 1 and mp > 1:
        q_specs = [pl.BlockSpec((bq, width), lambda i, sc: (sc[2 * nblk + i], 0))]
    else:
        q_specs = parts
    full = lambda a: pl.BlockSpec(a.shape, lambda i, sc: (0, 0))
    row = pl.BlockSpec((1, bq), lambda i, sc: (0, i))
    outs = pl.pallas_call(
        functools.partial(attend_back_kernel, nblk, per_part, len(q_parts), mp, heads, bq, bk),
        grid_spec=pltpu.PrefetchScalarGridSpec(
            num_scalar_prefetch=1,
            grid=(nblk,),
            in_specs=q_specs
            + parts
            + parts
            + [full(keys), full(keys_t), full(values), row, row]
            + [pl.BlockSpec((1, heads, bq), lambda i, sc: (i, 0, 0))],
            out_specs=q_specs + [full(keys), full(keys)],
            scratch_shapes=[
                pltpu.VMEM(keys.shape, F32),
                pltpu.VMEM(keys.shape, F32),
                pltpu.VMEM((width, bq), F32),
                pltpu.VMEM((heads * bq, group_of(heads) * DH), BF16),
                pltpu.VMEM((heads * bq, group_of(heads) * DH), BF16),
            ],
        ),
        out_shape=[jax.ShapeDtypeStruct(q.shape, BF16) for q in q_parts]
        + [jax.ShapeDtypeStruct(keys.shape, BF16)] * 2,
        compiler_params=params(26),
        cost_estimate=cost(10 * tokens * 512 * width, 12 * tokens * width, tokens * 512 * heads),
    )(sc, *q_parts, *do_parts, *o_parts, keys, keys_t, values, lo, hi, lse)
    return outs[: len(q_parts)], outs[-2], outs[-1]


def norm_stats(a):
    centre = a - jnp.mean(a, axis=-1, keepdims=True)
    rstd = lax.rsqrt(jnp.mean(centre * centre, axis=-1, keepdims=True) + 1e-05)
    return centre * rstd, rstd


def norm_back(dy, xhat, rstd, gain):
    t = dy * gain
    mean_t = jnp.mean(t, axis=-1, keepdims=True)
    mean_tx = jnp.mean(t * xhat, axis=-1, keepdims=True)
    return rstd * (t - mean_t - xhat * mean_tx)


def project_kernel(n, turned, x_ref, w_ref, *outs):
    x = x_ref[...]
    for c in range(n):
        y = mm(x, w_ref[c])
        outs[c][...] = y.astype(BF16)
        if c in turned:
            outs[n + turned.index(c)][...] = y.T.astype(BF16)


def project(x, w, turned, bt):
    n, d, width = w.shape
    tokens = x.shape[0]
    return pl.pallas_call(
        functools.partial(project_kernel, n, turned),
        grid=(tokens // bt,),
        in_specs=[pl.BlockSpec((bt, d), lambda i: (i, 0)), pl.BlockSpec(w.shape, lambda i: (0, 0, 0))],
        out_specs=[pl.BlockSpec((bt, width), lambda i: (i, 0))] * n
        + [pl.BlockSpec((width, bt), lambda i: (0, i))] * len(turned),
        out_shape=[jax.ShapeDtypeStruct((tokens, width), BF16)] * n
        + [jax.ShapeDtypeStruct((width, tokens), BF16)] * len(turned),
        compiler_params=params(14),
        cost_estimate=cost(2 * tokens * d * width * n, tokens * (d + 2 * n * width) * 2),
    )(x, w)


def post_self_kernel(mp, sc, *refs):
    x_ref = refs[0]
    ctx, wo, cq = refs[1 : 1 + mp], refs[1 + mp : 1 + 2 * mp], refs[1 + 2 * mp : 1 + 3 * mp]
    gain_ref, shift_ref = refs[1 + 3 * mp : 3 + 3 * mp]
    n1_ref, xhat_ref, rstd_ref = refs[3 + 3 * mp : 6 + 3 * mp]
    qc = refs[6 + 3 * mp :]
    a1 = x_ref[...].astype(F32)
    for r in range(mp):
        a1 += mm(ctx[r][...], wo[r][...])
    xhat, rstd = norm_stats(a1)
    n1 = (xhat * gain_ref[0:1, :] + shift_ref[0:1, :]).astype(BF16)
    n1_ref[...] = n1
    xhat_ref[...] = xhat
    rstd_ref[...] = rstd
    for r in range(mp):
        qc[r][...] = mm(n1, cq[r][...]).astype(BF16)


def whole(a):
    return pl.BlockSpec(a.shape, lambda i, sc: (0,) * a.ndim)


def rows_of(bt, width):
    return pl.BlockSpec((bt, width), lambda i, sc: (i, 0))


def post_self(sc, x, ctx, wo, cq, gain, shift, share, bt):
    mp, d = len(ctx), x.shape[1]
    width = ctx[0].shape[1]
    nb = share // bt
    outs = pl.pallas_call(
        functools.partial(post_self_kernel, mp),
        grid_spec=pltpu.PrefetchScalarGridSpec(
            num_scalar_prefetch=1,
            grid=(nb,),
            in_specs=[pl.BlockSpec((bt, d), lambda i, sc: (sc[0] * nb + i, 0))]
            + [rows_of(bt, width)] * mp
            + [whole(w) for w in (*wo, *cq, gain, shift)],
            out_specs=[rows_of(bt, d), rows_of(bt, d), rows_of(bt, 1)] + [rows_of(bt, width)] * mp,
        ),
        out_shape=[
            jax.ShapeDtypeStruct((share, d), BF16),
            jax.ShapeDtypeStruct((share, d), F32),
            jax.ShapeDtypeStruct((share, 1), F32),
        ]
        + [jax.ShapeDtypeStruct((share, width), BF16)] * mp,
        compiler_params=params(16),
        cost_estimate=cost(4 * share * d * d, share * d * 12),
    )(sc, x, *ctx, *wo, *cq, gain, shift)
    return outs[0], outs[1], outs[2], outs[3:]


def middle_kernel(mp, *refs):
    refs = list(refs)

    def take(n):
        got = refs[:n]
        del refs[:n]
        return got

    cctx, (n1_ref, cot_ref) = take(mp), take(2)
    co, up, down = take(mp), take(mp), take(mp)
    gain_ref, shift_ref = take(2)
    out_ref, da2_ref, n2_ref, e3_ref, e2_ref = take(5)
    dcctx, hid, dpre = take(mp), take(mp), take(mp)
    (small_ref,) = take(1)
    (slope_ref,) = take(1)
    ff = up[0].shape[0]
    i = pl.program_id(0)

    a2 = n1_ref[...].astype(F32)
    for r in range(mp):
        a2 += mm(cctx[r][...], co[r][...])
    xhat2, rstd2 = norm_stats(a2)
    n2 = (xhat2 * gain_ref[1:2, :] + shift_ref[1:2, :]).astype(BF16)
    n2_ref[...] = n2
    a3 = n2.astype(F32)
    for r in range(mp):
        u = mm(n2, up[r][...], NT)
        sg = 0.5 * jnp.tanh(0.5 * u) + 0.5
        h = u * sg
        hid[r][...] = h.astype(BF16)
        slope_ref[:, r * ff : (r + 1) * ff] = sg + h * (1.0 - sg)
        a3 += mm(hid[r][...], down[r][...])
    xhat3, rstd3 = norm_stats(a3)
    out_ref[...] = (xhat3 * gain_ref[2:3, :] + shift_ref[2:3, :]).astype(BF16)
    g = cot_ref[...].astype(F32)
    da3 = norm_back(g, xhat3, rstd3, gain_ref[2:3, :])
    e3 = da3.astype(BF16)
    e3_ref[...] = e3
    dn2 = da3
    for r in range(mp):
        dh = mm(e3, down[r][...], NT)
        dpre[r][...] = (dh * slope_ref[:, r * ff : (r + 1) * ff]).astype(BF16)
        dn2 += mm(dpre[r][...], up[r][...])
    da2 = norm_back(dn2, xhat2, rstd2, gain_ref[1:2, :])
    da2_ref[...] = da2
    e2 = da2.astype(BF16)
    e2_ref[...] = e2
    for r in range(mp):
        dcctx[r][...] = mm(e2, co[r][...], NT).astype(BF16)
    sums = jnp.concatenate(
        [
            jnp.sum(dn2 * xhat2, axis=0, keepdims=True),
            jnp.sum(g * xhat3, axis=0, keepdims=True),
            jnp.sum(dn2, axis=0, keepdims=True),
            jnp.sum(g, axis=0, keepdims=True),
        ],
        axis=0,
    )

    @pl.when(i == 0)
    def _():
        small_ref[...] = sums

    @pl.when(i > 0)
    def _():
        small_ref[...] += sums


def middle(cctx, n1, cot, co, up, down, gain, shift, bt):
    mp = len(cctx)
    share, d = n1.shape
    width = cctx[0].shape[1]
    ff = up[0].shape[0]
    row = lambda w: pl.BlockSpec((bt, w), lambda i: (i, 0))
    all_of = lambda a: pl.BlockSpec(a.shape, lambda i: (0,) * a.ndim)
    shape = lambda w, t: jax.ShapeDtypeStruct((share, w), t)
    outs = pl.pallas_call(
        functools.partial(middle_kernel, mp),
        grid=(share // bt,),
        in_specs=[row(width)] * mp + [row(d)] * 2 + [all_of(w) for w in (*co, *up, *down, gain, shift)],
        out_specs=[row(d)] * 5
        + [row(width)] * mp
        + [row(ff)] * (2 * mp)
        + [pl.BlockSpec((4, d), lambda i: (0, 0))],
        scratch_shapes=[pltpu.VMEM((bt, ff * mp), F32)],
        out_shape=[shape(d, BF16), shape(d, F32), shape(d, BF16), shape(d, BF16), shape(d, BF16)]
        + [shape(width, BF16)] * mp
        + [shape(ff, BF16)] * (2 * mp)
        + [jax.ShapeDtypeStruct((4, d), F32)],
        compiler_params=params(36),
        cost_estimate=cost(8 * share * d * ff * mp + 4 * share * d * d, share * ff * mp * 4, share * ff * mp),
    )(*cctx, n1, cot, *co, *up, *down, gain, shift)
    out, da2, n2, e3, e2 = outs[:5]
    return out, da2, n2, e3, e2, outs[5 : 5 + mp], outs[5 + mp : 5 + 2 * mp], outs[5 + 2 * mp : 5 + 3 * mp], outs[-1]


def pre_self_kernel(mp, *refs):
    dqc, cq, wo = refs[:mp], refs[mp : 2 * mp], refs[2 * mp : 3 * mp]
    da2_ref, xhat_ref, rstd_ref, gain_ref = refs[3 * mp : 3 * mp + 4]
    da1_ref, e1_ref = refs[3 * mp + 4 : 3 * mp + 6]
    dctx = refs[3 * mp + 6 : 4 * mp + 6]
    small_ref = refs[4 * mp + 6]
    i = pl.program_id(0)
    dn1 = da2_ref[...]
    for r in range(mp):
        dn1 += mm(dqc[r][...], cq[r][...], NT)
    xhat = xhat_ref[...]
    da1 = norm_back(dn1, xhat, rstd_ref[...], gain_ref[0:1, :])
    da1_ref[...] = da1
    e1 = da1.astype(BF16)
    e1_ref[...] = e1
    for r in range(mp):
        dctx[r][...] = mm(e1, wo[r][...], NT).astype(BF16)
    sums = jnp.concatenate(
        [jnp.sum(dn1 * xhat, axis=0, keepdims=True), jnp.sum(dn1, axis=0, keepdims=True)], axis=0
    )

    @pl.when(i == 0)
    def _():
        small_ref[...] = sums

    @pl.when(i > 0)
    def _():
        small_ref[...] += sums


def pre_self(dqc, cq, wo, da2, xhat, rstd, gain, bt):
    mp = len(dqc)
    share, d = da2.shape
    width = dqc[0].shape[1]
    row = lambda w: pl.BlockSpec((bt, w), lambda i: (i, 0))
    all_of = lambda a: pl.BlockSpec(a.shape, lambda i: (0,) * a.ndim)
    outs = pl.pallas_call(
        functools.partial(pre_self_kernel, mp),
        grid=(share // bt,),
        in_specs=[row(width)] * mp
        + [all_of(w) for w in (*cq, *wo)]
        + [row(d), row(d), row(1), all_of(gain)],
        out_specs=[row(d), row(d)] + [row(width)] * mp + [pl.BlockSpec((2, d), lambda i: (0, 0))],
        out_shape=[jax.ShapeDtypeStruct((share, d), F32), jax.ShapeDtypeStruct((share, d), BF16)]
        + [jax.ShapeDtypeStruct((share, width), BF16)] * mp
        + [jax.ShapeDtypeStruct((2, d), F32)],
        compiler_params=params(16),
        cost_estimate=cost(1, 1),
    )(*dqc, *cq, *wo, da2, xhat, rstd, gain)
    return outs[0], outs[1], outs[2 : 2 + mp], outs[-1]


def part_kernel(n_in, n_out, per_part, sc, *refs):
    grads, w_ref, outs = refs[:n_in], refs[n_in], refs[n_in + 1 :]
    i = pl.program_id(0)
    total = mm(jnp.concatenate([g[...] for g in grads], axis=1), w_ref[...])
    for r in range(n_out):

        @pl.when(jnp.logical_and(i >= r * per_part, i < (r + 1) * per_part))
        def _():
            outs[r][...] = total.astype(outs[r].dtype)


def input_part(sc, grads, w, mp, bt):
    tokens, width = grads[0].shape
    d = w.shape[1]
    w = w.swapaxes(1, 2).reshape(-1, d)
    nblk = tokens // bt
    per_part = nblk // mp
    outs = pl.pallas_call(
        functools.partial(part_kernel, len(grads), mp, per_part),
        grid_spec=pltpu.PrefetchScalarGridSpec(
            num_scalar_prefetch=1,
            grid=(nblk,),
            in_specs=[pl.BlockSpec((bt, width), lambda i, sc: (sc[i], 0))] * len(grads) + [whole(w)],
            out_specs=[pl.BlockSpec((bt, d), part_map(r, per_part)) for r in range(mp)],
        ),
        out_shape=[jax.ShapeDtypeStruct((tokens // mp, d), F32)]
        + [jax.ShapeDtypeStruct((tokens // mp, d), BF16)] * (mp - 1),
        compiler_params=params(16),
        cost_estimate=cost(1, 1),
    )(sc, *grads, w)
    return outs


MESH = pl.DeviceIdType.MESH


def all_sum_kernel(plan, nbits, n, *refs):
    ins, outs = refs[: n + 1], refs[n + 1 : 2 * n + 2]
    got = refs[2 * n + 2 : 2 * n + 3 + len(plan)]
    send_sem, recv_sem = refs[2 * n + 3 + len(plan) :]
    me, core = lax.axis_index("batch"), lax.axis_index("mp")
    bit = [(me // (1 << b)) % 2 for b in range(nbits)]
    partner = [(me + (1 << b) * (1 - 2 * bit[b]), core) for b in range(nbits)]
    barrier = pltpu.get_barrier_semaphore()
    for b in range(nbits):
        pl.semaphore_signal(barrier, inc=1, device_id=partner[b], device_id_type=MESH)
    pl.semaphore_wait(barrier, nbits)

    def send(c, s, b, src, dst):
        copy = pltpu.make_async_remote_copy(
            src_ref=src,
            dst_ref=dst,
            send_sem=send_sem.at[c, s],
            recv_sem=recv_sem.at[c, s],
            device_id=partner[b],
            device_id_type=MESH,
        )
        copy.start()
        copies[c][s] = copy

    def rows(off, count):
        return pl.ds(pl.multiple_of(off, 16), count)

    copies = [{} for _ in range(len(plan) + 1)]
    spans = []
    for _, count, order, _ in plan:
        span = [(0, count)]
        for b in order:
            off, size = span[-1]
            span.append((off + bit[b] * (size // 2), size // 2))
        spans.append(span)

    def held(c, s, b):
        a, count, _, _ = plan[c]
        half = count >> (s + 1)
        base = count - (count >> (s - 1)) if s else 0
        return (got[c] if s else ins[a]), base + (1 - bit[b]) * half, base + bit[b] * half, half

    def begin(c, s):
        a, count, order, _ = plan[c]
        if s < nbits:
            b = order[s]
            ref, gives, _, half = held(c, s, b)
            send(c, s, b, ref.at[rows(gives, half), :], got[c].at[pl.ds(count - (count >> s), half), :])
        else:
            j = 2 * nbits - 1 - s
            block = outs[a].at[rows(*spans[c][j + 1]), :]
            send(c, s, order[j], block, block)

    def finish(c, s):
        copies[c][s].wait_recv()
        if s < nbits:
            a, count, order, _ = plan[c]
            ref, _, stays, half = held(c, s, order[s])
            came = pl.ds(count - (count >> s), half)
            total = ref[rows(stays, half), :].astype(F32) + got[c][came, :].astype(F32)
            if s < nbits - 1:
                got[c][came, :] = total.astype(BF16)
            else:
                outs[a][rows(*spans[c][s + 1]), :] = total.astype(BF16)

    last = len(plan)
    size = ins[n].shape[0]
    outs[n][...] = ins[n][...]
    for c, (a, _, _, done) in enumerate(plan):
        if done:
            outs[a][rows(*spans[c][nbits]), :] = ins[a][...]
    for t in range(2 * nbits + 1):
        for c, (_, _, _, done) in enumerate(plan):
            s = t + done
            if done < s < 2 * nbits or (s == 2 * nbits and not done):
                finish(c, s - 1)
            if s < 2 * nbits:
                begin(c, s)
        if 1 <= t <= nbits:
            copies[last][t - 1].wait()
            outs[n][...] = (
                outs[n][...].astype(F32) + got[last][(t - 1) * size : t * size, :].astype(F32)
            ).astype(BF16)
        if t < nbits:
            send(last, t, t, outs[n], got[last].at[pl.ds(t * size, size), :])
    for c, (_, _, _, done) in enumerate(plan):
        if done:
            finish(c, 2 * nbits - 1)
        for copy in copies[c].values():
            copy.wait_send()


def all_sum(arrays, blocks, small, devices):
    nbits = devices.bit_length() - 1
    line = tuple(range(nbits - 1, 1, -1))
    flat = [a.reshape(-1, a.shape[-1]) for a in arrays]
    fits = [a.shape[0] % (16 * devices) == 0 for a in flat]
    plan, operands, shapes = [], [], []
    for a, first in blocks:
        plan.append((len(operands), a.shape[0] * devices, (*first, *line), nbits))
        operands.append(a)
        shapes.append((a.shape[0] * devices, a.shape[1]))
    for a, fit in zip(flat, fits):
        if fit:
            first = ((0, 1), (1, 0))[len(plan) % 2]
            plan.append((len(operands), a.shape[0], (*first, *range(2, nbits)), 0))
            operands.append(a)
            shapes.append(a.shape)
    small = jnp.pad(small, ((0, 16 - small.shape[0]), (0, 0)))
    operands.append(small)
    shapes.append(small.shape)
    vmem = pl.BlockSpec(memory_space=pltpu.VMEM)
    sums = pl.pallas_call(
        functools.partial(all_sum_kernel, plan, nbits, len(plan)),
        in_specs=[vmem] * len(operands),
        out_specs=[vmem] * len(operands),
        out_shape=[jax.ShapeDtypeStruct(shape, BF16) for shape in shapes],
        scratch_shapes=[pltpu.VMEM((16 if done else rows, operands[i].shape[1]), BF16) for i, rows, _, done in plan]
        + [pltpu.VMEM((16 * nbits, small.shape[1]), BF16)]
        + [pltpu.SemaphoreType.DMA((len(plan) + 1, 2 * nbits))] * 2,
        compiler_params=pltpu.CompilerParams(
            collective_id=7, has_side_effects=True, vmem_limit_bytes=28 << 20
        ),
    )(*operands)
    whole_ones = sums[: len(blocks)]
    rest = iter(sums[len(blocks) : -1])
    outs = [next(rest).reshape(a.shape) if fit else lax.psum(a, "batch") for a, fit in zip(arrays, fits)]
    return outs, whole_ones, sums[-1]


def across(r, shift, devices):
    return [(i, i ^ (r << shift)) for i in range(devices)]


def cut(blocks, shift, bits, me):
    place = (me >> shift) % (1 << bits)
    return [lax.dynamic_index_in_dim(blocks, place ^ r, 0, keepdims=False) for r in range(1 << bits)]


def scatter_step(blocks, shift, devices):
    return blocks[:1] + [lax.ppermute(b, "batch", across(r, shift, devices)) for r, b in enumerate(blocks) if r]


def add_up(blocks):
    total = blocks[0].astype(F32)
    for b in blocks[1:]:
        total += b.astype(F32)
    return total.astype(BF16)


def shards(
    block_input_slots,
    memory,
    target_sentence_lengths,
    source_lengths,
    self_qkv,
    self_out,
    cross_query,
    cross_kv,
    cross_out,
    up_proj,
    down_proj,
    norm_gains,
    norm_biases,
    cotangent,
    mp,
    devices,
):
    tokens, d = block_input_slots.shape
    mem_tokens = memory.shape[0]
    share = cotangent.shape[0]
    mem_share = mem_tokens // mp
    width = self_qkv.shape[2]
    me = lax.axis_index("mp")
    bt = min(256, share)
    bq = min(256, share)
    bk = min(256, mem_tokens)

    def spread(own):
        return [own] + [
            lax.ppermute(own, "mp", [(i, (i + r) % mp) for i in range(mp)]) for r in range(1, mp)
        ]

    def exchange(pieces):
        got = [pieces[0]] + [None] * (mp - 1)
        for r in range(1, mp):
            got[mp - r] = lax.ppermute(pieces[r], "mp", [(i, (i - r) % mp) for i in range(mp)])
        return got

    wo, cq, co = spread(self_out), spread(cross_query), spread(cross_out)
    up, down = spread(up_proj), spread(down_proj)
    gain, shift = norm_gains.T, norm_biases.T

    t_len = target_sentence_lengths.reshape(-1)
    s_len = source_lengths.reshape(-1)
    t_end, s_end = jnp.cumsum(t_len), jnp.cumsum(s_len)
    t_start, s_start = t_end - t_len, s_end - s_len
    first = ((me - jnp.arange(mp)) % mp) * share
    place = (first[:, None] + jnp.arange(share)[None, :]).reshape(-1).astype(jnp.int32)
    begun = place[:, None] >= t_start[None, :]
    self_lo = jnp.max(jnp.where(begun, t_start[None, :], 0), axis=1)
    self_hi = place + 1
    cross_lo = jnp.max(jnp.where(begun, s_start[None, :], 0), axis=1)
    cross_hi = jnp.max(jnp.where(begun, s_end[None, :], 0), axis=1)
    nblk = tokens // bq
    q_block = place.reshape(nblk, bq)[:, 0] // bq

    def table(lo, hi):
        return jnp.concatenate(
            [lo.reshape(nblk, bq)[:, 0] // bk, (hi.reshape(nblk, bq)[:, -1] + bk - 1) // bk, q_block]
        ).astype(jnp.int32)

    self_table, cross_table = table(self_lo, self_hi), table(cross_lo, cross_hi)
    as_row = lambda v: v.reshape(1, tokens).astype(jnp.int32)
    self_lo, self_hi, cross_lo, cross_hi = map(as_row, (self_lo, self_hi, cross_lo, cross_hi))

    *proj, self_kt, self_vt = project(block_input_slots, self_qkv, (1, 2), min(512, mem_tokens))
    *pair, cross_kt, cross_vt = project(memory, cross_kv, (0, 1), min(512, mem_tokens))
    ctx_parts, self_lse = attend(
        self_table, proj[:1], proj[1], self_vt, self_lo, self_hi, mp, bq, bk
    )
    ctx = exchange(ctx_parts)
    me_row = me.reshape(1).astype(jnp.int32)
    n1, xhat1, rstd1, qc = post_self(me_row, block_input_slots, ctx, wo, cq, gain, shift, share, bt)
    qc_parts = exchange(qc)
    cctx_parts, cross_lse = attend(
        cross_table, qc_parts, pair[0], cross_vt, cross_lo, cross_hi, mp, bq, bk
    )
    cctx = exchange(cctx_parts)
    layer_output, da2, n2, e3, e2, dcctx, hid, dpre, small23 = middle(
        cctx, n1, cotangent, co, up, down, gain, shift, min(512, share)
    )
    dcctx_parts = exchange(dcctx)

    def grads(lefts, rights):
        return [mm(a, b, TN).astype(BF16) for a, b in zip(lefts, rights)]

    def collect(pieces):
        got = exchange(pieces)
        total = got[0].astype(F32)
        for g in got[1:]:
            total += g.astype(F32)
        return total

    early = [
        collect(grads(dpre, [n2] * mp)).astype(BF16),
        collect(grads(hid, [e3] * mp)).astype(BF16),
        collect(grads(cctx, [e2] * mp)).astype(BF16),
    ]
    hidden = all(g.shape[0] % (16 * devices) == 0 for g in early)
    row = lax.axis_index("batch")
    far = devices.bit_length() - 3
    if hidden:
        one = early[0].reshape(4, 1 << far, -1, d)
        two = jnp.concatenate([g.reshape(4, 1 << far, -1, d) for g in early[1:]], axis=2)
        here = row % 4
        mirrored = here % 2 * 2 + here // 2
        blocks = [
            jnp.concatenate(
                [
                    lax.dynamic_index_in_dim(one, mirrored ^ (0, 2, 1, 3)[r], 0, keepdims=False),
                    lax.dynamic_index_in_dim(two, here ^ r, 0, keepdims=False),
                ],
                axis=1,
            )
            for r in range(4)
        ]
        dcctx_parts, blocks = lax.optimization_barrier((dcctx_parts, blocks))
        blocks = scatter_step(blocks, 0, devices)
    dqc_parts, dkc, dvc = attend_back(
        cross_table, qc_parts, dcctx_parts, cctx_parts, pair[0], cross_kt, pair[1], cross_lo, cross_hi, cross_lse, mp, bq, bk
    )
    dqc = exchange(dqc_parts)
    if hidden:
        dqc, block = lax.optimization_barrier((dqc, add_up(blocks)))
    da1, e1, dctx, small1 = pre_self(dqc, cq, wo, da2, xhat1, rstd1, gain, bt)
    dctx_parts = exchange(dctx)
    mem_bt = min(512, mem_share)
    mem_nb = mem_share // mem_bt
    mem_blocks = ((((me - jnp.arange(mp)) % mp) * mem_nb)[:, None] + jnp.arange(mem_nb)[None, :]).reshape(-1)
    memory_parts = input_part(mem_blocks.astype(jnp.int32), [dkc, dvc], cross_kv, mp, mem_bt)
    memory_grad = collect(memory_parts)
    cross_kv_grad = [mm(memory, g, TN) for g in (dkc, dvc)]
    cross_query_grad = collect(grads([n1] * mp, dqc))
    self_out_grad = collect(grads(ctx, [e1] * mp))
    if hidden:
        dctx_parts, blocks = lax.optimization_barrier((dctx_parts, cut(block, 2, far, row)))
        blocks = scatter_step(blocks, 2, devices)
    (dq,), dk, dv = attend_back(
        self_table, proj[:1], dctx_parts, ctx_parts, proj[1], self_kt, proj[2], self_lo, self_hi, self_lse, mp, bq, bk
    )
    in_bt = min(512, share)
    in_blocks = place.reshape(-1, in_bt)[:, 0] // in_bt
    input_parts = input_part(in_blocks.astype(jnp.int32), [dq, dk, dv], self_qkv, mp, in_bt)
    input_grad = collect(input_parts) + da1
    self_qkv_grad = [mm(block_input_slots, g, TN) for g in (dq, dk, dv)]

    small = jnp.concatenate([small1[:1], small23[:2], small1[1:], small23[2:]], axis=0)
    part = d // mp
    pieces = [
        lax.dynamic_slice_in_dim(small, ((me - r) % mp) * part, part, 1).astype(BF16) for r in range(mp)
    ]
    small = collect(pieces)
    late = [*self_qkv_grad, self_out_grad, cross_query_grad, *cross_kv_grad]
    late = [g.astype(BF16) for g in late]
    if hidden:
        block = add_up(blocks)
        count = early[0].shape[0] // devices
        summed, (up_grad, rest), small = all_sum(
            late, [(block[:count], (0, 1)), (block[count:], (1, 0))], small.astype(BF16), devices
        )
        up_grad = up_grad.astype(F32)
        rest = rest.reshape(devices, -1, d)
        count = early[1].shape[0] // devices
        down_grad = rest[:, :count].reshape(early[1].shape).astype(F32)
        cross_out_grad = rest[:, count:].reshape(early[2].shape).astype(F32)
    else:
        summed, _, small = all_sum(late + early, [], small.astype(BF16), devices)
        *summed, up_grad, down_grad, cross_out_grad = [g.astype(F32) for g in summed]
    dwq, dwk, dwv, self_out_grad, cross_query_grad, dck, dcv = [g.astype(F32) for g in summed]
    summed = [jnp.stack([dwq, dwk, dwv]), self_out_grad, cross_query_grad, jnp.stack([dck, dcv])]
    summed += [cross_out_grad, up_grad, down_grad]
    small = small.astype(F32).T
    return (layer_output, input_grad, memory_grad, *summed, small[:, :3], small[:, 3:6])


def solution(mesh):
    mp = mesh.shape["mp"]
    rows = P("batch", None)
    both = P(("batch", "mp"), None)
    first, last, last3 = P("mp", None), P(None, "mp"), P(None, None, "mp")
    return jax.shard_map(
        functools.partial(shards, mp=mp, devices=mesh.shape["batch"]),
        mesh=mesh,
        in_specs=(rows, rows, rows, rows, last3, first, last, last3, first, first, first, P(), P(), both),
        out_specs=(both, both, both, last3, first, last, last3, first, first, first, first, first),
        check_vma=False,
    )
```

```python
import functools
import math

import jax
import jax.numpy as jnp
from jax import lax
from jax.experimental import pallas as pl
from jax.experimental.pallas import tpu as pltpu
from jax.sharding import PartitionSpec as P

DH = 64
NEG = -1e30
F32 = jnp.float32
BF16 = jnp.bfloat16
SCALE = DH**-0.5
SCALE2 = SCALE * math.log2(math.e)
NT = (((1,), (1,)), ((), ()))
NN = (((1,), (0,)), ((), ()))
TN = (((0,), (0,)), ((), ()))


def mm(a, b, dims=NN):
    return lax.dot_general(a, b, dims, preferred_element_type=F32)


def params(mib):
    return pltpu.CompilerParams(dimension_semantics=("arbitrary",), vmem_limit_bytes=mib << 20)


def cost(flops, nbytes, exps=0):
    return pl.CostEstimate(flops=int(flops), bytes_accessed=int(nbytes), transcendentals=int(exps))


def pick(i, per_part, refs):
    value = refs[0][...]
    for r in range(1, len(refs)):
        value = jnp.where(i >= r * per_part, refs[r][...], value)
    return value


def part_map(r, per_part):
    return lambda i, sc: (jnp.clip(i - r * per_part, 0, per_part - 1), 0)


def group_of(heads):
    return min(heads, 128 // DH)


def per_head(block, heads):
    many = group_of(heads)
    wide = many * DH
    head = lax.broadcasted_iota(jnp.int32, (block.shape[0], wide), 1) // DH
    parts = []
    for h in range(heads):
        cols = block[:, h // many * wide : (h // many + 1) * wide]
        parts.append(jnp.where(head == h % many, cols, jnp.zeros_like(cols)))
    return jnp.concatenate(parts, axis=0)


def attend_kernel(nblk, per_part, n_q, n_out, heads, bq, bk, sc, *refs):
    q_refs, refs = refs[:n_q], refs[n_q:]
    k_ref, vt_ref, lo_ref, hi_ref = refs[:4]
    out_refs, (lse_ref, acc_ref, q_heads, s_ref, p_ref) = refs[4 : 4 + n_out], refs[4 + n_out :]
    i = pl.program_id(0)
    q_heads[...] = per_head(pick(i, per_part, q_refs), heads)
    lo = lo_ref[...]
    hi = hi_ref[...]
    acc_ref[...] = jnp.zeros_like(acc_ref)
    place = lax.broadcasted_iota(jnp.int32, (bk, bq), 0)
    span = [slice(h * bq, (h + 1) * bq) for h in range(heads)]
    cols = [slice(h * DH, (h + 1) * DH) for h in range(heads)]
    many = group_of(heads)
    wide = [slice(h // many * many * DH, (h // many + 1) * many * DH) for h in range(heads)]

    first, end = sc[i], sc[nblk + i]

    def rows(kb):
        return pl.ds(pl.multiple_of(kb * bk, bk), bk)

    def scores(kb, h):
        s_ref[:, span[h]] = mm(k_ref[rows(kb), wide[h]], q_heads[span[h], :], NT)

    def soften(kb, h, keep, top, total):
        t = jnp.where(keep, s_ref[:, span[h]] * SCALE2, NEG)
        new_top = jnp.maximum(top, jnp.max(t, axis=0, keepdims=True))
        e = jnp.exp2(t - new_top)
        decay = jnp.exp2(top - new_top)
        p_ref[:, span[h]] = e.astype(BF16)
        return new_top, total * decay + jnp.sum(e, axis=0, keepdims=True), decay

    def gather(kb, h, decay):
        acc_ref[cols[h], :] = acc_ref[cols[h], :] * decay + mm(vt_ref[cols[h], rows(kb)], p_ref[:, span[h]])

    def stage(kb, carry):
        start = kb * bk
        keep = jnp.logical_and(place >= lo - start, place < hi - start)
        after = jnp.minimum(kb + 1, end - 1)
        new = []
        for h in range(heads):
            top, total, decay = carry[h]
            if decay is not None:
                gather(kb - 1, h, decay)
            new.append(soften(kb, h, keep, top, total))
            scores(after, h)
        return new

    for h in range(heads):
        scores(first, h)
    none = jnp.full((1, bq), NEG, F32), jnp.zeros((1, bq), F32), None
    carry = lax.fori_loop(first + 1, end, stage, stage(first, [none] * heads))
    for h in range(heads):
        gather(end - 1, h, carry[h][2])
    top = [carry[h][0] for h in range(heads)]
    total = [carry[h][1] for h in range(heads)]
    for h in range(heads):
        acc_ref[cols[h], :] = acc_ref[cols[h], :] / total[h]
        lse_ref[0, h : h + 1, :] = top[h] + jnp.log2(total[h])
    ctx = acc_ref[...].T.astype(BF16)
    for r in range(n_out):

        @pl.when(jnp.logical_and(i >= r * per_part, i < (r + 1) * per_part))
        def _():
            out_refs[r][...] = ctx


def attend(sc, q_parts, keys, values_t, lo, hi, mp, bq, bk):
    tokens, width = sum(q.shape[0] for q in q_parts), keys.shape[1]
    heads = width // DH
    nblk, per_part = tokens // bq, tokens // bq // mp
    if len(q_parts) == 1 and mp > 1:
        q_specs = [pl.BlockSpec((bq, width), lambda i, sc: (sc[2 * nblk + i], 0))]
    else:
        q_specs = [pl.BlockSpec((bq, width), part_map(r, per_part)) for r in range(mp)]
    full = lambda a: pl.BlockSpec(a.shape, lambda i, sc: (0, 0))
    row = pl.BlockSpec((1, bq), lambda i, sc: (0, i))
    outs = pl.pallas_call(
        functools.partial(attend_kernel, nblk, per_part, len(q_parts), mp, heads, bq, bk),
        grid_spec=pltpu.PrefetchScalarGridSpec(
            num_scalar_prefetch=1,
            grid=(nblk,),
            in_specs=q_specs + [full(keys), full(values_t), row, row],
            out_specs=[pl.BlockSpec((bq, width), part_map(r, per_part)) for r in range(mp)]
            + [pl.BlockSpec((1, heads, bq), lambda i, sc: (i, 0, 0))],
            scratch_shapes=[
                pltpu.VMEM((width, bq), F32),
                pltpu.VMEM((heads * bq, group_of(heads) * DH), BF16),
                pltpu.VMEM((bk, heads * bq), F32),
                pltpu.VMEM((bk, heads * bq), BF16),
            ],
        ),
        out_shape=[jax.ShapeDtypeStruct((tokens // mp, width), BF16)] * mp
        + [jax.ShapeDtypeStruct((nblk, heads, bq), F32)],
        compiler_params=params(14),
        cost_estimate=cost(4 * tokens * 512 * width, 8 * tokens * width, tokens * 512 * heads),
    )(sc, *q_parts, keys, values_t, lo, hi)
    return outs[:mp], outs[mp]


def attend_back_kernel(nblk, per_part, n_q, n_part, heads, bq, bk, sc, *refs):
    q_refs, refs = refs[:n_q], refs[n_q:]
    do_refs, refs = refs[:n_part], refs[n_part:]
    o_refs, refs = refs[:n_part], refs[n_part:]
    k_ref, kt_ref, v_ref, lo_ref, hi_ref, lse_ref = refs[:6]
    dq_refs, refs = refs[6 : 6 + n_q], refs[6 + n_q :]
    dk_ref, dv_ref, dk_acc, dv_acc, dq_acc, q_heads, do_heads = refs
    i = pl.program_id(0)

    @pl.when(i == 0)
    def _():
        dk_acc[...] = jnp.zeros_like(dk_acc)
        dv_acc[...] = jnp.zeros_like(dv_acc)

    q_heads[...] = per_head(pick(i, per_part, q_refs), heads)
    do = pick(i, per_part, do_refs)
    do_heads[...] = per_head(do, heads)
    lo = lo_ref[...]
    hi = hi_ref[...]
    span = [slice(h * bq, (h + 1) * bq) for h in range(heads)]
    cols = [slice(h * DH, (h + 1) * DH) for h in range(heads)]
    many = group_of(heads)
    wide = [slice(h // many * many * DH, (h // many + 1) * many * DH) for h in range(heads)]
    prod = (do.astype(F32) * pick(i, per_part, o_refs).astype(F32)).T
    delta = [jnp.sum(prod[cols[h], :], axis=0, keepdims=True) for h in range(heads)]
    lse = [lse_ref[0, h : h + 1, :] for h in range(heads)]
    dq_acc[...] = jnp.zeros_like(dq_acc)
    place = lax.broadcasted_iota(jnp.int32, (bk, bq), 0)

    def step(kb, carry):
        start = pl.multiple_of(kb * bk, bk)
        rows = pl.ds(start, bk)
        kt = kt_ref[:, rows]
        keep = jnp.logical_and(place >= lo - start, place < hi - start)
        groups = [(slice(h * bq, (h + many) * bq), wide[h]) for h in range(0, heads, many)]
        s = [mm(k_ref[rows, w], q_heads[g, :], NT) * SCALE2 for g, w in groups]
        dp = [mm(v_ref[rows, w], do_heads[g, :], NT) for g, w in groups]
        at = [(h // many, slice(h % many * bq, (h % many + 1) * bq)) for h in range(heads)]
        p = [jnp.where(keep, jnp.exp2(s[g][:, c] - lse[h]), 0.0) for h, (g, c) in enumerate(at)]
        ds = [(p[h] * (dp[g][:, c] - delta[h])).astype(BF16) for h, (g, c) in enumerate(at)]
        p = [p[h].astype(BF16) for h in range(heads)]
        for g, (r, w) in enumerate(groups):
            here = slice(g * many, (g + 1) * many)
            dv_acc[rows, w] += mm(jnp.concatenate(p[here], axis=1), do_heads[r, :])
            dk_acc[rows, w] += mm(jnp.concatenate(ds[here], axis=1), q_heads[r, :])
        for h in range(heads):
            dq_acc[cols[h], :] += mm(kt[cols[h], :], ds[h])
        return carry

    lax.fori_loop(sc[i], sc[nblk + i], step, 0)
    dq = (dq_acc[...] * SCALE).T.astype(BF16)
    if n_q == 1:
        dq_refs[0][...] = dq
    else:
        for r in range(n_q):

            @pl.when(jnp.logical_and(i >= r * per_part, i < (r + 1) * per_part))
            def _():
                dq_refs[r][...] = dq

    @pl.when(i == nblk - 1)
    def _():
        dk_ref[...] = (dk_acc[...] * SCALE).astype(BF16)
        dv_ref[...] = dv_acc[...].astype(BF16)


def attend_back(sc, q_parts, do_parts, o_parts, keys, keys_t, values, lo, hi, lse, mp, bq, bk):
    tokens, width = sum(q.shape[0] for q in q_parts), keys.shape[1]
    heads = width // DH
    nblk, per_part = tokens // bq, tokens // bq // mp
    parts = [pl.BlockSpec((bq, width), part_map(r, per_part)) for r in range(mp)]
    if len(q_parts) == 1 and mp > 1:
        q_specs = [pl.BlockSpec((bq, width), lambda i, sc: (sc[2 * nblk + i], 0))]
    else:
        q_specs = parts
    full = lambda a: pl.BlockSpec(a.shape, lambda i, sc: (0, 0))
    row = pl.BlockSpec((1, bq), lambda i, sc: (0, i))
    outs = pl.pallas_call(
        functools.partial(attend_back_kernel, nblk, per_part, len(q_parts), mp, heads, bq, bk),
        grid_spec=pltpu.PrefetchScalarGridSpec(
            num_scalar_prefetch=1,
            grid=(nblk,),
            in_specs=q_specs
            + parts
            + parts
            + [full(keys), full(keys_t), full(values), row, row]
            + [pl.BlockSpec((1, heads, bq), lambda i, sc: (i, 0, 0))],
            out_specs=q_specs + [full(keys), full(keys)],
            scratch_shapes=[
                pltpu.VMEM(keys.shape, F32),
                pltpu.VMEM(keys.shape, F32),
                pltpu.VMEM((width, bq), F32),
                pltpu.VMEM((heads * bq, group_of(heads) * DH), BF16),
                pltpu.VMEM((heads * bq, group_of(heads) * DH), BF16),
            ],
        ),
        out_shape=[jax.ShapeDtypeStruct(q.shape, BF16) for q in q_parts]
        + [jax.ShapeDtypeStruct(keys.shape, BF16)] * 2,
        compiler_params=params(26),
        cost_estimate=cost(10 * tokens * 512 * width, 12 * tokens * width, tokens * 512 * heads),
    )(sc, *q_parts, *do_parts, *o_parts, keys, keys_t, values, lo, hi, lse)
    return outs[: len(q_parts)], outs[-2], outs[-1]


def norm_stats(a):
    centre = a - jnp.mean(a, axis=-1, keepdims=True)
    rstd = lax.rsqrt(jnp.mean(centre * centre, axis=-1, keepdims=True) + 1e-05)
    return centre * rstd, rstd


def norm_back(dy, xhat, rstd, gain):
    t = dy * gain
    mean_t = jnp.mean(t, axis=-1, keepdims=True)
    mean_tx = jnp.mean(t * xhat, axis=-1, keepdims=True)
    return rstd * (t - mean_t - xhat * mean_tx)


def project_kernel(n, turned, x_ref, w_ref, *outs):
    x = x_ref[...]
    for c in range(n):
        y = mm(x, w_ref[c])
        outs[c][...] = y.astype(BF16)
        if c in turned:
            outs[n + turned.index(c)][...] = y.T.astype(BF16)


def project(x, w, turned, bt):
    n, d, width = w.shape
    tokens = x.shape[0]
    return pl.pallas_call(
        functools.partial(project_kernel, n, turned),
        grid=(tokens // bt,),
        in_specs=[pl.BlockSpec((bt, d), lambda i: (i, 0)), pl.BlockSpec(w.shape, lambda i: (0, 0, 0))],
        out_specs=[pl.BlockSpec((bt, width), lambda i: (i, 0))] * n
        + [pl.BlockSpec((width, bt), lambda i: (0, i))] * len(turned),
        out_shape=[jax.ShapeDtypeStruct((tokens, width), BF16)] * n
        + [jax.ShapeDtypeStruct((width, tokens), BF16)] * len(turned),
        compiler_params=params(14),
        cost_estimate=cost(2 * tokens * d * width * n, tokens * (d + 2 * n * width) * 2),
    )(x, w)


def post_self_kernel(mp, sc, *refs):
    x_ref = refs[0]
    ctx, wo, cq = refs[1 : 1 + mp], refs[1 + mp : 1 + 2 * mp], refs[1 + 2 * mp : 1 + 3 * mp]
    gain_ref, shift_ref = refs[1 + 3 * mp : 3 + 3 * mp]
    n1_ref, xhat_ref, rstd_ref = refs[3 + 3 * mp : 6 + 3 * mp]
    qc = refs[6 + 3 * mp :]
    a1 = x_ref[...].astype(F32)
    for r in range(mp):
        a1 += mm(ctx[r][...], wo[r][...])
    xhat, rstd = norm_stats(a1)
    n1 = (xhat * gain_ref[0:1, :] + shift_ref[0:1, :]).astype(BF16)
    n1_ref[...] = n1
    xhat_ref[...] = xhat
    rstd_ref[...] = rstd
    for r in range(mp):
        qc[r][...] = mm(n1, cq[r][...]).astype(BF16)


def whole(a):
    return pl.BlockSpec(a.shape, lambda i, sc: (0,) * a.ndim)


def rows_of(bt, width):
    return pl.BlockSpec((bt, width), lambda i, sc: (i, 0))


def post_self(sc, x, ctx, wo, cq, gain, shift, share, bt):
    mp, d = len(ctx), x.shape[1]
    width = ctx[0].shape[1]
    nb = share // bt
    outs = pl.pallas_call(
        functools.partial(post_self_kernel, mp),
        grid_spec=pltpu.PrefetchScalarGridSpec(
            num_scalar_prefetch=1,
            grid=(nb,),
            in_specs=[pl.BlockSpec((bt, d), lambda i, sc: (sc[0] * nb + i, 0))]
            + [rows_of(bt, width)] * mp
            + [whole(w) for w in (*wo, *cq, gain, shift)],
            out_specs=[rows_of(bt, d), rows_of(bt, d), rows_of(bt, 1)] + [rows_of(bt, width)] * mp,
        ),
        out_shape=[
            jax.ShapeDtypeStruct((share, d), BF16),
            jax.ShapeDtypeStruct((share, d), F32),
            jax.ShapeDtypeStruct((share, 1), F32),
        ]
        + [jax.ShapeDtypeStruct((share, width), BF16)] * mp,
        compiler_params=params(16),
        cost_estimate=cost(4 * share * d * d, share * d * 12),
    )(sc, x, *ctx, *wo, *cq, gain, shift)
    return outs[0], outs[1], outs[2], outs[3:]


def middle_kernel(mp, *refs):
    refs = list(refs)

    def take(n):
        got = refs[:n]
        del refs[:n]
        return got

    cctx, (n1_ref, cot_ref) = take(mp), take(2)
    co, up, down = take(mp), take(mp), take(mp)
    gain_ref, shift_ref = take(2)
    out_ref, da2_ref, n2_ref, e3_ref, e2_ref = take(5)
    dcctx, hid, dpre = take(mp), take(mp), take(mp)
    (small_ref,) = take(1)
    (slope_ref,) = take(1)
    ff = up[0].shape[0]
    i = pl.program_id(0)

    a2 = n1_ref[...].astype(F32)
    for r in range(mp):
        a2 += mm(cctx[r][...], co[r][...])
    xhat2, rstd2 = norm_stats(a2)
    n2 = (xhat2 * gain_ref[1:2, :] + shift_ref[1:2, :]).astype(BF16)
    n2_ref[...] = n2
    a3 = n2.astype(F32)
    for r in range(mp):
        u = mm(n2, up[r][...], NT)
        sg = 0.5 * jnp.tanh(0.5 * u) + 0.5
        h = u * sg
        hid[r][...] = h.astype(BF16)
        slope_ref[:, r * ff : (r + 1) * ff] = sg + h * (1.0 - sg)
        a3 += mm(hid[r][...], down[r][...])
    xhat3, rstd3 = norm_stats(a3)
    out_ref[...] = (xhat3 * gain_ref[2:3, :] + shift_ref[2:3, :]).astype(BF16)
    g = cot_ref[...].astype(F32)
    da3 = norm_back(g, xhat3, rstd3, gain_ref[2:3, :])
    e3 = da3.astype(BF16)
    e3_ref[...] = e3
    dn2 = da3
    for r in range(mp):
        dh = mm(e3, down[r][...], NT)
        dpre[r][...] = (dh * slope_ref[:, r * ff : (r + 1) * ff]).astype(BF16)
        dn2 += mm(dpre[r][...], up[r][...])
    da2 = norm_back(dn2, xhat2, rstd2, gain_ref[1:2, :])
    da2_ref[...] = da2
    e2 = da2.astype(BF16)
    e2_ref[...] = e2
    for r in range(mp):
        dcctx[r][...] = mm(e2, co[r][...], NT).astype(BF16)
    sums = jnp.concatenate(
        [
            jnp.sum(dn2 * xhat2, axis=0, keepdims=True),
            jnp.sum(g * xhat3, axis=0, keepdims=True),
            jnp.sum(dn2, axis=0, keepdims=True),
            jnp.sum(g, axis=0, keepdims=True),
        ],
        axis=0,
    )

    @pl.when(i == 0)
    def _():
        small_ref[...] = sums

    @pl.when(i > 0)
    def _():
        small_ref[...] += sums


def middle(cctx, n1, cot, co, up, down, gain, shift, bt):
    mp = len(cctx)
    share, d = n1.shape
    width = cctx[0].shape[1]
    ff = up[0].shape[0]
    row = lambda w: pl.BlockSpec((bt, w), lambda i: (i, 0))
    all_of = lambda a: pl.BlockSpec(a.shape, lambda i: (0,) * a.ndim)
    shape = lambda w, t: jax.ShapeDtypeStruct((share, w), t)
    outs = pl.pallas_call(
        functools.partial(middle_kernel, mp),
        grid=(share // bt,),
        in_specs=[row(width)] * mp + [row(d)] * 2 + [all_of(w) for w in (*co, *up, *down, gain, shift)],
        out_specs=[row(d)] * 5
        + [row(width)] * mp
        + [row(ff)] * (2 * mp)
        + [pl.BlockSpec((4, d), lambda i: (0, 0))],
        scratch_shapes=[pltpu.VMEM((bt, ff * mp), F32)],
        out_shape=[shape(d, BF16), shape(d, F32), shape(d, BF16), shape(d, BF16), shape(d, BF16)]
        + [shape(width, BF16)] * mp
        + [shape(ff, BF16)] * (2 * mp)
        + [jax.ShapeDtypeStruct((4, d), F32)],
        compiler_params=params(36),
        cost_estimate=cost(8 * share * d * ff * mp + 4 * share * d * d, share * ff * mp * 4, share * ff * mp),
    )(*cctx, n1, cot, *co, *up, *down, gain, shift)
    out, da2, n2, e3, e2 = outs[:5]
    return out, da2, n2, e3, e2, outs[5 : 5 + mp], outs[5 + mp : 5 + 2 * mp], outs[5 + 2 * mp : 5 + 3 * mp], outs[-1]


def pre_self_kernel(mp, *refs):
    dqc, cq, wo = refs[:mp], refs[mp : 2 * mp], refs[2 * mp : 3 * mp]
    da2_ref, xhat_ref, rstd_ref, gain_ref = refs[3 * mp : 3 * mp + 4]
    da1_ref, e1_ref = refs[3 * mp + 4 : 3 * mp + 6]
    dctx = refs[3 * mp + 6 : 4 * mp + 6]
    small_ref = refs[4 * mp + 6]
    i = pl.program_id(0)
    dn1 = da2_ref[...]
    for r in range(mp):
        dn1 += mm(dqc[r][...], cq[r][...], NT)
    xhat = xhat_ref[...]
    da1 = norm_back(dn1, xhat, rstd_ref[...], gain_ref[0:1, :])
    da1_ref[...] = da1
    e1 = da1.astype(BF16)
    e1_ref[...] = e1
    for r in range(mp):
        dctx[r][...] = mm(e1, wo[r][...], NT).astype(BF16)
    sums = jnp.concatenate(
        [jnp.sum(dn1 * xhat, axis=0, keepdims=True), jnp.sum(dn1, axis=0, keepdims=True)], axis=0
    )

    @pl.when(i == 0)
    def _():
        small_ref[...] = sums

    @pl.when(i > 0)
    def _():
        small_ref[...] += sums


def pre_self(dqc, cq, wo, da2, xhat, rstd, gain, bt):
    mp = len(dqc)
    share, d = da2.shape
    width = dqc[0].shape[1]
    row = lambda w: pl.BlockSpec((bt, w), lambda i: (i, 0))
    all_of = lambda a: pl.BlockSpec(a.shape, lambda i: (0,) * a.ndim)
    outs = pl.pallas_call(
        functools.partial(pre_self_kernel, mp),
        grid=(share // bt,),
        in_specs=[row(width)] * mp
        + [all_of(w) for w in (*cq, *wo)]
        + [row(d), row(d), row(1), all_of(gain)],
        out_specs=[row(d), row(d)] + [row(width)] * mp + [pl.BlockSpec((2, d), lambda i: (0, 0))],
        out_shape=[jax.ShapeDtypeStruct((share, d), F32), jax.ShapeDtypeStruct((share, d), BF16)]
        + [jax.ShapeDtypeStruct((share, width), BF16)] * mp
        + [jax.ShapeDtypeStruct((2, d), F32)],
        compiler_params=params(16),
        cost_estimate=cost(1, 1),
    )(*dqc, *cq, *wo, da2, xhat, rstd, gain)
    return outs[0], outs[1], outs[2 : 2 + mp], outs[-1]


def part_kernel(n_in, n_out, per_part, sc, *refs):
    grads, w_ref, outs = refs[:n_in], refs[n_in], refs[n_in + 1 :]
    i = pl.program_id(0)
    total = mm(jnp.concatenate([g[...] for g in grads], axis=1), w_ref[...])
    for r in range(n_out):

        @pl.when(jnp.logical_and(i >= r * per_part, i < (r + 1) * per_part))
        def _():
            outs[r][...] = total.astype(outs[r].dtype)


def input_part(sc, grads, w, mp, bt):
    tokens, width = grads[0].shape
    d = w.shape[1]
    w = w.swapaxes(1, 2).reshape(-1, d)
    nblk = tokens // bt
    per_part = nblk // mp
    outs = pl.pallas_call(
        functools.partial(part_kernel, len(grads), mp, per_part),
        grid_spec=pltpu.PrefetchScalarGridSpec(
            num_scalar_prefetch=1,
            grid=(nblk,),
            in_specs=[pl.BlockSpec((bt, width), lambda i, sc: (sc[i], 0))] * len(grads) + [whole(w)],
            out_specs=[pl.BlockSpec((bt, d), part_map(r, per_part)) for r in range(mp)],
        ),
        out_shape=[jax.ShapeDtypeStruct((tokens // mp, d), F32)]
        + [jax.ShapeDtypeStruct((tokens // mp, d), BF16)] * (mp - 1),
        compiler_params=params(16),
        cost_estimate=cost(1, 1),
    )(sc, *grads, w)
    return outs


MESH = pl.DeviceIdType.MESH


def all_sum_kernel(plan, nbits, n, *refs):
    ins, outs = refs[: n + 1], refs[n + 1 : 2 * n + 2]
    got = refs[2 * n + 2 : 2 * n + 3 + len(plan)]
    send_sem, recv_sem = refs[2 * n + 3 + len(plan) :]
    me, core = lax.axis_index("batch"), lax.axis_index("mp")
    bit = [(me // (1 << b)) % 2 for b in range(nbits)]
    partner = [(me + (1 << b) * (1 - 2 * bit[b]), core) for b in range(nbits)]
    barrier = pltpu.get_barrier_semaphore()
    for b in range(nbits):
        pl.semaphore_signal(barrier, inc=1, device_id=partner[b], device_id_type=MESH)
    pl.semaphore_wait(barrier, nbits)

    def send(c, s, b, src, dst):
        copy = pltpu.make_async_remote_copy(
            src_ref=src,
            dst_ref=dst,
            send_sem=send_sem.at[c, s],
            recv_sem=recv_sem.at[c, s],
            device_id=partner[b],
            device_id_type=MESH,
        )
        copy.start()
        copies[c][s] = copy

    def rows(off, count):
        return pl.ds(pl.multiple_of(off, 16), count)

    copies = [{} for _ in range(len(plan) + 1)]
    spans = []
    for _, count, order, _ in plan:
        span = [(0, count)]
        for b in order:
            off, size = span[-1]
            span.append((off + bit[b] * (size // 2), size // 2))
        spans.append(span)

    def held(c, s, b):
        a, count, _, _ = plan[c]
        half = count >> (s + 1)
        base = count - (count >> (s - 1)) if s else 0
        return (got[c] if s else ins[a]), base + (1 - bit[b]) * half, base + bit[b] * half, half

    def begin(c, s):
        a, count, order, _ = plan[c]
        if s < nbits:
            b = order[s]
            ref, gives, _, half = held(c, s, b)
            send(c, s, b, ref.at[rows(gives, half), :], got[c].at[pl.ds(count - (count >> s), half), :])
        else:
            j = 2 * nbits - 1 - s
            block = outs[a].at[rows(*spans[c][j + 1]), :]
            send(c, s, order[j], block, block)

    def finish(c, s):
        copies[c][s].wait_recv()
        if s < nbits:
            a, count, order, _ = plan[c]
            ref, _, stays, half = held(c, s, order[s])
            came = pl.ds(count - (count >> s), half)
            total = ref[rows(stays, half), :].astype(F32) + got[c][came, :].astype(F32)
            if s < nbits - 1:
                got[c][came, :] = total.astype(BF16)
            else:
                outs[a][rows(*spans[c][s + 1]), :] = total.astype(BF16)

    last = len(plan)
    size = ins[n].shape[0]
    outs[n][...] = ins[n][...]
    for c, (a, _, _, done) in enumerate(plan):
        if done:
            outs[a][rows(*spans[c][nbits]), :] = ins[a][...]
    for t in range(2 * nbits + 1):
        for c, (_, _, _, done) in enumerate(plan):
            s = t + done
            if done < s < 2 * nbits or (s == 2 * nbits and not done):
                finish(c, s - 1)
            if s < 2 * nbits:
                begin(c, s)
        if 1 <= t <= nbits:
            copies[last][t - 1].wait()
            outs[n][...] = (
                outs[n][...].astype(F32) + got[last][(t - 1) * size : t * size, :].astype(F32)
            ).astype(BF16)
        if t < nbits:
            send(last, t, t, outs[n], got[last].at[pl.ds(t * size, size), :])
    for c, (_, _, _, done) in enumerate(plan):
        if done:
            finish(c, 2 * nbits - 1)
        for copy in copies[c].values():
            copy.wait_send()


def all_sum(arrays, blocks, small, devices):
    nbits = devices.bit_length() - 1
    line = tuple(range(nbits - 1, 1, -1))
    flat = [a.reshape(-1, a.shape[-1]) for a in arrays]
    fits = [a.shape[0] % (16 * devices) == 0 for a in flat]
    plan, operands, shapes = [], [], []
    for a, first in blocks:
        plan.append((len(operands), a.shape[0] * devices, (*first, *line), nbits))
        operands.append(a)
        shapes.append((a.shape[0] * devices, a.shape[1]))
    for a, fit in zip(flat, fits):
        if fit:
            first = ((0, 1), (1, 0))[len(plan) % 2]
            plan.append((len(operands), a.shape[0], (*first, *range(2, nbits)), 0))
            operands.append(a)
            shapes.append(a.shape)
    small = jnp.pad(small, ((0, 16 - small.shape[0]), (0, 0)))
    operands.append(small)
    shapes.append(small.shape)
    vmem = pl.BlockSpec(memory_space=pltpu.VMEM)
    sums = pl.pallas_call(
        functools.partial(all_sum_kernel, plan, nbits, len(plan)),
        in_specs=[vmem] * len(operands),
        out_specs=[vmem] * len(operands),
        out_shape=[jax.ShapeDtypeStruct(shape, BF16) for shape in shapes],
        scratch_shapes=[pltpu.VMEM((16 if done else rows, operands[i].shape[1]), BF16) for i, rows, _, done in plan]
        + [pltpu.VMEM((16 * nbits, small.shape[1]), BF16)]
        + [pltpu.SemaphoreType.DMA((len(plan) + 1, 2 * nbits))] * 2,
        compiler_params=pltpu.CompilerParams(
            collective_id=7, has_side_effects=True, vmem_limit_bytes=28 << 20
        ),
    )(*operands)
    whole_ones = sums[: len(blocks)]
    rest = iter(sums[len(blocks) : -1])
    outs = [next(rest).reshape(a.shape) if fit else lax.psum(a, "batch") for a, fit in zip(arrays, fits)]
    return outs, whole_ones, sums[-1]


def across(r, shift, devices):
    return [(i, i ^ (r << shift)) for i in range(devices)]


def cut(blocks, shift, bits, me):
    place = (me >> shift) % (1 << bits)
    return [lax.dynamic_index_in_dim(blocks, place ^ r, 0, keepdims=False) for r in range(1 << bits)]


def scatter_step(blocks, shift, devices):
    return blocks[:1] + [lax.ppermute(b, "batch", across(r, shift, devices)) for r, b in enumerate(blocks) if r]


def add_up(blocks):
    total = blocks[0].astype(F32)
    for b in blocks[1:]:
        total += b.astype(F32)
    return total.astype(BF16)


def widen_kernel(layout, n, *refs):
    ins, outs = refs[:n], refs[n:]
    for out, sources in zip(outs, layout):
        for c, (i, at, count) in enumerate(sources):
            block = ins[i][...]
            if at is not None:
                block = block[:, at : at + count, :].reshape(-1, block.shape[-1])
            if len(out.shape) == 3:
                out[c] = block.astype(F32)
            else:
                out[...] = block.astype(F32)


def widen(arrays, layout, shapes, steps):
    def spec(shape):
        if len(shape) == 2:
            return pl.BlockSpec((shape[0] // steps, shape[1]), lambda i: (i, 0))
        return pl.BlockSpec((shape[0], shape[1] // steps, shape[2]), lambda i: (0, i, 0))

    def in_spec(a):
        if a.ndim == 2:
            return spec(a.shape)
        return pl.BlockSpec((a.shape[0] // steps, *a.shape[1:]), lambda i: (i, 0, 0))

    return pl.pallas_call(
        functools.partial(widen_kernel, layout, len(arrays)),
        grid=(steps,),
        in_specs=[in_spec(a) for a in arrays],
        out_specs=[spec(s) for s in shapes],
        out_shape=[jax.ShapeDtypeStruct(s, F32) for s in shapes],
        compiler_params=params(24),
        cost_estimate=cost(0, sum(math.prod(s) * 6 for s in shapes)),
    )(*arrays)


def shards(
    block_input_slots,
    memory,
    target_sentence_lengths,
    source_lengths,
    self_qkv,
    self_out,
    cross_query,
    cross_kv,
    cross_out,
    up_proj,
    down_proj,
    norm_gains,
    norm_biases,
    cotangent,
    mp,
    devices,
):
    tokens, d = block_input_slots.shape
    mem_tokens = memory.shape[0]
    share = cotangent.shape[0]
    mem_share = mem_tokens // mp
    width = self_qkv.shape[2]
    me = lax.axis_index("mp")
    bt = min(512, share)
    bq = min(256, share)
    bk = min(256, mem_tokens)

    def spread(own):
        return [own] + [
            lax.ppermute(own, "mp", [(i, (i + r) % mp) for i in range(mp)]) for r in range(1, mp)
        ]

    def exchange(pieces):
        got = [pieces[0]] + [None] * (mp - 1)
        for r in range(1, mp):
            got[mp - r] = lax.ppermute(pieces[r], "mp", [(i, (i - r) % mp) for i in range(mp)])
        return got

    wo, cq, co = spread(self_out), spread(cross_query), spread(cross_out)
    up, down = spread(up_proj), spread(down_proj)
    gain, shift = norm_gains.T, norm_biases.T

    t_len = target_sentence_lengths.reshape(-1)
    s_len = source_lengths.reshape(-1)
    t_end, s_end = jnp.cumsum(t_len), jnp.cumsum(s_len)
    t_start, s_start = t_end - t_len, s_end - s_len
    first = ((me - jnp.arange(mp)) % mp) * share
    place = (first[:, None] + jnp.arange(share)[None, :]).reshape(-1).astype(jnp.int32)
    begun = place[:, None] >= t_start[None, :]
    self_lo = jnp.max(jnp.where(begun, t_start[None, :], 0), axis=1)
    self_hi = place + 1
    cross_lo = jnp.max(jnp.where(begun, s_start[None, :], 0), axis=1)
    cross_hi = jnp.max(jnp.where(begun, s_end[None, :], 0), axis=1)
    nblk = tokens // bq
    q_block = place.reshape(nblk, bq)[:, 0] // bq

    def table(lo, hi):
        return jnp.concatenate(
            [lo.reshape(nblk, bq)[:, 0] // bk, (hi.reshape(nblk, bq)[:, -1] + bk - 1) // bk, q_block]
        ).astype(jnp.int32)

    self_table, cross_table = table(self_lo, self_hi), table(cross_lo, cross_hi)
    as_row = lambda v: v.reshape(1, tokens).astype(jnp.int32)
    self_lo, self_hi, cross_lo, cross_hi = map(as_row, (self_lo, self_hi, cross_lo, cross_hi))

    *proj, self_kt, self_vt = project(block_input_slots, self_qkv, (1, 2), min(512, mem_tokens))
    *pair, cross_kt, cross_vt = project(memory, cross_kv, (0, 1), min(512, mem_tokens))
    ctx_parts, self_lse = attend(
        self_table, proj[:1], proj[1], self_vt, self_lo, self_hi, mp, bq, bk
    )
    ctx = exchange(ctx_parts)
    me_row = me.reshape(1).astype(jnp.int32)
    n1, xhat1, rstd1, qc = post_self(me_row, block_input_slots, ctx, wo, cq, gain, shift, share, bt)
    qc_parts = exchange(qc)
    cctx_parts, cross_lse = attend(
        cross_table, qc_parts, pair[0], cross_vt, cross_lo, cross_hi, mp, bq, bk
    )
    cctx = exchange(cctx_parts)
    layer_output, da2, n2, e3, e2, dcctx, hid, dpre, small23 = middle(
        cctx, n1, cotangent, co, up, down, gain, shift, min(512, share)
    )
    dcctx_parts = exchange(dcctx)

    def grads(lefts, rights):
        return [mm(a, b, TN).astype(BF16) for a, b in zip(lefts, rights)]

    def collect(pieces):
        got = exchange(pieces)
        total = got[0].astype(F32)
        for g in got[1:]:
            total += g.astype(F32)
        return total

    early = [
        collect(grads(dpre, [n2] * mp)).astype(BF16),
        collect(grads(hid, [e3] * mp)).astype(BF16),
        collect(grads(cctx, [e2] * mp)).astype(BF16),
    ]
    hidden = all(g.shape[0] % (16 * devices) == 0 for g in early)
    row = lax.axis_index("batch")
    far = devices.bit_length() - 3
    if hidden:
        one = early[0].reshape(4, 1 << far, -1, d)
        two = jnp.concatenate([g.reshape(4, 1 << far, -1, d) for g in early[1:]], axis=2)
        here = row % 4
        mirrored = here % 2 * 2 + here // 2
        blocks = [
            jnp.concatenate(
                [
                    lax.dynamic_index_in_dim(one, mirrored ^ (0, 2, 1, 3)[r], 0, keepdims=False),
                    lax.dynamic_index_in_dim(two, here ^ r, 0, keepdims=False),
                ],
                axis=1,
            )
            for r in range(4)
        ]
        dcctx_parts, blocks = lax.optimization_barrier((dcctx_parts, blocks))
        blocks = scatter_step(blocks, 0, devices)
    dqc_parts, dkc, dvc = attend_back(
        cross_table, qc_parts, dcctx_parts, cctx_parts, pair[0], cross_kt, pair[1], cross_lo, cross_hi, cross_lse, mp, bq, bk
    )
    dqc = exchange(dqc_parts)
    if hidden:
        dqc, block = lax.optimization_barrier((dqc, add_up(blocks)))
    da1, e1, dctx, small1 = pre_self(dqc, cq, wo, da2, xhat1, rstd1, gain, bt)
    dctx_parts = exchange(dctx)
    mem_bt = min(512, mem_share)
    mem_nb = mem_share // mem_bt
    mem_blocks = ((((me - jnp.arange(mp)) % mp) * mem_nb)[:, None] + jnp.arange(mem_nb)[None, :]).reshape(-1)
    memory_parts = input_part(mem_blocks.astype(jnp.int32), [dkc, dvc], cross_kv, mp, mem_bt)
    memory_grad = collect(memory_parts)
    cross_kv_grad = [mm(memory, g, TN) for g in (dkc, dvc)]
    cross_query_grad = collect(grads([n1] * mp, dqc))
    self_out_grad = collect(grads(ctx, [e1] * mp))
    if hidden:
        dctx_parts, blocks = lax.optimization_barrier((dctx_parts, cut(block, 2, far, row)))
        blocks = scatter_step(blocks, 2, devices)
    (dq,), dk, dv = attend_back(
        self_table, proj[:1], dctx_parts, ctx_parts, proj[1], self_kt, proj[2], self_lo, self_hi, self_lse, mp, bq, bk
    )
    if hidden:
        dq, dk, dv, block = lax.optimization_barrier((dq, dk, dv, add_up(blocks)))
    in_bt = min(512, share)
    in_blocks = place.reshape(-1, in_bt)[:, 0] // in_bt
    input_parts = input_part(in_blocks.astype(jnp.int32), [dq, dk, dv], self_qkv, mp, in_bt)
    input_grad = collect(input_parts) + da1
    self_qkv_grad = [mm(block_input_slots, g, TN) for g in (dq, dk, dv)]

    small = jnp.concatenate([small1[:1], small23[:2], small1[1:], small23[2:]], axis=0)
    part = d // mp
    pieces = [
        lax.dynamic_slice_in_dim(small, ((me - r) % mp) * part, part, 1).astype(BF16) for r in range(mp)
    ]
    small = collect(pieces)
    late = [*self_qkv_grad, self_out_grad, cross_query_grad, *cross_kv_grad]
    late = [g.astype(BF16) for g in late]
    if hidden:
        count = early[0].shape[0] // devices
        summed, (up_grad, rest), small = all_sum(
            late, [(block[:count], (0, 1)), (block[count:], (1, 0))], small.astype(BF16), devices
        )
        rest = rest.reshape(devices, -1, d)
        count = early[1].shape[0] // devices
        more = early[2].shape[0] // devices
        late_shapes = [
            self_qkv.shape,
            self_out.shape,
            cross_query.shape,
            cross_kv.shape,
        ]
        *summed, up_grad, down_grad, cross_out_grad = widen(
            [*summed, up_grad, rest],
            [
                [(0, None, 0), (1, None, 0), (2, None, 0)],
                [(3, None, 0)],
                [(4, None, 0)],
                [(5, None, 0), (6, None, 0)],
                [(7, None, 0)],
                [(8, 0, count)],
                [(8, count, more)],
            ],
            late_shapes + [g.shape for g in early],
            8,
        )
    else:
        summed, _, small = all_sum(late + early, [], small.astype(BF16), devices)
        *summed, up_grad, down_grad, cross_out_grad = [g.astype(F32) for g in summed]
        dwq, dwk, dwv, self_out_grad, cross_query_grad, dck, dcv = summed
        summed = [jnp.stack([dwq, dwk, dwv]), self_out_grad, cross_query_grad, jnp.stack([dck, dcv])]
    summed += [cross_out_grad, up_grad, down_grad]
    small = small.astype(F32).T
    return (layer_output, input_grad, memory_grad, *summed, small[:, :3], small[:, 3:6])


def solution(mesh):
    mp = mesh.shape["mp"]
    rows = P("batch", None)
    both = P(("batch", "mp"), None)
    first, last, last3 = P("mp", None), P(None, "mp"), P(None, None, "mp")
    return jax.shard_map(
        functools.partial(shards, mp=mp, devices=mesh.shape["batch"]),
        mesh=mesh,
        in_specs=(rows, rows, rows, rows, last3, first, last, last3, first, first, first, P(), P(), both),
        out_specs=(both, both, both, last3, first, last, last3, first, first, first, first, first),
        check_vma=False,
    )
```

```python
import functools
import math

import jax
import jax.numpy as jnp
from jax import lax
from jax.experimental import pallas as pl
from jax.experimental.pallas import tpu as pltpu
from jax.sharding import PartitionSpec as P

DH = 64
NEG = -1e30
F32 = jnp.float32
BF16 = jnp.bfloat16
SCALE = DH**-0.5
SCALE2 = SCALE * math.log2(math.e)
NT = (((1,), (1,)), ((), ()))
NN = (((1,), (0,)), ((), ()))
TN = (((0,), (0,)), ((), ()))


def mm(a, b, dims=NN):
    return lax.dot_general(a, b, dims, preferred_element_type=F32)


def params(mib):
    return pltpu.CompilerParams(dimension_semantics=("arbitrary",), vmem_limit_bytes=mib << 20)


def cost(flops, nbytes, exps=0):
    return pl.CostEstimate(flops=int(flops), bytes_accessed=int(nbytes), transcendentals=int(exps))


def pick(i, per_part, refs):
    value = refs[0][...]
    for r in range(1, len(refs)):
        value = jnp.where(i >= r * per_part, refs[r][...], value)
    return value


def part_map(r, per_part):
    return lambda i, sc: (jnp.clip(i - r * per_part, 0, per_part - 1), 0)


def group_of(heads):
    return min(heads, 128 // DH)


def per_head(block, heads):
    many = group_of(heads)
    wide = many * DH
    head = lax.broadcasted_iota(jnp.int32, (block.shape[0], wide), 1) // DH
    parts = []
    for h in range(heads):
        cols = block[:, h // many * wide : (h // many + 1) * wide]
        parts.append(jnp.where(head == h % many, cols, jnp.zeros_like(cols)))
    return jnp.concatenate(parts, axis=0)


def attend_kernel(nblk, per_part, n_q, n_out, heads, bq, bk, sc, *refs):
    q_refs, refs = refs[:n_q], refs[n_q:]
    k_ref, vt_ref, lo_ref, hi_ref = refs[:4]
    out_refs, (lse_ref, acc_ref, q_heads, s_ref, p_ref) = refs[4 : 4 + n_out], refs[4 + n_out :]
    i = pl.program_id(0)
    q_heads[...] = per_head(pick(i, per_part, q_refs), heads)
    lo = lo_ref[...]
    hi = hi_ref[...]
    acc_ref[...] = jnp.zeros_like(acc_ref)
    place = lax.broadcasted_iota(jnp.int32, (bk, bq), 0)
    span = [slice(h * bq, (h + 1) * bq) for h in range(heads)]
    cols = [slice(h * DH, (h + 1) * DH) for h in range(heads)]
    many = group_of(heads)
    wide = [slice(h // many * many * DH, (h // many + 1) * many * DH) for h in range(heads)]

    first, end = sc[i], sc[nblk + i]

    def rows(kb):
        return pl.ds(pl.multiple_of(kb * bk, bk), bk)

    def scores(kb, h):
        s_ref[:, span[h]] = mm(k_ref[rows(kb), wide[h]], q_heads[span[h], :], NT)

    def soften(kb, h, keep, top, total):
        t = jnp.where(keep, s_ref[:, span[h]] * SCALE2, NEG)
        new_top = jnp.maximum(top, jnp.max(t, axis=0, keepdims=True))
        e = jnp.exp2(t - new_top)
        decay = jnp.exp2(top - new_top)
        p_ref[:, span[h]] = e.astype(BF16)
        return new_top, total * decay + jnp.sum(e, axis=0, keepdims=True), decay

    def gather(kb, h, decay):
        acc_ref[cols[h], :] = acc_ref[cols[h], :] * decay + mm(vt_ref[cols[h], rows(kb)], p_ref[:, span[h]])

    def stage(kb, carry):
        start = kb * bk
        keep = jnp.logical_and(place >= lo - start, place < hi - start)
        after = jnp.minimum(kb + 1, end - 1)
        new = []
        for h in range(heads):
            top, total, decay = carry[h]
            if decay is not None:
                gather(kb - 1, h, decay)
            new.append(soften(kb, h, keep, top, total))
            scores(after, h)
        return new

    for h in range(heads):
        scores(first, h)
    none = jnp.full((1, bq), NEG, F32), jnp.zeros((1, bq), F32), None
    carry = lax.fori_loop(first + 1, end, stage, stage(first, [none] * heads))
    for h in range(heads):
        gather(end - 1, h, carry[h][2])
    top = [carry[h][0] for h in range(heads)]
    total = [carry[h][1] for h in range(heads)]
    for h in range(heads):
        acc_ref[cols[h], :] = acc_ref[cols[h], :] / total[h]
        lse_ref[0, h : h + 1, :] = top[h] + jnp.log2(total[h])
    ctx = acc_ref[...].T.astype(BF16)
    for r in range(n_out):

        @pl.when(jnp.logical_and(i >= r * per_part, i < (r + 1) * per_part))
        def _():
            out_refs[r][...] = ctx


def attend(sc, q_parts, keys, values_t, lo, hi, mp, bq, bk):
    tokens, width = sum(q.shape[0] for q in q_parts), keys.shape[1]
    heads = width // DH
    nblk, per_part = tokens // bq, tokens // bq // mp
    if len(q_parts) == 1 and mp > 1:
        q_specs = [pl.BlockSpec((bq, width), lambda i, sc: (sc[2 * nblk + i], 0))]
    else:
        q_specs = [pl.BlockSpec((bq, width), part_map(r, per_part)) for r in range(mp)]
    full = lambda a: pl.BlockSpec(a.shape, lambda i, sc: (0, 0))
    row = pl.BlockSpec((1, bq), lambda i, sc: (0, i))
    outs = pl.pallas_call(
        functools.partial(attend_kernel, nblk, per_part, len(q_parts), mp, heads, bq, bk),
        grid_spec=pltpu.PrefetchScalarGridSpec(
            num_scalar_prefetch=1,
            grid=(nblk,),
            in_specs=q_specs + [full(keys), full(values_t), row, row],
            out_specs=[pl.BlockSpec((bq, width), part_map(r, per_part)) for r in range(mp)]
            + [pl.BlockSpec((1, heads, bq), lambda i, sc: (i, 0, 0))],
            scratch_shapes=[
                pltpu.VMEM((width, bq), F32),
                pltpu.VMEM((heads * bq, group_of(heads) * DH), BF16),
                pltpu.VMEM((bk, heads * bq), F32),
                pltpu.VMEM((bk, heads * bq), BF16),
            ],
        ),
        out_shape=[jax.ShapeDtypeStruct((tokens // mp, width), BF16)] * mp
        + [jax.ShapeDtypeStruct((nblk, heads, bq), F32)],
        compiler_params=params(14),
        cost_estimate=cost(4 * tokens * 512 * width, 8 * tokens * width, tokens * 512 * heads),
    )(sc, *q_parts, keys, values_t, lo, hi)
    return outs[:mp], outs[mp]


def attend_back_kernel(nblk, per_part, n_q, n_part, heads, bq, bk, sc, *refs):
    q_refs, refs = refs[:n_q], refs[n_q:]
    do_refs, refs = refs[:n_part], refs[n_part:]
    o_refs, refs = refs[:n_part], refs[n_part:]
    k_ref, kt_ref, v_ref, lo_ref, hi_ref, lse_ref = refs[:6]
    dq_refs, refs = refs[6 : 6 + n_q], refs[6 + n_q :]
    dk_ref, dv_ref, dk_acc, dv_acc, dq_acc, q_heads, do_heads = refs
    i = pl.program_id(0)

    @pl.when(i == 0)
    def _():
        dk_acc[...] = jnp.zeros_like(dk_acc)
        dv_acc[...] = jnp.zeros_like(dv_acc)

    q_heads[...] = per_head(pick(i, per_part, q_refs), heads)
    do = pick(i, per_part, do_refs)
    do_heads[...] = per_head(do, heads)
    lo = lo_ref[...]
    hi = hi_ref[...]
    span = [slice(h * bq, (h + 1) * bq) for h in range(heads)]
    cols = [slice(h * DH, (h + 1) * DH) for h in range(heads)]
    many = group_of(heads)
    wide = [slice(h // many * many * DH, (h // many + 1) * many * DH) for h in range(heads)]
    prod = (do.astype(F32) * pick(i, per_part, o_refs).astype(F32)).T
    delta = [jnp.sum(prod[cols[h], :], axis=0, keepdims=True) for h in range(heads)]
    lse = [lse_ref[0, h : h + 1, :] for h in range(heads)]
    dq_acc[...] = jnp.zeros_like(dq_acc)
    place = lax.broadcasted_iota(jnp.int32, (bk, bq), 0)

    def step(kb, carry):
        start = pl.multiple_of(kb * bk, bk)
        rows = pl.ds(start, bk)
        kt = kt_ref[:, rows]
        keep = jnp.logical_and(place >= lo - start, place < hi - start)
        groups = [(slice(h * bq, (h + many) * bq), wide[h]) for h in range(0, heads, many)]
        s = [mm(k_ref[rows, w], q_heads[g, :], NT) * SCALE2 for g, w in groups]
        dp = [mm(v_ref[rows, w], do_heads[g, :], NT) for g, w in groups]
        at = [(h // many, slice(h % many * bq, (h % many + 1) * bq)) for h in range(heads)]
        p = [jnp.where(keep, jnp.exp2(s[g][:, c] - lse[h]), 0.0) for h, (g, c) in enumerate(at)]
        ds = [(p[h] * (dp[g][:, c] - delta[h])).astype(BF16) for h, (g, c) in enumerate(at)]
        p = [p[h].astype(BF16) for h in range(heads)]
        for g, (r, w) in enumerate(groups):
            here = slice(g * many, (g + 1) * many)
            dv_acc[rows, w] += mm(jnp.concatenate(p[here], axis=1), do_heads[r, :])
            dk_acc[rows, w] += mm(jnp.concatenate(ds[here], axis=1), q_heads[r, :])
        for h in range(heads):
            dq_acc[cols[h], :] += mm(kt[cols[h], :], ds[h])
        return carry

    lax.fori_loop(sc[i], sc[nblk + i], step, 0)
    dq = (dq_acc[...] * SCALE).T.astype(BF16)
    if n_q == 1:
        dq_refs[0][...] = dq
    else:
        for r in range(n_q):

            @pl.when(jnp.logical_and(i >= r * per_part, i < (r + 1) * per_part))
            def _():
                dq_refs[r][...] = dq

    @pl.when(i == nblk - 1)
    def _():
        dk_ref[...] = (dk_acc[...] * SCALE).astype(BF16)
        dv_ref[...] = dv_acc[...].astype(BF16)


def attend_back(sc, q_parts, do_parts, o_parts, keys, keys_t, values, lo, hi, lse, mp, bq, bk):
    tokens, width = sum(q.shape[0] for q in q_parts), keys.shape[1]
    heads = width // DH
    nblk, per_part = tokens // bq, tokens // bq // mp
    parts = [pl.BlockSpec((bq, width), part_map(r, per_part)) for r in range(mp)]
    if len(q_parts) == 1 and mp > 1:
        q_specs = [pl.BlockSpec((bq, width), lambda i, sc: (sc[2 * nblk + i], 0))]
    else:
        q_specs = parts
    full = lambda a: pl.BlockSpec(a.shape, lambda i, sc: (0, 0))
    row = pl.BlockSpec((1, bq), lambda i, sc: (0, i))
    outs = pl.pallas_call(
        functools.partial(attend_back_kernel, nblk, per_part, len(q_parts), mp, heads, bq, bk),
        grid_spec=pltpu.PrefetchScalarGridSpec(
            num_scalar_prefetch=1,
            grid=(nblk,),
            in_specs=q_specs
            + parts
            + parts
            + [full(keys), full(keys_t), full(values), row, row]
            + [pl.BlockSpec((1, heads, bq), lambda i, sc: (i, 0, 0))],
            out_specs=q_specs + [full(keys), full(keys)],
            scratch_shapes=[
                pltpu.VMEM(keys.shape, F32),
                pltpu.VMEM(keys.shape, F32),
                pltpu.VMEM((width, bq), F32),
                pltpu.VMEM((heads * bq, group_of(heads) * DH), BF16),
                pltpu.VMEM((heads * bq, group_of(heads) * DH), BF16),
            ],
        ),
        out_shape=[jax.ShapeDtypeStruct(q.shape, BF16) for q in q_parts]
        + [jax.ShapeDtypeStruct(keys.shape, BF16)] * 2,
        compiler_params=params(26),
        cost_estimate=cost(10 * tokens * 512 * width, 12 * tokens * width, tokens * 512 * heads),
    )(sc, *q_parts, *do_parts, *o_parts, keys, keys_t, values, lo, hi, lse)
    return outs[: len(q_parts)], outs[-2], outs[-1]


def norm_stats(a):
    centre = a - jnp.mean(a, axis=-1, keepdims=True)
    rstd = lax.rsqrt(jnp.mean(centre * centre, axis=-1, keepdims=True) + 1e-05)
    return centre * rstd, rstd


def norm_back(dy, xhat, rstd, gain):
    t = dy * gain
    mean_t = jnp.mean(t, axis=-1, keepdims=True)
    mean_tx = jnp.mean(t * xhat, axis=-1, keepdims=True)
    return rstd * (t - mean_t - xhat * mean_tx)


def project_kernel(n, turned, x_ref, w_ref, *outs):
    x = x_ref[...]
    for c in range(n):
        y = mm(x, w_ref[c])
        outs[c][...] = y.astype(BF16)
        if c in turned:
            outs[n + turned.index(c)][...] = y.T.astype(BF16)


def project(x, w, turned, bt):
    n, d, width = w.shape
    tokens = x.shape[0]
    return pl.pallas_call(
        functools.partial(project_kernel, n, turned),
        grid=(tokens // bt,),
        in_specs=[pl.BlockSpec((bt, d), lambda i: (i, 0)), pl.BlockSpec(w.shape, lambda i: (0, 0, 0))],
        out_specs=[pl.BlockSpec((bt, width), lambda i: (i, 0))] * n
        + [pl.BlockSpec((width, bt), lambda i: (0, i))] * len(turned),
        out_shape=[jax.ShapeDtypeStruct((tokens, width), BF16)] * n
        + [jax.ShapeDtypeStruct((width, tokens), BF16)] * len(turned),
        compiler_params=params(14),
        cost_estimate=cost(2 * tokens * d * width * n, tokens * (d + 2 * n * width) * 2),
    )(x, w)


def post_self_kernel(mp, sc, *refs):
    x_ref = refs[0]
    ctx, wo, cq = refs[1 : 1 + mp], refs[1 + mp : 1 + 2 * mp], refs[1 + 2 * mp : 1 + 3 * mp]
    gain_ref, shift_ref = refs[1 + 3 * mp : 3 + 3 * mp]
    n1_ref, xhat_ref, rstd_ref = refs[3 + 3 * mp : 6 + 3 * mp]
    qc = refs[6 + 3 * mp :]
    a1 = x_ref[...].astype(F32)
    for r in range(mp):
        a1 += mm(ctx[r][...], wo[r][...])
    xhat, rstd = norm_stats(a1)
    n1 = (xhat * gain_ref[0:1, :] + shift_ref[0:1, :]).astype(BF16)
    n1_ref[...] = n1
    xhat_ref[...] = xhat
    rstd_ref[...] = rstd
    for r in range(mp):
        qc[r][...] = mm(n1, cq[r][...]).astype(BF16)


def whole(a):
    return pl.BlockSpec(a.shape, lambda i, sc: (0,) * a.ndim)


def rows_of(bt, width):
    return pl.BlockSpec((bt, width), lambda i, sc: (i, 0))


def post_self(sc, x, ctx, wo, cq, gain, shift, share, bt):
    mp, d = len(ctx), x.shape[1]
    width = ctx[0].shape[1]
    nb = share // bt
    outs = pl.pallas_call(
        functools.partial(post_self_kernel, mp),
        grid_spec=pltpu.PrefetchScalarGridSpec(
            num_scalar_prefetch=1,
            grid=(nb,),
            in_specs=[pl.BlockSpec((bt, d), lambda i, sc: (sc[0] * nb + i, 0))]
            + [rows_of(bt, width)] * mp
            + [whole(w) for w in (*wo, *cq, gain, shift)],
            out_specs=[rows_of(bt, d), rows_of(bt, d), rows_of(bt, 1)] + [rows_of(bt, width)] * mp,
        ),
        out_shape=[
            jax.ShapeDtypeStruct((share, d), BF16),
            jax.ShapeDtypeStruct((share, d), F32),
            jax.ShapeDtypeStruct((share, 1), F32),
        ]
        + [jax.ShapeDtypeStruct((share, width), BF16)] * mp,
        compiler_params=params(16),
        cost_estimate=cost(4 * share * d * d, share * d * 12),
    )(sc, x, *ctx, *wo, *cq, gain, shift)
    return outs[0], outs[1], outs[2], outs[3:]


def middle_kernel(mp, *refs):
    refs = list(refs)

    def take(n):
        got = refs[:n]
        del refs[:n]
        return got

    cctx, (n1_ref, cot_ref) = take(mp), take(2)
    co, up, down = take(mp), take(mp), take(mp)
    gain_ref, shift_ref = take(2)
    out_ref, da2_ref, n2_ref, e3_ref, e2_ref = take(5)
    dcctx, hid, dpre = take(mp), take(mp), take(mp)
    (small_ref,) = take(1)
    (slope_ref,) = take(1)
    ff = up[0].shape[0]
    i = pl.program_id(0)

    a2 = n1_ref[...].astype(F32)
    for r in range(mp):
        a2 += mm(cctx[r][...], co[r][...])
    xhat2, rstd2 = norm_stats(a2)
    n2 = (xhat2 * gain_ref[1:2, :] + shift_ref[1:2, :]).astype(BF16)
    n2_ref[...] = n2
    a3 = n2.astype(F32)
    for r in range(mp):
        u = mm(n2, up[r][...], NT)
        sg = 0.5 * jnp.tanh(0.5 * u) + 0.5
        h = u * sg
        hid[r][...] = h.astype(BF16)
        slope_ref[:, r * ff : (r + 1) * ff] = sg + h * (1.0 - sg)
        a3 += mm(hid[r][...], down[r][...])
    xhat3, rstd3 = norm_stats(a3)
    out_ref[...] = (xhat3 * gain_ref[2:3, :] + shift_ref[2:3, :]).astype(BF16)
    g = cot_ref[...].astype(F32)
    da3 = norm_back(g, xhat3, rstd3, gain_ref[2:3, :])
    e3 = da3.astype(BF16)
    e3_ref[...] = e3
    dn2 = da3
    for r in range(mp):
        dh = mm(e3, down[r][...], NT)
        dpre[r][...] = (dh * slope_ref[:, r * ff : (r + 1) * ff]).astype(BF16)
        dn2 += mm(dpre[r][...], up[r][...])
    da2 = norm_back(dn2, xhat2, rstd2, gain_ref[1:2, :])
    da2_ref[...] = da2
    e2 = da2.astype(BF16)
    e2_ref[...] = e2
    for r in range(mp):
        dcctx[r][...] = mm(e2, co[r][...], NT).astype(BF16)
    sums = jnp.concatenate(
        [
            jnp.sum(dn2 * xhat2, axis=0, keepdims=True),
            jnp.sum(g * xhat3, axis=0, keepdims=True),
            jnp.sum(dn2, axis=0, keepdims=True),
            jnp.sum(g, axis=0, keepdims=True),
        ],
        axis=0,
    )

    @pl.when(i == 0)
    def _():
        small_ref[...] = sums

    @pl.when(i > 0)
    def _():
        small_ref[...] += sums


def middle(cctx, n1, cot, co, up, down, gain, shift, bt):
    mp = len(cctx)
    share, d = n1.shape
    width = cctx[0].shape[1]
    ff = up[0].shape[0]
    row = lambda w: pl.BlockSpec((bt, w), lambda i: (i, 0))
    all_of = lambda a: pl.BlockSpec(a.shape, lambda i: (0,) * a.ndim)
    shape = lambda w, t: jax.ShapeDtypeStruct((share, w), t)
    outs = pl.pallas_call(
        functools.partial(middle_kernel, mp),
        grid=(share // bt,),
        in_specs=[row(width)] * mp + [row(d)] * 2 + [all_of(w) for w in (*co, *up, *down, gain, shift)],
        out_specs=[row(d)] * 5
        + [row(width)] * mp
        + [row(ff)] * (2 * mp)
        + [pl.BlockSpec((4, d), lambda i: (0, 0))],
        scratch_shapes=[pltpu.VMEM((bt, ff * mp), F32)],
        out_shape=[shape(d, BF16), shape(d, F32), shape(d, BF16), shape(d, BF16), shape(d, BF16)]
        + [shape(width, BF16)] * mp
        + [shape(ff, BF16)] * (2 * mp)
        + [jax.ShapeDtypeStruct((4, d), F32)],
        compiler_params=params(36),
        cost_estimate=cost(8 * share * d * ff * mp + 4 * share * d * d, share * ff * mp * 4, share * ff * mp),
    )(*cctx, n1, cot, *co, *up, *down, gain, shift)
    out, da2, n2, e3, e2 = outs[:5]
    return out, da2, n2, e3, e2, outs[5 : 5 + mp], outs[5 + mp : 5 + 2 * mp], outs[5 + 2 * mp : 5 + 3 * mp], outs[-1]


def pre_self_kernel(mp, *refs):
    dqc, cq, wo = refs[:mp], refs[mp : 2 * mp], refs[2 * mp : 3 * mp]
    da2_ref, xhat_ref, rstd_ref, gain_ref = refs[3 * mp : 3 * mp + 4]
    da1_ref, e1_ref = refs[3 * mp + 4 : 3 * mp + 6]
    dctx = refs[3 * mp + 6 : 4 * mp + 6]
    small_ref = refs[4 * mp + 6]
    i = pl.program_id(0)
    dn1 = da2_ref[...]
    for r in range(mp):
        dn1 += mm(dqc[r][...], cq[r][...], NT)
    xhat = xhat_ref[...]
    da1 = norm_back(dn1, xhat, rstd_ref[...], gain_ref[0:1, :])
    da1_ref[...] = da1
    e1 = da1.astype(BF16)
    e1_ref[...] = e1
    for r in range(mp):
        dctx[r][...] = mm(e1, wo[r][...], NT).astype(BF16)
    sums = jnp.concatenate(
        [jnp.sum(dn1 * xhat, axis=0, keepdims=True), jnp.sum(dn1, axis=0, keepdims=True)], axis=0
    )

    @pl.when(i == 0)
    def _():
        small_ref[...] = sums

    @pl.when(i > 0)
    def _():
        small_ref[...] += sums


def pre_self(dqc, cq, wo, da2, xhat, rstd, gain, bt):
    mp = len(dqc)
    share, d = da2.shape
    width = dqc[0].shape[1]
    row = lambda w: pl.BlockSpec((bt, w), lambda i: (i, 0))
    all_of = lambda a: pl.BlockSpec(a.shape, lambda i: (0,) * a.ndim)
    outs = pl.pallas_call(
        functools.partial(pre_self_kernel, mp),
        grid=(share // bt,),
        in_specs=[row(width)] * mp
        + [all_of(w) for w in (*cq, *wo)]
        + [row(d), row(d), row(1), all_of(gain)],
        out_specs=[row(d), row(d)] + [row(width)] * mp + [pl.BlockSpec((2, d), lambda i: (0, 0))],
        out_shape=[jax.ShapeDtypeStruct((share, d), F32), jax.ShapeDtypeStruct((share, d), BF16)]
        + [jax.ShapeDtypeStruct((share, width), BF16)] * mp
        + [jax.ShapeDtypeStruct((2, d), F32)],
        compiler_params=params(16),
        cost_estimate=cost(1, 1),
    )(*dqc, *cq, *wo, da2, xhat, rstd, gain)
    return outs[0], outs[1], outs[2 : 2 + mp], outs[-1]


def part_kernel(n_in, n_out, per_part, sc, *refs):
    grads, w_ref, outs = refs[:n_in], refs[n_in], refs[n_in + 1 :]
    i = pl.program_id(0)
    total = mm(jnp.concatenate([g[...] for g in grads], axis=1), w_ref[...])
    for r in range(n_out):

        @pl.when(jnp.logical_and(i >= r * per_part, i < (r + 1) * per_part))
        def _():
            outs[r][...] = total.astype(outs[r].dtype)


def input_part(sc, grads, w, mp, bt):
    tokens, width = grads[0].shape
    d = w.shape[1]
    w = w.swapaxes(1, 2).reshape(-1, d)
    nblk = tokens // bt
    per_part = nblk // mp
    outs = pl.pallas_call(
        functools.partial(part_kernel, len(grads), mp, per_part),
        grid_spec=pltpu.PrefetchScalarGridSpec(
            num_scalar_prefetch=1,
            grid=(nblk,),
            in_specs=[pl.BlockSpec((bt, width), lambda i, sc: (sc[i], 0))] * len(grads) + [whole(w)],
            out_specs=[pl.BlockSpec((bt, d), part_map(r, per_part)) for r in range(mp)],
        ),
        out_shape=[jax.ShapeDtypeStruct((tokens // mp, d), F32)]
        + [jax.ShapeDtypeStruct((tokens // mp, d), BF16)] * (mp - 1),
        compiler_params=params(16),
        cost_estimate=cost(1, 1),
    )(sc, *grads, w)
    return outs


MESH = pl.DeviceIdType.MESH


def all_sum_kernel(plan, nbits, n, *refs):
    ins, outs = refs[: n + 1], refs[n + 1 : 2 * n + 2]
    got = refs[2 * n + 2 : 2 * n + 3 + len(plan)]
    send_sem, recv_sem = refs[2 * n + 3 + len(plan) :]
    me, core = lax.axis_index("batch"), lax.axis_index("mp")
    bit = [(me // (1 << b)) % 2 for b in range(nbits)]
    partner = [(me + (1 << b) * (1 - 2 * bit[b]), core) for b in range(nbits)]
    barrier = pltpu.get_barrier_semaphore()
    for b in range(nbits):
        pl.semaphore_signal(barrier, inc=1, device_id=partner[b], device_id_type=MESH)
    pl.semaphore_wait(barrier, nbits)

    def send(c, s, b, src, dst):
        copy = pltpu.make_async_remote_copy(
            src_ref=src,
            dst_ref=dst,
            send_sem=send_sem.at[c, s],
            recv_sem=recv_sem.at[c, s],
            device_id=partner[b],
            device_id_type=MESH,
        )
        copy.start()
        copies[c][s] = copy

    def rows(off, count):
        return pl.ds(pl.multiple_of(off, 16), count)

    copies = [{} for _ in range(len(plan) + 1)]
    spans = []
    for _, count, order, _ in plan:
        span = [(0, count)]
        for b in order:
            off, size = span[-1]
            span.append((off + bit[b] * (size // 2), size // 2))
        spans.append(span)

    def held(c, s, b):
        a, count, _, _ = plan[c]
        half = count >> (s + 1)
        base = count - (count >> (s - 1)) if s else 0
        return (got[c] if s else ins[a]), base + (1 - bit[b]) * half, base + bit[b] * half, half

    def begin(c, s):
        a, count, order, _ = plan[c]
        if s < nbits:
            b = order[s]
            ref, gives, _, half = held(c, s, b)
            send(c, s, b, ref.at[rows(gives, half), :], got[c].at[pl.ds(count - (count >> s), half), :])
        else:
            j = 2 * nbits - 1 - s
            block = outs[a].at[rows(*spans[c][j + 1]), :]
            send(c, s, order[j], block, block)

    def finish(c, s):
        copies[c][s].wait_recv()
        if s < nbits:
            a, count, order, _ = plan[c]
            ref, _, stays, half = held(c, s, order[s])
            came = pl.ds(count - (count >> s), half)
            total = ref[rows(stays, half), :].astype(F32) + got[c][came, :].astype(F32)
            if s < nbits - 1:
                got[c][came, :] = total.astype(BF16)
            else:
                outs[a][rows(*spans[c][s + 1]), :] = total.astype(BF16)

    last = len(plan)
    size = ins[n].shape[0]
    outs[n][...] = ins[n][...]
    for c, (a, _, _, done) in enumerate(plan):
        if done:
            outs[a][rows(*spans[c][nbits]), :] = ins[a][...]
    for t in range(2 * nbits + 1):
        for c, (_, _, _, done) in enumerate(plan):
            s = t + done
            if done < s < 2 * nbits or (s == 2 * nbits and not done):
                finish(c, s - 1)
            if s < 2 * nbits:
                begin(c, s)
        if 1 <= t <= nbits:
            copies[last][t - 1].wait()
            outs[n][...] = (
                outs[n][...].astype(F32) + got[last][(t - 1) * size : t * size, :].astype(F32)
            ).astype(BF16)
        if t < nbits:
            send(last, t, t, outs[n], got[last].at[pl.ds(t * size, size), :])
    for c, (_, _, _, done) in enumerate(plan):
        if done:
            finish(c, 2 * nbits - 1)
        for copy in copies[c].values():
            copy.wait_send()


def all_sum(arrays, blocks, small, devices):
    nbits = devices.bit_length() - 1
    line = tuple(range(nbits - 1, 1, -1))
    flat = [a.reshape(-1, a.shape[-1]) for a in arrays]
    fits = [a.shape[0] % (16 * devices) == 0 for a in flat]
    plan, operands, shapes = [], [], []
    for a, first in blocks:
        plan.append((len(operands), a.shape[0] * devices, (*first, *line), nbits))
        operands.append(a)
        shapes.append((a.shape[0] * devices, a.shape[1]))
    for a, fit in zip(flat, fits):
        if fit:
            first = ((0, 1), (1, 0))[len(plan) % 2]
            plan.append((len(operands), a.shape[0], (*first, *range(2, nbits)), 0))
            operands.append(a)
            shapes.append(a.shape)
    small = jnp.pad(small, ((0, 16 - small.shape[0]), (0, 0)))
    operands.append(small)
    shapes.append(small.shape)
    vmem = pl.BlockSpec(memory_space=pltpu.VMEM)
    sums = pl.pallas_call(
        functools.partial(all_sum_kernel, plan, nbits, len(plan)),
        in_specs=[vmem] * len(operands),
        out_specs=[vmem] * len(operands),
        out_shape=[jax.ShapeDtypeStruct(shape, BF16) for shape in shapes],
        scratch_shapes=[pltpu.VMEM((16 if done else rows, operands[i].shape[1]), BF16) for i, rows, _, done in plan]
        + [pltpu.VMEM((16 * nbits, small.shape[1]), BF16)]
        + [pltpu.SemaphoreType.DMA((len(plan) + 1, 2 * nbits))] * 2,
        compiler_params=pltpu.CompilerParams(
            collective_id=7, has_side_effects=True, vmem_limit_bytes=28 << 20
        ),
    )(*operands)
    whole_ones = sums[: len(blocks)]
    rest = iter(sums[len(blocks) : -1])
    outs = [next(rest).reshape(a.shape) if fit else lax.psum(a, "batch") for a, fit in zip(arrays, fits)]
    return outs, whole_ones, sums[-1]


def across(r, shift, devices):
    return [(i, i ^ (r << shift)) for i in range(devices)]


def cut(blocks, shift, bits, me):
    place = (me >> shift) % (1 << bits)
    return [lax.dynamic_index_in_dim(blocks, place ^ r, 0, keepdims=False) for r in range(1 << bits)]


def scatter_step(blocks, shift, devices):
    return blocks[:1] + [lax.ppermute(b, "batch", across(r, shift, devices)) for r, b in enumerate(blocks) if r]


def add_up(blocks):
    total = blocks[0].astype(F32)
    for b in blocks[1:]:
        total += b.astype(F32)
    return total.astype(BF16)


def widen_kernel(layout, n, terms, *refs):
    ins, adds, outs, total_ref = refs[:n], refs[n : n + terms], refs[n + terms : -1], refs[-1]
    total = adds[0][...].astype(F32)
    for r in range(1, terms):
        total += adds[r][...].astype(F32)
    total_ref[...] = total
    for out, sources in zip(outs, layout):
        for c, (i, at, count) in enumerate(sources):
            block = ins[i][...]
            if at is not None:
                block = block[:, at : at + count, :].reshape(-1, block.shape[-1])
            if len(out.shape) == 3:
                out[c] = block.astype(F32)
            else:
                out[...] = block.astype(F32)


def widen(arrays, layout, shapes, adds, steps):
    def spec(shape):
        if len(shape) == 2:
            return pl.BlockSpec((shape[0] // steps, shape[1]), lambda i: (i, 0))
        return pl.BlockSpec((shape[0], shape[1] // steps, shape[2]), lambda i: (0, i, 0))

    def in_spec(a):
        if a.ndim == 2:
            return spec(a.shape)
        return pl.BlockSpec((a.shape[0] // steps, *a.shape[1:]), lambda i: (i, 0, 0))

    return pl.pallas_call(
        functools.partial(widen_kernel, layout, len(arrays), len(adds)),
        grid=(steps,),
        in_specs=[in_spec(a) for a in (*arrays, *adds)],
        out_specs=[spec(s) for s in (*shapes, adds[0].shape)],
        out_shape=[jax.ShapeDtypeStruct(s, F32) for s in (*shapes, adds[0].shape)],
        compiler_params=params(24),
        cost_estimate=cost(0, sum(math.prod(s) * 6 for s in shapes)),
    )(*arrays, *adds)


def shards(
    block_input_slots,
    memory,
    target_sentence_lengths,
    source_lengths,
    self_qkv,
    self_out,
    cross_query,
    cross_kv,
    cross_out,
    up_proj,
    down_proj,
    norm_gains,
    norm_biases,
    cotangent,
    mp,
    devices,
):
    tokens, d = block_input_slots.shape
    mem_tokens = memory.shape[0]
    share = cotangent.shape[0]
    mem_share = mem_tokens // mp
    width = self_qkv.shape[2]
    me = lax.axis_index("mp")
    bt = min(512, share)
    bq = min(256, share)
    bk = min(256, mem_tokens)

    def spread(own):
        return [own] + [
            lax.ppermute(own, "mp", [(i, (i + r) % mp) for i in range(mp)]) for r in range(1, mp)
        ]

    def exchange(pieces):
        got = [pieces[0]] + [None] * (mp - 1)
        for r in range(1, mp):
            got[mp - r] = lax.ppermute(pieces[r], "mp", [(i, (i - r) % mp) for i in range(mp)])
        return got

    wo, cq, co = spread(self_out), spread(cross_query), spread(cross_out)
    up, down = spread(up_proj), spread(down_proj)
    gain, shift = norm_gains.T, norm_biases.T

    t_len = target_sentence_lengths.reshape(-1)
    s_len = source_lengths.reshape(-1)
    t_end, s_end = jnp.cumsum(t_len), jnp.cumsum(s_len)
    t_start, s_start = t_end - t_len, s_end - s_len
    first = ((me - jnp.arange(mp)) % mp) * share
    place = (first[:, None] + jnp.arange(share)[None, :]).reshape(-1).astype(jnp.int32)
    begun = place[:, None] >= t_start[None, :]
    self_lo = jnp.max(jnp.where(begun, t_start[None, :], 0), axis=1)
    self_hi = place + 1
    cross_lo = jnp.max(jnp.where(begun, s_start[None, :], 0), axis=1)
    cross_hi = jnp.max(jnp.where(begun, s_end[None, :], 0), axis=1)
    nblk = tokens // bq
    q_block = place.reshape(nblk, bq)[:, 0] // bq

    def table(lo, hi):
        return jnp.concatenate(
            [lo.reshape(nblk, bq)[:, 0] // bk, (hi.reshape(nblk, bq)[:, -1] + bk - 1) // bk, q_block]
        ).astype(jnp.int32)

    self_table, cross_table = table(self_lo, self_hi), table(cross_lo, cross_hi)
    as_row = lambda v: v.reshape(1, tokens).astype(jnp.int32)
    self_lo, self_hi, cross_lo, cross_hi = map(as_row, (self_lo, self_hi, cross_lo, cross_hi))

    *proj, self_kt, self_vt = project(block_input_slots, self_qkv, (1, 2), min(512, mem_tokens))
    *pair, cross_kt, cross_vt = project(memory, cross_kv, (0, 1), min(512, mem_tokens))
    ctx_parts, self_lse = attend(
        self_table, proj[:1], proj[1], self_vt, self_lo, self_hi, mp, bq, bk
    )
    ctx = exchange(ctx_parts)
    me_row = me.reshape(1).astype(jnp.int32)
    n1, xhat1, rstd1, qc = post_self(me_row, block_input_slots, ctx, wo, cq, gain, shift, share, bt)
    qc_parts = exchange(qc)
    cctx_parts, cross_lse = attend(
        cross_table, qc_parts, pair[0], cross_vt, cross_lo, cross_hi, mp, bq, bk
    )
    cctx = exchange(cctx_parts)
    layer_output, da2, n2, e3, e2, dcctx, hid, dpre, small23 = middle(
        cctx, n1, cotangent, co, up, down, gain, shift, min(512, share)
    )
    dcctx_parts = exchange(dcctx)

    def grads(lefts, rights):
        return [mm(a, b, TN).astype(BF16) for a, b in zip(lefts, rights)]

    def collect(pieces):
        got = exchange(pieces)
        total = got[0].astype(F32)
        for g in got[1:]:
            total += g.astype(F32)
        return total

    early = [
        collect(grads(dpre, [n2] * mp)).astype(BF16),
        collect(grads(hid, [e3] * mp)).astype(BF16),
        collect(grads(cctx, [e2] * mp)).astype(BF16),
    ]
    hidden = all(g.shape[0] % (16 * devices) == 0 for g in early)
    row = lax.axis_index("batch")
    far = devices.bit_length() - 3
    if hidden:
        one = early[0].reshape(4, 1 << far, -1, d)
        two = jnp.concatenate([g.reshape(4, 1 << far, -1, d) for g in early[1:]], axis=2)
        here = row % 4
        mirrored = here % 2 * 2 + here // 2
        blocks = [
            jnp.concatenate(
                [
                    lax.dynamic_index_in_dim(one, mirrored ^ (0, 2, 1, 3)[r], 0, keepdims=False),
                    lax.dynamic_index_in_dim(two, here ^ r, 0, keepdims=False),
                ],
                axis=1,
            )
            for r in range(4)
        ]
        dcctx_parts, blocks = lax.optimization_barrier((dcctx_parts, blocks))
        blocks = scatter_step(blocks, 0, devices)
    dqc_parts, dkc, dvc = attend_back(
        cross_table, qc_parts, dcctx_parts, cctx_parts, pair[0], cross_kt, pair[1], cross_lo, cross_hi, cross_lse, mp, bq, bk
    )
    dqc = exchange(dqc_parts)
    if hidden:
        dqc, block = lax.optimization_barrier((dqc, add_up(blocks)))
    da1, e1, dctx, small1 = pre_self(dqc, cq, wo, da2, xhat1, rstd1, gain, bt)
    dctx_parts = exchange(dctx)
    mem_bt = min(512, mem_share)
    mem_nb = mem_share // mem_bt
    mem_blocks = ((((me - jnp.arange(mp)) % mp) * mem_nb)[:, None] + jnp.arange(mem_nb)[None, :]).reshape(-1)
    memory_parts = input_part(mem_blocks.astype(jnp.int32), [dkc, dvc], cross_kv, mp, mem_bt)
    memory_grad = collect(memory_parts)
    cross_kv_grad = [mm(memory, g, TN) for g in (dkc, dvc)]
    cross_query_grad = collect(grads([n1] * mp, dqc))
    self_out_grad = collect(grads(ctx, [e1] * mp))
    if hidden:
        dctx_parts, blocks = lax.optimization_barrier((dctx_parts, cut(block, 2, far, row)))
        blocks = scatter_step(blocks, 2, devices)
    (dq,), dk, dv = attend_back(
        self_table, proj[:1], dctx_parts, ctx_parts, proj[1], self_kt, proj[2], self_lo, self_hi, self_lse, mp, bq, bk
    )
    if hidden:
        dq, dk, dv, block = lax.optimization_barrier((dq, dk, dv, add_up(blocks)))
    in_bt = min(512, share)
    in_blocks = place.reshape(-1, in_bt)[:, 0] // in_bt
    input_parts = input_part(in_blocks.astype(jnp.int32), [dq, dk, dv], self_qkv, mp, in_bt)
    self_qkv_grad = [mm(block_input_slots, g, TN) for g in (dq, dk, dv)]

    small = jnp.concatenate([small1[:1], small23[:2], small1[1:], small23[2:]], axis=0)
    part = d // mp
    pieces = [
        lax.dynamic_slice_in_dim(small, ((me - r) % mp) * part, part, 1).astype(BF16) for r in range(mp)
    ]
    small = collect(pieces)
    late = [*self_qkv_grad, self_out_grad, cross_query_grad, *cross_kv_grad]
    late = [g.astype(BF16) for g in late]
    if hidden:
        count = early[0].shape[0] // devices
        summed, (up_grad, rest), small = all_sum(
            late, [(block[:count], (0, 1)), (block[count:], (1, 0))], small.astype(BF16), devices
        )
        rest = rest.reshape(devices, -1, d)
        count = early[1].shape[0] // devices
        more = early[2].shape[0] // devices
        late_shapes = [
            self_qkv.shape,
            self_out.shape,
            cross_query.shape,
            cross_kv.shape,
        ]
        *summed, up_grad, down_grad, cross_out_grad, input_grad = widen(
            [*summed, up_grad, rest],
            [
                [(0, None, 0), (1, None, 0), (2, None, 0)],
                [(3, None, 0)],
                [(4, None, 0)],
                [(5, None, 0), (6, None, 0)],
                [(7, None, 0)],
                [(8, 0, count)],
                [(8, count, more)],
            ],
            late_shapes + [g.shape for g in early],
            [da1, *exchange(input_parts)],
            8,
        )
    else:
        input_grad = collect(input_parts) + da1
        summed, _, small = all_sum(late + early, [], small.astype(BF16), devices)
        *summed, up_grad, down_grad, cross_out_grad = [g.astype(F32) for g in summed]
        dwq, dwk, dwv, self_out_grad, cross_query_grad, dck, dcv = summed
        summed = [jnp.stack([dwq, dwk, dwv]), self_out_grad, cross_query_grad, jnp.stack([dck, dcv])]
    summed += [cross_out_grad, up_grad, down_grad]
    small = small.astype(F32).T
    return (layer_output, input_grad, memory_grad, *summed, small[:, :3], small[:, 3:6])


def solution(mesh):
    mp = mesh.shape["mp"]
    rows = P("batch", None)
    both = P(("batch", "mp"), None)
    first, last, last3 = P("mp", None), P(None, "mp"), P(None, None, "mp")
    return jax.shard_map(
        functools.partial(shards, mp=mp, devices=mesh.shape["batch"]),
        mesh=mesh,
        in_specs=(rows, rows, rows, rows, last3, first, last, last3, first, first, first, P(), P(), both),
        out_specs=(both, both, both, last3, first, last, last3, first, first, first, first, first),
        check_vma=False,
    )
```
